32 devices in a mesh: ta: 2 (over x), tp: 16 (over z, y, core).
Axes of the slice: x: 2, y: 2, z: 4, core: 2. Of those that a mesh axis runs over, the one named last changes fastest.
Arguments:
- green: float32 [2, 2, 16, 16, 512], P(None, None, 'tp', None, 'ta'), may hold values from -5 to 5
- hamiltonian: float32 [32, 32], replicated, may hold values from -1 to 1
- interaction: float32 [32, 32], replicated, may hold values from 0.4 to 1.2
Outputs:
- green_next: float32 [2, 2, 16, 16, 512], P(None, None, 'tp', None, 'ta')
The draws below stay inside these ranges and needn't reach their ends.
All inputs are finite; a program needn't handle non-finite values.
Results may differ from the reference program's by a relative error of at most 0.0091.
Values may be sent and summed in bfloat16 or wider, within the bound.
No kernel may reach another device: no remote copies, remote signals or barrier semaphores. Data moves between devices by JAX's collectives and lax.ppermute only.
A program may use at most 64 MiB of HBM per device.

```python
import math
import jax
import jax.numpy as jnp
from jax import lax

NO = 32
W = 16
ITERS = 2
ORDER = 512
MEMT = 16
N_TA = 2
N_TP = 16


def level_of(own_key, dims, pieces, low, largest):
    factor_of = 1.0
    for dim, blocks in pieces:
        steps = jax.random.uniform(jax.random.fold_in(jax.random.fold_in(own_key, 6), dim), (blocks,), jnp.float32, low / len(pieces), largest / len(pieces))
        factor_of = factor_of * jnp.repeat(jnp.exp(steps), dims[dim] // blocks).reshape((-1,) + (1,) * (len(dims) - 1 - dim))
    return factor_of


def centred(rng, shape, width, reach, pieces=(), held_as=jnp.bfloat16):
    entries = width * jax.random.normal(rng, shape, jnp.float32)
    if pieces:
        entries = entries * level_of(rng, shape, pieces, -0.22, 0.18)
    return jnp.clip(entries, -reach, reach).astype(held_as)


def setup_inputs(seed: int = 0) -> dict:
    streams_of = jax.random.split(jax.random.key(seed), 4)
    green = centred(streams_of[0], (2, N_TA, N_TP, W, ORDER), 0.7, 5.0, ((2, 16), (4, 2)), jnp.float32)
    hamiltonian = centred(streams_of[1], (NO, NO), NO ** -0.5, 1.0, (), jnp.float32)
    interaction = jnp.clip(jnp.exp(jax.random.uniform(streams_of[2], (NO, NO), jnp.float32, math.log(0.4), math.log(1.2))), 0.4, 1.2)
    return dict(green=green, hamiltonian=hamiltonian, interaction=interaction)


highest = lax.Precision.HIGHEST

def real_dot(left_side, right_side):
    return jnp.dot(left_side, right_side, precision=highest, preferred_element_type=jnp.float32)

def reference(green, hamiltonian, interaction):
    full_order = N_TA * N_TP * W
    block_rows = N_TP * W
    time_count = full_order // NO
    factor = 1.0 / math.sqrt(MEMT * NO)
    current = green.reshape(2, full_order, full_order)
    coupling = (interaction * interaction).T.reshape(1, NO, 1, NO)
    row_time = jnp.arange(full_order, dtype=jnp.int32) // NO
    inside = (row_time[:, None] <= row_time[None, :]) & (row_time[:, None] > row_time[None, :] - MEMT)
    padding = 2 * block_rows
    for iteration in range(ITERS):
        rounded = current.astype(jnp.bfloat16)
        lowered = lax.optimization_barrier(rounded).astype(jnp.float32)
        mirrored = jnp.swapaxes(lowered, 1, 2)
        real_square = current[0] * current[0] - current[1] * current[1]
        imag_square = 2.0 * current[0] * current[1]
        sigma_real = real_square * mirrored[0] - imag_square * mirrored[1]
        sigma_imag = real_square * mirrored[1] + imag_square * mirrored[0]
        sigma = jnp.stack([sigma_real, sigma_imag]).reshape(2, time_count, NO, time_count, NO) * coupling
        sigma = jnp.where(inside, sigma.reshape(2, full_order, full_order), 0.0)
        window = sigma.astype(jnp.bfloat16)
        window_low = lax.optimization_barrier(window).astype(jnp.float32)
        padded_green = jnp.pad(lowered, ((0, 0), (0, 0), (padding, 0)))
        padded_sigma = jnp.pad(window_low, ((0, 0), (padding, 0), (0, 0)))

        def one_block(block_index):
            begin_at = block_index * block_rows
            left_side = lax.dynamic_slice_in_dim(padded_green, begin_at, 3 * block_rows, 2)
            right_side = lax.dynamic_slice_in_dim(padded_sigma, begin_at, 3 * block_rows, 1)
            right_side = lax.dynamic_slice_in_dim(right_side, begin_at, block_rows, 2)
            product_real = real_dot(left_side[0], right_side[0]) - real_dot(left_side[1], right_side[1])
            product_imag = real_dot(left_side[0], right_side[1]) + real_dot(left_side[1], right_side[0])
            return jnp.stack([product_real, product_imag])
        block_results = lax.map(one_block, jnp.arange(N_TA, dtype=jnp.int32))
        memory = jnp.transpose(block_results, (1, 2, 0, 3)).reshape(2, full_order, full_order)
        hamilton_term = jnp.einsum('pxtk,ik->pxti', current.reshape(2, full_order, time_count, NO), hamiltonian, precision=highest).reshape(2, full_order, full_order)
        next_real = current[0] + 0.5 * (hamilton_term[1] + factor * memory[1])
        next_imag = current[1] - 0.5 * (hamilton_term[0] + factor * memory[0])
        current = jnp.stack([next_real, next_imag])
    return current.reshape(2, N_TA, N_TP, W, full_order)
```

```python
import math

import jax
import jax.numpy as jnp
from jax import lax
from jax.experimental import pallas as pl
from jax.experimental.pallas import tpu as pltpu
from jax.sharding import PartitionSpec as P

NO = 32
ITERS = 2


highest = lax.Precision.HIGHEST


def shifted(block, axis, distance):
    devices = range(lax.axis_size(axis))
    route = [(i - distance, i) for i in devices if i - distance in devices]
    return lax.ppermute(block, axis, route)


def half_dot(left_side, right_side):
    return jnp.dot(left_side, right_side, preferred_element_type=jnp.float32)


def accumulate(left_side, right_side):
    product_real = half_dot(left_side[0], right_side[0]) - half_dot(left_side[1], right_side[1])
    product_imag = half_dot(left_side[0], right_side[1]) + half_dot(left_side[1], right_side[0])
    return (product_real, product_imag)


def self_energy(values, mirror_part, weights):
    real_square = values[0] * values[0] - values[1] * values[1]
    imag_square = 2.0 * values[0] * values[1]
    sigma_real = weights * (real_square * mirror_part[0] - imag_square * mirror_part[1])
    sigma_imag = weights * (real_square * mirror_part[1] + imag_square * mirror_part[0])
    return jnp.stack([sigma_real, sigma_imag])


def windowed(green, hamiltonian, interaction):
    tp_count = lax.axis_size("tp")
    ta_place = lax.axis_index("ta")
    tp_place = lax.axis_index("tp")
    groups = green.shape[1]
    stripe = green.shape[3]
    block_rows = green.shape[4]
    columns = groups * stripe
    factor = 1.0 / math.sqrt(2 * block_rows)
    current = green[:, :, 0].reshape(2, columns, block_rows)
    squared = interaction * interaction
    column_global = (
        jnp.arange(groups, dtype=jnp.int32)[:, None] * tp_count + tp_place
    ) * stripe + jnp.arange(stripe, dtype=jnp.int32)[None, :]
    column_orbital = (column_global % NO).reshape(columns)
    onehot = (column_orbital[:, None] == jnp.arange(NO, dtype=jnp.int32)[None, :]).astype(
        jnp.float32
    )
    lookup_table = jnp.dot(onehot, squared.T, precision=highest)
    coupling = jnp.tile(lookup_table, (1, block_rows // NO))
    row_time = jnp.arange(block_rows, dtype=jnp.int32) // NO
    column_time = (tp_place * stripe + jnp.arange(stripe, dtype=jnp.int32)) // NO
    is_later = column_time[:, None] > row_time[None, :]
    block_width = math.gcd(block_rows, 128)
    blocked = jnp.kron(jnp.eye(block_width // NO, dtype=jnp.float32), hamiltonian.T)
    zero_half = jnp.zeros((), jnp.bfloat16)
    for iteration in range(ITERS):
        rounded = current.astype(jnp.bfloat16)
        outgoing = rounded.reshape(2, groups, stripe, tp_count, stripe)
        previous = shifted(rounded, "ta", 1)
        earliest = shifted(rounded, "ta", 2)
        hamilton_term = jnp.dot(
            current.reshape(-1, block_width), blocked, precision=highest
        ).reshape(2, columns, block_rows)
        selected = []
        nearby = jnp.stack(
            [
                lax.dynamic_index_in_dim(
                    outgoing, jnp.minimum(ta_place + step_ahead, groups - 1), 1, keepdims=False
                )
                for step_ahead in range(3)
            ],
            1,
        )
        spread = lax.all_to_all(nearby, "tp", split_axis=3, concat_axis=3, tiled=True)
        from_one = shifted(spread[:, 1], "ta", 1)
        from_two = shifted(spread[:, 2], "ta", 2)
        received = (from_two, from_one, spread[:, 0])
        by_current = current.reshape(2, groups, stripe, block_rows)
        for window_index in range(3):
            group_pick = jnp.maximum(ta_place - 2 + window_index, 0)
            own_part = lax.dynamic_index_in_dim(by_current, group_pick, 1, keepdims=False)
            flipped = (
                jnp.transpose(received[window_index], (0, 3, 2, 1))
                .reshape(2, stripe, block_rows)
                .astype(jnp.float32)
            )
            selected.append(self_energy(own_part, flipped, coupling[:stripe]))
        oldest = jnp.where(is_later[None], selected[0], 0.0)
        middle = selected[1]
        newest = jnp.where(is_later[None], 0.0, selected[2])
        sending = jnp.stack([oldest + newest, middle], 1).astype(jnp.bfloat16)[:, :, None]
        portion = lax.all_gather(sending, "tp", axis=2, tiled=True)
        row_count = portion.shape[2] * stripe
        arriving_time = jnp.arange(row_count, dtype=jnp.int32) // NO
        later_here = (arriving_time[:, None] > row_time[None, :])[None]
        merged = portion[:, 0].reshape(2, row_count, block_rows)
        recent = portion[:, 1].reshape(2, row_count, block_rows)
        right_side = jnp.concatenate(
            [
                jnp.where(later_here, merged, zero_half),
                recent,
                jnp.where(later_here, zero_half, merged),
            ],
            1,
        )
        memory = accumulate(
            jnp.concatenate([source for source in (earliest, previous, rounded)], 2), right_side
        )
        next_real = current[0] + 0.5 * (hamilton_term[1] + factor * memory[1])
        next_imag = current[1] - 0.5 * (hamilton_term[0] + factor * memory[0])
        current = jnp.stack([next_real, next_imag])
    return current.reshape(2, groups, 1, stripe, block_rows)


def exchange_orders(ta_count, tp_count):
    tp_bits = [1 << bit for bit in reversed(range(1, tp_count.bit_length() - 1))]
    even = tp_bits + [tp_count]
    odd = tp_bits[:1] + tp_bits[2:] + [tp_count] + tp_bits[1:2]
    return even, odd


def gathered(own, orders, count):
    held = own[None]
    for masks in zip(*orders):
        route = [(i, i ^ masks[i % 2]) for i in range(count)]
        held = jnp.concatenate([held, lax.ppermute(held, ("ta", "tp"), route)])
    return held


def offsets_of(order):
    offsets = [0]
    for mask in order:
        offsets = offsets + [known ^ mask for known in offsets]
    return offsets


def bf16_dot(left_side, right_side):
    return lax.dot_general(
        left_side, right_side, (((1,), (0,)), ((), ())), preferred_element_type=jnp.float32
    )


def make_iterations(orders, ta_count, tp_count, stripe, block_rows, factor):
    order_size = ta_count * block_rows
    offsets = [offsets_of(order) for order in orders]
    half = jnp.bfloat16

    def square_of(values):
        real, imag = values
        return real * real - imag * imag, 2.0 * real * imag

    def window_of(values, mirror, weights, first_time):
        rows, width = values[0].shape
        real_square, imag_square = square_of(values)
        mirror_real = mirror[0].astype(jnp.float32)
        mirror_imag = mirror[1].astype(jnp.float32)
        real = real_square * mirror_real - imag_square * mirror_imag
        imag = real_square * mirror_imag + imag_square * mirror_real
        source_time = lax.broadcasted_iota(jnp.int32, (rows, width), 0) // NO
        target_time = lax.broadcasted_iota(jnp.int32, (rows, width), 1) // NO + first_time
        inside = source_time <= target_time

        def weighted(part):
            part = (part.reshape(rows // NO, NO, width) * weights[None]).reshape(rows, width)
            return jnp.where(inside, part, 0.0).astype(half)

        return weighted(real), weighted(imag)

    def products(left_side, right_side):
        real = bf16_dot(left_side[0], right_side[0]) - bf16_dot(left_side[1], right_side[1])
        imag = bf16_dot(left_side[0], right_side[1]) + bf16_dot(left_side[1], right_side[0])
        return real, imag

    def rotated(values, high_table, low_table):
        high = values.astype(half)
        low = (values - high.astype(jnp.float32)).astype(half)
        return (
            bf16_dot(high, high_table) + bf16_dot(low, high_table) + bf16_dot(high, low_table)
        )

    def kernel(place, near, far, weights_ref, high_ref, low_ref, out, values, lows, nexts, low_next):
        ta_place = place[0]
        tp_place = place[1]
        me = ta_place * tp_count + tp_place
        odd = me % 2
        for source, flip in ((near, 0), (far, 1)):
            for index in range(len(offsets[0])):
                mask = jnp.where(odd == flip, offsets[0][index], offsets[1][index])
                device = (me ^ flip) ^ mask
                row = pl.multiple_of((device % tp_count) * stripe, stripe)
                block = device // tp_count
                for part in range(2):
                    for group in range(ta_count):
                        values[part, block, group, pl.ds(row, stripe), :] = source[
                            index, part, group
                        ]
        weights = weights_ref[...]
        high_table = high_ref[...]
        low_table = low_ref[...]
        for block in range(ta_count):
            for part in range(2):
                for group in range(ta_count):
                    lows[part, group, :, block * block_rows : (block + 1) * block_rows] = values[
                        part, block, group
                    ].astype(half)
        rounded = [lows[part].reshape(order_size, order_size) for part in range(2)]
        for block in range(ta_count):
            current = [values[part, block].reshape(order_size, block_rows) for part in range(2)]
            mirror = [
                jnp.transpose(lows[part, block].astype(jnp.float32)) for part in range(2)
            ]
            window = window_of(current, mirror, weights, block * (block_rows // NO))
            memory = products(rounded, window)
            hamilton = [rotated(current[part], high_table, low_table) for part in range(2)]
            shape = (ta_count, block_rows, block_rows)
            next_real = current[0] + 0.5 * (hamilton[1] + factor * memory[1])
            next_imag = current[1] - 0.5 * (hamilton[0] + factor * memory[0])
            for part, result in ((0, next_real), (1, next_imag)):
                nexts[part, block] = result.reshape(shape)
                low_next[part, :, :, block * block_rows : (block + 1) * block_rows] = (
                    result.reshape(shape).astype(half)
                )
        current = [nexts[part, ta_place].reshape(order_size, block_rows) for part in range(2)]
        mirror = [
            jnp.transpose(low_next[part, ta_place].astype(jnp.float32)) for part in range(2)
        ]
        window = window_of(current, mirror, weights, ta_place * (block_rows // NO))
        row = pl.multiple_of(tp_place * stripe, stripe)
        own = [
            nexts[part, ta_place, :, pl.ds(row, stripe), :].reshape(ta_count * stripe, block_rows)
            for part in range(2)
        ]
        own_rounded = [
            low_next[part, :, pl.ds(row, stripe), :].reshape(ta_count * stripe, order_size)
            for part in range(2)
        ]
        memory = products(own_rounded, window)
        hamilton = [rotated(own[part], high_table, low_table) for part in range(2)]
        shape = (ta_count, stripe, block_rows)
        out[0] = (own[0] + 0.5 * (hamilton[1] + factor * memory[1])).reshape(shape)
        out[1] = (own[1] - 0.5 * (hamilton[0] + factor * memory[0])).reshape(shape)

    big = (2, ta_count, ta_count, block_rows, block_rows)
    flat = (2, ta_count, block_rows, order_size)
    return pl.pallas_call(
        kernel,
        out_shape=jax.ShapeDtypeStruct((2, ta_count, stripe, block_rows), jnp.float32),
        in_specs=[pl.BlockSpec(memory_space=pltpu.SMEM)]
        + [pl.BlockSpec(memory_space=pltpu.VMEM)] * 5,
        out_specs=pl.BlockSpec(memory_space=pltpu.VMEM),
        scratch_shapes=[
            pltpu.VMEM(big, jnp.float32),
            pltpu.VMEM(flat, half),
            pltpu.VMEM(big, jnp.float32),
            pltpu.VMEM(flat, half),
        ],
        name="iterations",
    )


def replicated(green, hamiltonian, interaction):
    ta_count = lax.axis_size("ta")
    tp_count = lax.axis_size("tp")
    stripe = green.shape[3]
    block_rows = green.shape[4]
    factor = 1.0 / math.sqrt(2 * block_rows)
    orders = exchange_orders(ta_count, tp_count)
    count = ta_count * tp_count
    near = gathered(green[:, :, 0], orders, count)
    far = lax.ppermute(near, ("ta", "tp"), [(i, i ^ 1) for i in range(count)])
    place = jnp.stack([lax.axis_index("ta"), lax.axis_index("tp")]).astype(jnp.int32)
    weights = jnp.tile((interaction * interaction).T, (1, block_rows // NO))
    table = jnp.kron(jnp.eye(block_rows // NO, dtype=jnp.float32), hamiltonian.T)
    high_table = table.astype(jnp.bfloat16)
    low_table = (table - high_table.astype(jnp.float32)).astype(jnp.bfloat16)
    step = make_iterations(orders, ta_count, tp_count, stripe, block_rows, factor)
    result = step(place, near, far, weights, high_table, low_table)
    return result[:, :, None]


def solution(mesh):
    in_specs = (P(None, None, "tp", None, "ta"), P(), P())
    out_specs = P(None, None, "tp", None, "ta")
    ta_count = mesh.shape["ta"]
    tp_count = mesh.shape["tp"]

    def shards(green, hamiltonian, interaction):
        whole_bytes = green.size * green.dtype.itemsize * ta_count * tp_count
        covered = ta_count == 2 and green.shape[1] == 2 and tp_count >= 4
        if covered and tp_count & (tp_count - 1) == 0 and whole_bytes <= 1 << 22:
            return replicated(green, hamiltonian, interaction)
        return windowed(green, hamiltonian, interaction)

    return jax.shard_map(shards, mesh=mesh, in_specs=in_specs, out_specs=out_specs, check_vma=False)
```

```python
import math

import jax
import jax.numpy as jnp
from jax import lax
from jax.experimental import pallas as pl
from jax.experimental.pallas import tpu as pltpu
from jax.sharding import PartitionSpec as P

NO = 32
ITERS = 2


highest = lax.Precision.HIGHEST


def shifted(block, axis, distance):
    devices = range(lax.axis_size(axis))
    route = [(i - distance, i) for i in devices if i - distance in devices]
    return lax.ppermute(block, axis, route)


def half_dot(left_side, right_side):
    return jnp.dot(left_side, right_side, preferred_element_type=jnp.float32)


def accumulate(left_side, right_side):
    product_real = half_dot(left_side[0], right_side[0]) - half_dot(left_side[1], right_side[1])
    product_imag = half_dot(left_side[0], right_side[1]) + half_dot(left_side[1], right_side[0])
    return (product_real, product_imag)


def self_energy(values, mirror_part, weights):
    real_square = values[0] * values[0] - values[1] * values[1]
    imag_square = 2.0 * values[0] * values[1]
    sigma_real = weights * (real_square * mirror_part[0] - imag_square * mirror_part[1])
    sigma_imag = weights * (real_square * mirror_part[1] + imag_square * mirror_part[0])
    return jnp.stack([sigma_real, sigma_imag])


def windowed(green, hamiltonian, interaction):
    tp_count = lax.axis_size("tp")
    ta_place = lax.axis_index("ta")
    tp_place = lax.axis_index("tp")
    groups = green.shape[1]
    stripe = green.shape[3]
    block_rows = green.shape[4]
    columns = groups * stripe
    factor = 1.0 / math.sqrt(2 * block_rows)
    current = green[:, :, 0].reshape(2, columns, block_rows)
    squared = interaction * interaction
    column_global = (
        jnp.arange(groups, dtype=jnp.int32)[:, None] * tp_count + tp_place
    ) * stripe + jnp.arange(stripe, dtype=jnp.int32)[None, :]
    column_orbital = (column_global % NO).reshape(columns)
    onehot = (column_orbital[:, None] == jnp.arange(NO, dtype=jnp.int32)[None, :]).astype(
        jnp.float32
    )
    lookup_table = jnp.dot(onehot, squared.T, precision=highest)
    coupling = jnp.tile(lookup_table, (1, block_rows // NO))
    row_time = jnp.arange(block_rows, dtype=jnp.int32) // NO
    column_time = (tp_place * stripe + jnp.arange(stripe, dtype=jnp.int32)) // NO
    is_later = column_time[:, None] > row_time[None, :]
    block_width = math.gcd(block_rows, 128)
    blocked = jnp.kron(jnp.eye(block_width // NO, dtype=jnp.float32), hamiltonian.T)
    zero_half = jnp.zeros((), jnp.bfloat16)
    for iteration in range(ITERS):
        rounded = current.astype(jnp.bfloat16)
        outgoing = rounded.reshape(2, groups, stripe, tp_count, stripe)
        previous = shifted(rounded, "ta", 1)
        earliest = shifted(rounded, "ta", 2)
        hamilton_term = jnp.dot(
            current.reshape(-1, block_width), blocked, precision=highest
        ).reshape(2, columns, block_rows)
        selected = []
        nearby = jnp.stack(
            [
                lax.dynamic_index_in_dim(
                    outgoing, jnp.minimum(ta_place + step_ahead, groups - 1), 1, keepdims=False
                )
                for step_ahead in range(3)
            ],
            1,
        )
        spread = lax.all_to_all(nearby, "tp", split_axis=3, concat_axis=3, tiled=True)
        from_one = shifted(spread[:, 1], "ta", 1)
        from_two = shifted(spread[:, 2], "ta", 2)
        received = (from_two, from_one, spread[:, 0])
        by_current = current.reshape(2, groups, stripe, block_rows)
        for window_index in range(3):
            group_pick = jnp.maximum(ta_place - 2 + window_index, 0)
            own_part = lax.dynamic_index_in_dim(by_current, group_pick, 1, keepdims=False)
            flipped = (
                jnp.transpose(received[window_index], (0, 3, 2, 1))
                .reshape(2, stripe, block_rows)
                .astype(jnp.float32)
            )
            selected.append(self_energy(own_part, flipped, coupling[:stripe]))
        oldest = jnp.where(is_later[None], selected[0], 0.0)
        middle = selected[1]
        newest = jnp.where(is_later[None], 0.0, selected[2])
        sending = jnp.stack([oldest + newest, middle], 1).astype(jnp.bfloat16)[:, :, None]
        portion = lax.all_gather(sending, "tp", axis=2, tiled=True)
        row_count = portion.shape[2] * stripe
        arriving_time = jnp.arange(row_count, dtype=jnp.int32) // NO
        later_here = (arriving_time[:, None] > row_time[None, :])[None]
        merged = portion[:, 0].reshape(2, row_count, block_rows)
        recent = portion[:, 1].reshape(2, row_count, block_rows)
        right_side = jnp.concatenate(
            [
                jnp.where(later_here, merged, zero_half),
                recent,
                jnp.where(later_here, zero_half, merged),
            ],
            1,
        )
        memory = accumulate(
            jnp.concatenate([source for source in (earliest, previous, rounded)], 2), right_side
        )
        next_real = current[0] + 0.5 * (hamilton_term[1] + factor * memory[1])
        next_imag = current[1] - 0.5 * (hamilton_term[0] + factor * memory[0])
        current = jnp.stack([next_real, next_imag])
    return current.reshape(2, groups, 1, stripe, block_rows)


def exchange_orders(ta_count, tp_count):
    tp_bits = [1 << bit for bit in reversed(range(1, tp_count.bit_length() - 1))]
    first, middle, last = tp_bits[:1], tp_bits[1:-1], tp_bits[-1:]
    ta_bit = [tp_count]
    return [
        (first + middle + last + ta_bit, first + middle + ta_bit + last),
        (first + middle + ta_bit + last, first + middle + last + ta_bit),
    ]


def gathered(pieces, orders, count):
    held = [piece[None] for piece in pieces]
    for step in range(len(orders[0][0])):
        for index, (even, odd) in enumerate(orders):
            masks = (even[step], odd[step])
            route = [(i, i ^ masks[i % 2]) for i in range(count)]
            arriving = lax.ppermute(held[index], ("ta", "tp"), route)
            held[index] = jnp.concatenate([held[index], arriving])
    return held


def offsets_of(order):
    offsets = [0]
    for mask in order:
        offsets = offsets + [known ^ mask for known in offsets]
    return offsets


def bf16_dot(left_side, right_side):
    return lax.dot_general(
        left_side, right_side, (((1,), (0,)), ((), ())), preferred_element_type=jnp.float32
    )


def make_iterations(orders, ta_count, tp_count, stripe, block_rows, factor):
    order_size = ta_count * block_rows
    offsets = [[offsets_of(order) for order in pair] for pair in orders]
    half = jnp.bfloat16

    def square_of(values):
        real, imag = values
        return real * real - imag * imag, 2.0 * real * imag

    def window_of(values, mirror, weights, first_time):
        rows, width = values[0].shape
        real_square, imag_square = square_of(values)
        mirror_real = mirror[0].astype(jnp.float32)
        mirror_imag = mirror[1].astype(jnp.float32)
        real = real_square * mirror_real - imag_square * mirror_imag
        imag = real_square * mirror_imag + imag_square * mirror_real
        source_time = lax.broadcasted_iota(jnp.int32, (rows, width), 0) // NO
        target_time = lax.broadcasted_iota(jnp.int32, (rows, width), 1) // NO + first_time
        inside = source_time <= target_time

        def weighted(part):
            part = (part.reshape(rows // NO, NO, width) * weights[None]).reshape(rows, width)
            return jnp.where(inside, part, 0.0).astype(half)

        return weighted(real), weighted(imag)

    def products(left_side, right_side):
        real = bf16_dot(left_side[0], right_side[0]) - bf16_dot(left_side[1], right_side[1])
        imag = bf16_dot(left_side[0], right_side[1]) + bf16_dot(left_side[1], right_side[0])
        return real, imag

    def rotated(values, high_table, low_table):
        high = values.astype(half)
        low = (values - high.astype(jnp.float32)).astype(half)
        return (
            bf16_dot(high, high_table) + bf16_dot(low, high_table) + bf16_dot(high, low_table)
        )

    def repeated(tile):
        return jnp.concatenate([tile] * (block_rows // NO), axis=1)

    def kernel(*refs):
        sources = refs[: 2 * ta_count]
        hamiltonian, interaction, out, values, lows, nexts, low_next = refs[2 * ta_count :]
        ta_place = lax.axis_index("ta")
        tp_place = lax.axis_index("tp")
        me = ta_place * tp_count + tp_place
        odd = me % 2
        for group in range(ta_count):
            for flip in range(2):
                source = sources[2 * group + flip]
                pair = offsets[group]
                for index in range(len(pair[0])):
                    mask = jnp.where(odd == flip, pair[0][index], pair[1][index])
                    device = (me ^ flip) ^ mask
                    row = pl.multiple_of((device % tp_count) * stripe, stripe)
                    block = device // tp_count
                    for part in range(2):
                        values[part, block, group, pl.ds(row, stripe), :] = source[index, part]
        weights = repeated(jnp.transpose(interaction[...] * interaction[...]))
        table = jnp.concatenate([repeated(jnp.transpose(hamiltonian[...]))] * (block_rows // NO))
        same_time = (
            lax.broadcasted_iota(jnp.int32, table.shape, 0) // NO
            == lax.broadcasted_iota(jnp.int32, table.shape, 1) // NO
        )
        table = jnp.where(same_time, table, 0.0)
        high_table = table.astype(half)
        low_table = (table - high_table.astype(jnp.float32)).astype(half)
        for block in range(ta_count):
            for part in range(2):
                for group in range(ta_count):
                    lows[part, group, :, block * block_rows : (block + 1) * block_rows] = values[
                        part, block, group
                    ].astype(half)
        rounded = [lows[part].reshape(order_size, order_size) for part in range(2)]
        for block in range(ta_count):
            current = [values[part, block].reshape(order_size, block_rows) for part in range(2)]
            mirror = [
                jnp.transpose(lows[part, block].astype(jnp.float32)) for part in range(2)
            ]
            window = window_of(current, mirror, weights, block * (block_rows // NO))
            memory = products(rounded, window)
            hamilton = [rotated(current[part], high_table, low_table) for part in range(2)]
            shape = (ta_count, block_rows, block_rows)
            next_real = current[0] + 0.5 * (hamilton[1] + factor * memory[1])
            next_imag = current[1] - 0.5 * (hamilton[0] + factor * memory[0])
            for part, result in ((0, next_real), (1, next_imag)):
                nexts[part, block] = result.reshape(shape)
                low_next[part, :, :, block * block_rows : (block + 1) * block_rows] = (
                    result.reshape(shape).astype(half)
                )
        current = [nexts[part, ta_place].reshape(order_size, block_rows) for part in range(2)]
        mirror = [
            jnp.transpose(low_next[part, ta_place].astype(jnp.float32)) for part in range(2)
        ]
        window = window_of(current, mirror, weights, ta_place * (block_rows // NO))
        row = pl.multiple_of(tp_place * stripe, stripe)
        own = [
            nexts[part, ta_place, :, pl.ds(row, stripe), :].reshape(ta_count * stripe, block_rows)
            for part in range(2)
        ]
        own_rounded = [
            low_next[part, :, pl.ds(row, stripe), :].reshape(ta_count * stripe, order_size)
            for part in range(2)
        ]
        memory = products(own_rounded, window)
        hamilton = [rotated(own[part], high_table, low_table) for part in range(2)]
        shape = (ta_count, stripe, block_rows)
        out[0] = (own[0] + 0.5 * (hamilton[1] + factor * memory[1])).reshape(shape)
        out[1] = (own[1] - 0.5 * (hamilton[0] + factor * memory[0])).reshape(shape)

    big = (2, ta_count, ta_count, block_rows, block_rows)
    flat = (2, ta_count, block_rows, order_size)
    return pl.pallas_call(
        kernel,
        out_shape=jax.ShapeDtypeStruct((2, ta_count, stripe, block_rows), jnp.float32),
        in_specs=[pl.BlockSpec(memory_space=pltpu.VMEM)] * (2 * ta_count + 2),
        out_specs=pl.BlockSpec(memory_space=pltpu.VMEM),
        scratch_shapes=[
            pltpu.VMEM(big, jnp.float32),
            pltpu.VMEM(flat, half),
            pltpu.VMEM(big, jnp.float32),
            pltpu.VMEM(flat, half),
        ],
        compiler_params=pltpu.CompilerParams(vmem_limit_bytes=24 << 20),
        name="iterations",
    )


def replicated(green, hamiltonian, interaction):
    ta_count = lax.axis_size("ta")
    tp_count = lax.axis_size("tp")
    stripe = green.shape[3]
    block_rows = green.shape[4]
    factor = 1.0 / math.sqrt(2 * block_rows)
    orders = exchange_orders(ta_count, tp_count)
    count = ta_count * tp_count
    held = gathered([green[:, group, 0] for group in range(ta_count)], orders, count)
    swap = [(i, i ^ 1) for i in range(count)]
    sources = []
    for near in held:
        sources += [near, lax.ppermute(near, ("ta", "tp"), swap)]
    step = make_iterations(orders, ta_count, tp_count, stripe, block_rows, factor)
    result = step(*sources, hamiltonian, interaction)
    return result[:, :, None]


def solution(mesh):
    in_specs = (P(None, None, "tp", None, "ta"), P(), P())
    out_specs = P(None, None, "tp", None, "ta")
    ta_count = mesh.shape["ta"]
    tp_count = mesh.shape["tp"]

    def shards(green, hamiltonian, interaction):
        whole_bytes = green.size * green.dtype.itemsize * ta_count * tp_count
        covered = ta_count == 2 and green.shape[1] == 2 and tp_count >= 4
        if covered and tp_count & (tp_count - 1) == 0 and whole_bytes <= 1 << 22:
            return replicated(green, hamiltonian, interaction)
        return windowed(green, hamiltonian, interaction)

    return jax.shard_map(shards, mesh=mesh, in_specs=in_specs, out_specs=out_specs, check_vma=False)
```

```python
import math

import jax
import jax.numpy as jnp
from jax import lax
from jax.experimental import pallas as pl
from jax.experimental.pallas import tpu as pltpu
from jax.sharding import PartitionSpec as P

NO = 32
ITERS = 2


highest = lax.Precision.HIGHEST


def shifted(block, axis, distance):
    devices = range(lax.axis_size(axis))
    route = [(i - distance, i) for i in devices if i - distance in devices]
    return lax.ppermute(block, axis, route)


def half_dot(left_side, right_side):
    return jnp.dot(left_side, right_side, preferred_element_type=jnp.float32)


def accumulate(left_side, right_side):
    product_real = half_dot(left_side[0], right_side[0]) - half_dot(left_side[1], right_side[1])
    product_imag = half_dot(left_side[0], right_side[1]) + half_dot(left_side[1], right_side[0])
    return (product_real, product_imag)


def self_energy(values, mirror_part, weights):
    real_square = values[0] * values[0] - values[1] * values[1]
    imag_square = 2.0 * values[0] * values[1]
    sigma_real = weights * (real_square * mirror_part[0] - imag_square * mirror_part[1])
    sigma_imag = weights * (real_square * mirror_part[1] + imag_square * mirror_part[0])
    return jnp.stack([sigma_real, sigma_imag])


def windowed(green, hamiltonian, interaction):
    tp_count = lax.axis_size("tp")
    ta_place = lax.axis_index("ta")
    tp_place = lax.axis_index("tp")
    groups = green.shape[1]
    stripe = green.shape[3]
    block_rows = green.shape[4]
    columns = groups * stripe
    factor = 1.0 / math.sqrt(2 * block_rows)
    current = green[:, :, 0].reshape(2, columns, block_rows)
    squared = interaction * interaction
    column_global = (
        jnp.arange(groups, dtype=jnp.int32)[:, None] * tp_count + tp_place
    ) * stripe + jnp.arange(stripe, dtype=jnp.int32)[None, :]
    column_orbital = (column_global % NO).reshape(columns)
    onehot = (column_orbital[:, None] == jnp.arange(NO, dtype=jnp.int32)[None, :]).astype(
        jnp.float32
    )
    lookup_table = jnp.dot(onehot, squared.T, precision=highest)
    coupling = jnp.tile(lookup_table, (1, block_rows // NO))
    row_time = jnp.arange(block_rows, dtype=jnp.int32) // NO
    column_time = (tp_place * stripe + jnp.arange(stripe, dtype=jnp.int32)) // NO
    is_later = column_time[:, None] > row_time[None, :]
    block_width = math.gcd(block_rows, 128)
    blocked = jnp.kron(jnp.eye(block_width // NO, dtype=jnp.float32), hamiltonian.T)
    zero_half = jnp.zeros((), jnp.bfloat16)
    for iteration in range(ITERS):
        rounded = current.astype(jnp.bfloat16)
        outgoing = rounded.reshape(2, groups, stripe, tp_count, stripe)
        previous = shifted(rounded, "ta", 1)
        earliest = shifted(rounded, "ta", 2)
        hamilton_term = jnp.dot(
            current.reshape(-1, block_width), blocked, precision=highest
        ).reshape(2, columns, block_rows)
        selected = []
        nearby = jnp.stack(
            [
                lax.dynamic_index_in_dim(
                    outgoing, jnp.minimum(ta_place + step_ahead, groups - 1), 1, keepdims=False
                )
                for step_ahead in range(3)
            ],
            1,
        )
        spread = lax.all_to_all(nearby, "tp", split_axis=3, concat_axis=3, tiled=True)
        from_one = shifted(spread[:, 1], "ta", 1)
        from_two = shifted(spread[:, 2], "ta", 2)
        received = (from_two, from_one, spread[:, 0])
        by_current = current.reshape(2, groups, stripe, block_rows)
        for window_index in range(3):
            group_pick = jnp.maximum(ta_place - 2 + window_index, 0)
            own_part = lax.dynamic_index_in_dim(by_current, group_pick, 1, keepdims=False)
            flipped = (
                jnp.transpose(received[window_index], (0, 3, 2, 1))
                .reshape(2, stripe, block_rows)
                .astype(jnp.float32)
            )
            selected.append(self_energy(own_part, flipped, coupling[:stripe]))
        oldest = jnp.where(is_later[None], selected[0], 0.0)
        middle = selected[1]
        newest = jnp.where(is_later[None], 0.0, selected[2])
        sending = jnp.stack([oldest + newest, middle], 1).astype(jnp.bfloat16)[:, :, None]
        portion = lax.all_gather(sending, "tp", axis=2, tiled=True)
        row_count = portion.shape[2] * stripe
        arriving_time = jnp.arange(row_count, dtype=jnp.int32) // NO
        later_here = (arriving_time[:, None] > row_time[None, :])[None]
        merged = portion[:, 0].reshape(2, row_count, block_rows)
        recent = portion[:, 1].reshape(2, row_count, block_rows)
        right_side = jnp.concatenate(
            [
                jnp.where(later_here, merged, zero_half),
                recent,
                jnp.where(later_here, zero_half, merged),
            ],
            1,
        )
        memory = accumulate(
            jnp.concatenate([source for source in (earliest, previous, rounded)], 2), right_side
        )
        next_real = current[0] + 0.5 * (hamilton_term[1] + factor * memory[1])
        next_imag = current[1] - 0.5 * (hamilton_term[0] + factor * memory[0])
        current = jnp.stack([next_real, next_imag])
    return current.reshape(2, groups, 1, stripe, block_rows)


def exchange_orders(ta_count, tp_count):
    tp_bits = [1 << bit for bit in reversed(range(1, tp_count.bit_length() - 1))]
    high, low, ta_bit = tp_bits[:-1], tp_bits[-1:], [tp_count]
    turned = high[::-1]
    return [
        (high + low + ta_bit, turned + low + ta_bit),
        (low + ta_bit + high, low + ta_bit + turned),
    ]


def gathered(pieces, orders, count):
    swap = [(i, i ^ 1) for i in range(count)]
    held = [piece[None] for piece in pieces]
    near = [[] for _ in pieces]
    far = [[] for _ in pieces]
    steps = len(orders[0][0])
    for step in range(steps):
        for index, (even, odd) in enumerate(orders):
            masks = (even[step], odd[step])
            route = [(i, i ^ masks[i % 2]) for i in range(count)]
            arriving = lax.ppermute(held[index], ("ta", "tp"), route)
            if step == steps - 1:
                near[index] = [held[index], arriving]
                far[index] = [lax.ppermute(part, ("ta", "tp"), swap) for part in near[index]]
            else:
                held[index] = jnp.concatenate([held[index], arriving])
    return [near[index] + far[index] for index in range(len(pieces))]


def offsets_of(order):
    offsets = [0]
    for mask in order:
        offsets = offsets + [known ^ mask for known in offsets]
    return offsets


def bf16_dot(left_side, right_side):
    return lax.dot_general(
        left_side, right_side, (((1,), (0,)), ((), ())), preferred_element_type=jnp.float32
    )


def make_iterations(orders, ta_count, tp_count, stripe, block_rows, factor):
    order_size = ta_count * block_rows
    offsets = [[offsets_of(order) for order in pair] for pair in orders]
    half = jnp.bfloat16

    def square_of(values):
        real, imag = values
        return real * real - imag * imag, 2.0 * real * imag

    def window_of(values, mirror, weights, first_time):
        rows, width = values[0].shape
        real_square, imag_square = square_of(values)
        mirror_real = mirror[0].astype(jnp.float32)
        mirror_imag = mirror[1].astype(jnp.float32)
        real = real_square * mirror_real - imag_square * mirror_imag
        imag = real_square * mirror_imag + imag_square * mirror_real
        source_time = lax.broadcasted_iota(jnp.int32, (rows, width), 0) // NO
        target_time = lax.broadcasted_iota(jnp.int32, (rows, width), 1) // NO + first_time
        inside = source_time <= target_time

        def weighted(part):
            part = (part.reshape(rows // NO, NO, width) * weights[None]).reshape(rows, width)
            return jnp.where(inside, part, 0.0).astype(half)

        return weighted(real), weighted(imag)

    def products(left_side, right_side):
        real = bf16_dot(left_side[0], right_side[0]) - bf16_dot(left_side[1], right_side[1])
        imag = bf16_dot(left_side[0], right_side[1]) + bf16_dot(left_side[1], right_side[0])
        return real, imag

    def rotated(values, high_table, low_table):
        high = values.astype(half)
        low = (values - high.astype(jnp.float32)).astype(half)
        return (
            bf16_dot(high, high_table) + bf16_dot(low, high_table) + bf16_dot(high, low_table)
        )

    def repeated(tile):
        return jnp.concatenate([tile] * (block_rows // NO), axis=1)

    def kernel(*refs):
        sources = refs[: 4 * ta_count]
        hamiltonian, interaction, out, values, lows, nexts, low_next = refs[4 * ta_count :]
        ta_place = lax.axis_index("ta")
        tp_place = lax.axis_index("tp")
        me = ta_place * tp_count + tp_place
        odd = me % 2
        for group in range(ta_count):
            for flip in range(2):
                pair = offsets[group]
                steps = len(pair[0])
                for index in range(steps):
                    late, slot = divmod(index, steps // 2)
                    source = sources[4 * group + 2 * flip + late]
                    mask = jnp.where(odd == flip, pair[0][index], pair[1][index])
                    device = (me ^ flip) ^ mask
                    row = pl.multiple_of((device % tp_count) * stripe, stripe)
                    block = device // tp_count
                    for part in range(2):
                        values[part, block, group, pl.ds(row, stripe), :] = source[slot, part]
        weights = repeated(jnp.transpose(interaction[...] * interaction[...]))
        table = jnp.concatenate([repeated(jnp.transpose(hamiltonian[...]))] * (block_rows // NO))
        same_time = (
            lax.broadcasted_iota(jnp.int32, table.shape, 0) // NO
            == lax.broadcasted_iota(jnp.int32, table.shape, 1) // NO
        )
        table = jnp.where(same_time, table, 0.0)
        high_table = table.astype(half)
        low_table = (table - high_table.astype(jnp.float32)).astype(half)
        for block in range(ta_count):
            for part in range(2):
                for group in range(ta_count):
                    lows[part, group, :, block * block_rows : (block + 1) * block_rows] = values[
                        part, block, group
                    ].astype(half)
        rounded = [lows[part].reshape(order_size, order_size) for part in range(2)]
        for block in range(ta_count):
            current = [values[part, block].reshape(order_size, block_rows) for part in range(2)]
            mirror = [
                jnp.transpose(lows[part, block].astype(jnp.float32)) for part in range(2)
            ]
            window = window_of(current, mirror, weights, block * (block_rows // NO))
            memory = products(rounded, window)
            hamilton = [rotated(current[part], high_table, low_table) for part in range(2)]
            shape = (ta_count, block_rows, block_rows)
            next_real = current[0] + 0.5 * (hamilton[1] + factor * memory[1])
            next_imag = current[1] - 0.5 * (hamilton[0] + factor * memory[0])
            for part, result in ((0, next_real), (1, next_imag)):
                nexts[part, block] = result.reshape(shape)
                low_next[part, :, :, block * block_rows : (block + 1) * block_rows] = (
                    result.reshape(shape).astype(half)
                )
        current = [nexts[part, ta_place].reshape(order_size, block_rows) for part in range(2)]
        mirror = [
            jnp.transpose(low_next[part, ta_place].astype(jnp.float32)) for part in range(2)
        ]
        window = window_of(current, mirror, weights, ta_place * (block_rows // NO))
        row = pl.multiple_of(tp_place * stripe, stripe)
        own = [
            nexts[part, ta_place, :, pl.ds(row, stripe), :].reshape(ta_count * stripe, block_rows)
            for part in range(2)
        ]
        own_rounded = [
            low_next[part, :, pl.ds(row, stripe), :].reshape(ta_count * stripe, order_size)
            for part in range(2)
        ]
        memory = products(own_rounded, window)
        hamilton = [rotated(own[part], high_table, low_table) for part in range(2)]
        shape = (ta_count, stripe, block_rows)
        out[0] = (own[0] + 0.5 * (hamilton[1] + factor * memory[1])).reshape(shape)
        out[1] = (own[1] - 0.5 * (hamilton[0] + factor * memory[0])).reshape(shape)

    big = (2, ta_count, ta_count, block_rows, block_rows)
    flat = (2, ta_count, block_rows, order_size)
    return pl.pallas_call(
        kernel,
        out_shape=jax.ShapeDtypeStruct((2, ta_count, stripe, block_rows), jnp.float32),
        in_specs=[pl.BlockSpec(memory_space=pltpu.VMEM)] * (4 * ta_count + 2),
        out_specs=pl.BlockSpec(memory_space=pltpu.VMEM),
        scratch_shapes=[
            pltpu.VMEM(big, jnp.float32),
            pltpu.VMEM(flat, half),
            pltpu.VMEM(big, jnp.float32),
            pltpu.VMEM(flat, half),
        ],
        compiler_params=pltpu.CompilerParams(vmem_limit_bytes=24 << 20),
        name="iterations",
    )


def replicated(green, hamiltonian, interaction):
    ta_count = lax.axis_size("ta")
    tp_count = lax.axis_size("tp")
    stripe = green.shape[3]
    block_rows = green.shape[4]
    factor = 1.0 / math.sqrt(2 * block_rows)
    orders = exchange_orders(ta_count, tp_count)
    count = ta_count * tp_count
    pieces = [green[:, group, 0] for group in range(ta_count)]
    sources = sum(gathered(pieces, orders, count), [])
    step = make_iterations(orders, ta_count, tp_count, stripe, block_rows, factor)
    result = step(*sources, hamiltonian, interaction)
    return result[:, :, None]


def solution(mesh):
    in_specs = (P(None, None, "tp", None, "ta"), P(), P())
    out_specs = P(None, None, "tp", None, "ta")
    ta_count = mesh.shape["ta"]
    tp_count = mesh.shape["tp"]

    def shards(green, hamiltonian, interaction):
        whole_bytes = green.size * green.dtype.itemsize * ta_count * tp_count
        covered = ta_count == 2 and green.shape[1] == 2 and tp_count >= 4
        if covered and tp_count & (tp_count - 1) == 0 and whole_bytes <= 1 << 22:
            return replicated(green, hamiltonian, interaction)
        return windowed(green, hamiltonian, interaction)

    return jax.shard_map(shards, mesh=mesh, in_specs=in_specs, out_specs=out_specs, check_vma=False)
```

```python
import math

import jax
import jax.numpy as jnp
from jax import lax
from jax.experimental import pallas as pl
from jax.experimental.pallas import tpu as pltpu
from jax.sharding import PartitionSpec as P

NO = 32
ITERS = 2


highest = lax.Precision.HIGHEST


def shifted(block, axis, distance):
    devices = range(lax.axis_size(axis))
    route = [(i - distance, i) for i in devices if i - distance in devices]
    return lax.ppermute(block, axis, route)


def half_dot(left_side, right_side):
    return jnp.dot(left_side, right_side, preferred_element_type=jnp.float32)


def accumulate(left_side, right_side):
    product_real = half_dot(left_side[0], right_side[0]) - half_dot(left_side[1], right_side[1])
    product_imag = half_dot(left_side[0], right_side[1]) + half_dot(left_side[1], right_side[0])
    return (product_real, product_imag)


def self_energy(values, mirror_part, weights):
    real_square = values[0] * values[0] - values[1] * values[1]
    imag_square = 2.0 * values[0] * values[1]
    sigma_real = weights * (real_square * mirror_part[0] - imag_square * mirror_part[1])
    sigma_imag = weights * (real_square * mirror_part[1] + imag_square * mirror_part[0])
    return jnp.stack([sigma_real, sigma_imag])


def windowed(green, hamiltonian, interaction):
    tp_count = lax.axis_size("tp")
    ta_place = lax.axis_index("ta")
    tp_place = lax.axis_index("tp")
    groups = green.shape[1]
    stripe = green.shape[3]
    block_rows = green.shape[4]
    columns = groups * stripe
    factor = 1.0 / math.sqrt(2 * block_rows)
    current = green[:, :, 0].reshape(2, columns, block_rows)
    squared = interaction * interaction
    column_global = (
        jnp.arange(groups, dtype=jnp.int32)[:, None] * tp_count + tp_place
    ) * stripe + jnp.arange(stripe, dtype=jnp.int32)[None, :]
    column_orbital = (column_global % NO).reshape(columns)
    onehot = (column_orbital[:, None] == jnp.arange(NO, dtype=jnp.int32)[None, :]).astype(
        jnp.float32
    )
    lookup_table = jnp.dot(onehot, squared.T, precision=highest)
    coupling = jnp.tile(lookup_table, (1, block_rows // NO))
    row_time = jnp.arange(block_rows, dtype=jnp.int32) // NO
    column_time = (tp_place * stripe + jnp.arange(stripe, dtype=jnp.int32)) // NO
    is_later = column_time[:, None] > row_time[None, :]
    block_width = math.gcd(block_rows, 128)
    blocked = jnp.kron(jnp.eye(block_width // NO, dtype=jnp.float32), hamiltonian.T)
    zero_half = jnp.zeros((), jnp.bfloat16)
    for iteration in range(ITERS):
        rounded = current.astype(jnp.bfloat16)
        outgoing = rounded.reshape(2, groups, stripe, tp_count, stripe)
        previous = shifted(rounded, "ta", 1)
        earliest = shifted(rounded, "ta", 2)
        hamilton_term = jnp.dot(
            current.reshape(-1, block_width), blocked, precision=highest
        ).reshape(2, columns, block_rows)
        selected = []
        nearby = jnp.stack(
            [
                lax.dynamic_index_in_dim(
                    outgoing, jnp.minimum(ta_place + step_ahead, groups - 1), 1, keepdims=False
                )
                for step_ahead in range(3)
            ],
            1,
        )
        spread = lax.all_to_all(nearby, "tp", split_axis=3, concat_axis=3, tiled=True)
        from_one = shifted(spread[:, 1], "ta", 1)
        from_two = shifted(spread[:, 2], "ta", 2)
        received = (from_two, from_one, spread[:, 0])
        by_current = current.reshape(2, groups, stripe, block_rows)
        for window_index in range(3):
            group_pick = jnp.maximum(ta_place - 2 + window_index, 0)
            own_part = lax.dynamic_index_in_dim(by_current, group_pick, 1, keepdims=False)
            flipped = (
                jnp.transpose(received[window_index], (0, 3, 2, 1))
                .reshape(2, stripe, block_rows)
                .astype(jnp.float32)
            )
            selected.append(self_energy(own_part, flipped, coupling[:stripe]))
        oldest = jnp.where(is_later[None], selected[0], 0.0)
        middle = selected[1]
        newest = jnp.where(is_later[None], 0.0, selected[2])
        sending = jnp.stack([oldest + newest, middle], 1).astype(jnp.bfloat16)[:, :, None]
        portion = lax.all_gather(sending, "tp", axis=2, tiled=True)
        row_count = portion.shape[2] * stripe
        arriving_time = jnp.arange(row_count, dtype=jnp.int32) // NO
        later_here = (arriving_time[:, None] > row_time[None, :])[None]
        merged = portion[:, 0].reshape(2, row_count, block_rows)
        recent = portion[:, 1].reshape(2, row_count, block_rows)
        right_side = jnp.concatenate(
            [
                jnp.where(later_here, merged, zero_half),
                recent,
                jnp.where(later_here, zero_half, merged),
            ],
            1,
        )
        memory = accumulate(
            jnp.concatenate([source for source in (earliest, previous, rounded)], 2), right_side
        )
        next_real = current[0] + 0.5 * (hamilton_term[1] + factor * memory[1])
        next_imag = current[1] - 0.5 * (hamilton_term[0] + factor * memory[0])
        current = jnp.stack([next_real, next_imag])
    return current.reshape(2, groups, 1, stripe, block_rows)


def exchange_orders(ta_count, tp_count):
    tp_bits = [1 << bit for bit in reversed(range(1, tp_count.bit_length() - 1))]
    first, middle, last, ta_bit = tp_bits[:1], tp_bits[1:-1], tp_bits[-1:], [tp_count]
    return [
        (first + last + ta_bit + middle,) * 2,
        (ta_bit + first + middle + last,) * 2,
    ]


def gathered(pieces, orders, count):
    swap = [(i, i ^ 1) for i in range(count)]
    held = [piece[None] for piece in pieces]
    near = [[] for _ in pieces]
    far = [[] for _ in pieces]
    steps = len(orders[0][0])
    for step in range(steps):
        for index, (even, odd) in enumerate(orders):
            masks = (even[step], odd[step])
            route = [(i, i ^ masks[i % 2]) for i in range(count)]
            arriving = lax.ppermute(held[index], ("ta", "tp"), route)
            if step == steps - 1:
                near[index] = [held[index], arriving]
                far[index] = [lax.ppermute(part, ("ta", "tp"), swap) for part in near[index]]
            else:
                held[index] = jnp.concatenate([held[index], arriving])
    return [near[index] + far[index] for index in range(len(pieces))]


def offsets_of(order):
    offsets = [0]
    for mask in order:
        offsets = offsets + [known ^ mask for known in offsets]
    return offsets


def bf16_dot(left_side, right_side):
    return lax.dot_general(
        left_side, right_side, (((1,), (0,)), ((), ())), preferred_element_type=jnp.float32
    )


def make_iterations(orders, ta_count, tp_count, stripe, block_rows, factor):
    order_size = ta_count * block_rows
    offsets = [[offsets_of(order) for order in pair] for pair in orders]
    half = jnp.bfloat16

    def square_of(values):
        real, imag = values
        return real * real - imag * imag, 2.0 * real * imag

    def window_of(values, mirror, weights, first_time):
        rows, width = values[0].shape
        real_square, imag_square = square_of(values)
        mirror_real = mirror[0].astype(jnp.float32)
        mirror_imag = mirror[1].astype(jnp.float32)
        real = real_square * mirror_real - imag_square * mirror_imag
        imag = real_square * mirror_imag + imag_square * mirror_real
        source_time = lax.broadcasted_iota(jnp.int32, (rows, width), 0) // NO
        target_time = lax.broadcasted_iota(jnp.int32, (rows, width), 1) // NO + first_time
        inside = source_time <= target_time

        def weighted(part):
            part = (part.reshape(rows // NO, NO, width) * weights[None]).reshape(rows, width)
            return jnp.where(inside, part, 0.0).astype(half)

        return weighted(real), weighted(imag)

    def products(left_side, right_side):
        real = bf16_dot(left_side[0], right_side[0]) - bf16_dot(left_side[1], right_side[1])
        imag = bf16_dot(left_side[0], right_side[1]) + bf16_dot(left_side[1], right_side[0])
        return real, imag

    def rotated(values, high_table, low_table):
        high = values.astype(half)
        low = (values - high.astype(jnp.float32)).astype(half)
        return (
            bf16_dot(high, high_table) + bf16_dot(low, high_table) + bf16_dot(high, low_table)
        )

    def repeated(tile):
        return jnp.concatenate([tile] * (block_rows // NO), axis=1)

    def kernel(*refs):
        sources = refs[: 4 * ta_count]
        hamiltonian, interaction, out, values, lows, nexts, low_next = refs[4 * ta_count :]
        ta_place = lax.axis_index("ta")
        tp_place = lax.axis_index("tp")
        me = ta_place * tp_count + tp_place
        odd = me % 2
        for group in range(ta_count):
            for flip in range(2):
                pair = offsets[group]
                steps = len(pair[0])
                for index in range(steps):
                    late, slot = divmod(index, steps // 2)
                    source = sources[4 * group + 2 * flip + late]
                    mask = jnp.where(odd == flip, pair[0][index], pair[1][index])
                    device = (me ^ flip) ^ mask
                    row = pl.multiple_of((device % tp_count) * stripe, stripe)
                    block = device // tp_count
                    for part in range(2):
                        values[part, block, group, pl.ds(row, stripe), :] = source[slot, part]
        weights = repeated(jnp.transpose(interaction[...] * interaction[...]))
        table = jnp.concatenate([repeated(jnp.transpose(hamiltonian[...]))] * (block_rows // NO))
        same_time = (
            lax.broadcasted_iota(jnp.int32, table.shape, 0) // NO
            == lax.broadcasted_iota(jnp.int32, table.shape, 1) // NO
        )
        table = jnp.where(same_time, table, 0.0)
        high_table = table.astype(half)
        low_table = (table - high_table.astype(jnp.float32)).astype(half)
        for block in range(ta_count):
            for part in range(2):
                for group in range(ta_count):
                    lows[part, group, :, block * block_rows : (block + 1) * block_rows] = values[
                        part, block, group
                    ].astype(half)
        rounded = [lows[part].reshape(order_size, order_size) for part in range(2)]
        for block in range(ta_count):
            current = [values[part, block].reshape(order_size, block_rows) for part in range(2)]
            width = (block + 1) * block_rows
            mirror = [
                jnp.transpose(lows[part, block, :, :width].astype(jnp.float32))
                for part in range(2)
            ]
            window = window_of(
                [current[part][:width] for part in range(2)],
                mirror,
                weights,
                block * (block_rows // NO),
            )
            memory = products([rounded[part][:, :width] for part in range(2)], window)
            hamilton = [rotated(current[part], high_table, low_table) for part in range(2)]
            shape = (ta_count, block_rows, block_rows)
            next_real = current[0] + 0.5 * (hamilton[1] + factor * memory[1])
            next_imag = current[1] - 0.5 * (hamilton[0] + factor * memory[0])
            for part, result in ((0, next_real), (1, next_imag)):
                nexts[part, block] = result.reshape(shape)
                low_next[part, :, :, block * block_rows : (block + 1) * block_rows] = (
                    result.reshape(shape).astype(half)
                )
        current = [nexts[part, ta_place].reshape(order_size, block_rows) for part in range(2)]
        mirror = [
            jnp.transpose(low_next[part, ta_place].astype(jnp.float32)) for part in range(2)
        ]
        window = window_of(current, mirror, weights, ta_place * (block_rows // NO))
        row = pl.multiple_of(tp_place * stripe, stripe)
        own = [
            nexts[part, ta_place, :, pl.ds(row, stripe), :].reshape(ta_count * stripe, block_rows)
            for part in range(2)
        ]
        own_rounded = [
            low_next[part, :, pl.ds(row, stripe), :].reshape(ta_count * stripe, order_size)
            for part in range(2)
        ]
        memory = products(own_rounded, window)
        hamilton = [rotated(own[part], high_table, low_table) for part in range(2)]
        shape = (ta_count, stripe, block_rows)
        out[0] = (own[0] + 0.5 * (hamilton[1] + factor * memory[1])).reshape(shape)
        out[1] = (own[1] - 0.5 * (hamilton[0] + factor * memory[0])).reshape(shape)

    big = (2, ta_count, ta_count, block_rows, block_rows)
    flat = (2, ta_count, block_rows, order_size)
    return pl.pallas_call(
        kernel,
        out_shape=jax.ShapeDtypeStruct((2, ta_count, stripe, block_rows), jnp.float32),
        in_specs=[pl.BlockSpec(memory_space=pltpu.VMEM)] * (4 * ta_count + 2),
        out_specs=pl.BlockSpec(memory_space=pltpu.VMEM),
        scratch_shapes=[
            pltpu.VMEM(big, jnp.float32),
            pltpu.VMEM(flat, half),
            pltpu.VMEM(big, jnp.float32),
            pltpu.VMEM(flat, half),
        ],
        compiler_params=pltpu.CompilerParams(vmem_limit_bytes=24 << 20),
        name="iterations",
    )


def replicated(green, hamiltonian, interaction):
    ta_count = lax.axis_size("ta")
    tp_count = lax.axis_size("tp")
    stripe = green.shape[3]
    block_rows = green.shape[4]
    factor = 1.0 / math.sqrt(2 * block_rows)
    orders = exchange_orders(ta_count, tp_count)
    count = ta_count * tp_count
    pieces = [green[:, group, 0] for group in range(ta_count)]
    sources = sum(gathered(pieces, orders, count), [])
    step = make_iterations(orders, ta_count, tp_count, stripe, block_rows, factor)
    result = step(*sources, hamiltonian, interaction)
    return result[:, :, None]


def solution(mesh):
    in_specs = (P(None, None, "tp", None, "ta"), P(), P())
    out_specs = P(None, None, "tp", None, "ta")
    ta_count = mesh.shape["ta"]
    tp_count = mesh.shape["tp"]

    def shards(green, hamiltonian, interaction):
        whole_bytes = green.size * green.dtype.itemsize * ta_count * tp_count
        covered = ta_count == 2 and green.shape[1] == 2 and tp_count >= 8
        if covered and tp_count & (tp_count - 1) == 0 and whole_bytes <= 1 << 22:
            return replicated(green, hamiltonian, interaction)
        return windowed(green, hamiltonian, interaction)

    return jax.shard_map(shards, mesh=mesh, in_specs=in_specs, out_specs=out_specs, check_vma=False)
```

```python
import math

import jax
import jax.numpy as jnp
from jax import lax
from jax.experimental import pallas as pl
from jax.experimental.pallas import tpu as pltpu
from jax.sharding import PartitionSpec as P

NO = 32
ITERS = 2


highest = lax.Precision.HIGHEST


def shifted(block, axis, distance):
    devices = range(lax.axis_size(axis))
    route = [(i - distance, i) for i in devices if i - distance in devices]
    return lax.ppermute(block, axis, route)


def half_dot(left_side, right_side):
    return jnp.dot(left_side, right_side, preferred_element_type=jnp.float32)


def accumulate(left_side, right_side):
    product_real = half_dot(left_side[0], right_side[0]) - half_dot(left_side[1], right_side[1])
    product_imag = half_dot(left_side[0], right_side[1]) + half_dot(left_side[1], right_side[0])
    return (product_real, product_imag)


def self_energy(values, mirror_part, weights):
    real_square = values[0] * values[0] - values[1] * values[1]
    imag_square = 2.0 * values[0] * values[1]
    sigma_real = weights * (real_square * mirror_part[0] - imag_square * mirror_part[1])
    sigma_imag = weights * (real_square * mirror_part[1] + imag_square * mirror_part[0])
    return jnp.stack([sigma_real, sigma_imag])


def windowed(green, hamiltonian, interaction):
    tp_count = lax.axis_size("tp")
    ta_place = lax.axis_index("ta")
    tp_place = lax.axis_index("tp")
    groups = green.shape[1]
    stripe = green.shape[3]
    block_rows = green.shape[4]
    columns = groups * stripe
    factor = 1.0 / math.sqrt(2 * block_rows)
    current = green[:, :, 0].reshape(2, columns, block_rows)
    squared = interaction * interaction
    column_global = (
        jnp.arange(groups, dtype=jnp.int32)[:, None] * tp_count + tp_place
    ) * stripe + jnp.arange(stripe, dtype=jnp.int32)[None, :]
    column_orbital = (column_global % NO).reshape(columns)
    onehot = (column_orbital[:, None] == jnp.arange(NO, dtype=jnp.int32)[None, :]).astype(
        jnp.float32
    )
    lookup_table = jnp.dot(onehot, squared.T, precision=highest)
    coupling = jnp.tile(lookup_table, (1, block_rows // NO))
    row_time = jnp.arange(block_rows, dtype=jnp.int32) // NO
    column_time = (tp_place * stripe + jnp.arange(stripe, dtype=jnp.int32)) // NO
    is_later = column_time[:, None] > row_time[None, :]
    block_width = math.gcd(block_rows, 128)
    blocked = jnp.kron(jnp.eye(block_width // NO, dtype=jnp.float32), hamiltonian.T)
    zero_half = jnp.zeros((), jnp.bfloat16)
    for iteration in range(ITERS):
        rounded = current.astype(jnp.bfloat16)
        outgoing = rounded.reshape(2, groups, stripe, tp_count, stripe)
        previous = shifted(rounded, "ta", 1)
        earliest = shifted(rounded, "ta", 2)
        hamilton_term = jnp.dot(
            current.reshape(-1, block_width), blocked, precision=highest
        ).reshape(2, columns, block_rows)
        selected = []
        nearby = jnp.stack(
            [
                lax.dynamic_index_in_dim(
                    outgoing, jnp.minimum(ta_place + step_ahead, groups - 1), 1, keepdims=False
                )
                for step_ahead in range(3)
            ],
            1,
        )
        spread = lax.all_to_all(nearby, "tp", split_axis=3, concat_axis=3, tiled=True)
        from_one = shifted(spread[:, 1], "ta", 1)
        from_two = shifted(spread[:, 2], "ta", 2)
        received = (from_two, from_one, spread[:, 0])
        by_current = current.reshape(2, groups, stripe, block_rows)
        for window_index in range(3):
            group_pick = jnp.maximum(ta_place - 2 + window_index, 0)
            own_part = lax.dynamic_index_in_dim(by_current, group_pick, 1, keepdims=False)
            flipped = (
                jnp.transpose(received[window_index], (0, 3, 2, 1))
                .reshape(2, stripe, block_rows)
                .astype(jnp.float32)
            )
            selected.append(self_energy(own_part, flipped, coupling[:stripe]))
        oldest = jnp.where(is_later[None], selected[0], 0.0)
        middle = selected[1]
        newest = jnp.where(is_later[None], 0.0, selected[2])
        sending = jnp.stack([oldest + newest, middle], 1).astype(jnp.bfloat16)[:, :, None]
        portion = lax.all_gather(sending, "tp", axis=2, tiled=True)
        row_count = portion.shape[2] * stripe
        arriving_time = jnp.arange(row_count, dtype=jnp.int32) // NO
        later_here = (arriving_time[:, None] > row_time[None, :])[None]
        merged = portion[:, 0].reshape(2, row_count, block_rows)
        recent = portion[:, 1].reshape(2, row_count, block_rows)
        right_side = jnp.concatenate(
            [
                jnp.where(later_here, merged, zero_half),
                recent,
                jnp.where(later_here, zero_half, merged),
            ],
            1,
        )
        memory = accumulate(
            jnp.concatenate([source for source in (earliest, previous, rounded)], 2), right_side
        )
        next_real = current[0] + 0.5 * (hamilton_term[1] + factor * memory[1])
        next_imag = current[1] - 0.5 * (hamilton_term[0] + factor * memory[0])
        current = jnp.stack([next_real, next_imag])
    return current.reshape(2, groups, 1, stripe, block_rows)


def exchange_masks(ta_count, tp_count):
    bits = [1 << bit for bit in reversed(range(1, tp_count.bit_length() - 1))]
    first, middle, last = bits[:1], bits[1:-1], bits[-1:]
    return first + last + [ta_count * tp_count // 2] + middle, first + middle + last


def offsets_of(masks):
    offsets = [0]
    for mask in masks:
        offsets = offsets + [known ^ mask for known in offsets]
    return offsets


def bf16_dot(left_side, right_side):
    return lax.dot_general(
        left_side, right_side, (((1,), (0,)), ((), ())), preferred_element_type=jnp.float32
    )


def halves(values):
    high = values.astype(jnp.bfloat16)
    return high, (values - high.astype(jnp.float32)).astype(jnp.bfloat16)


def window_of(values, mirror, weights, first_time):
    rows, width = values[0].shape
    real_square = values[0] * values[0] - values[1] * values[1]
    imag_square = 2.0 * values[0] * values[1]
    real = real_square * mirror[0] - imag_square * mirror[1]
    imag = real_square * mirror[1] + imag_square * mirror[0]
    source_time = lax.broadcasted_iota(jnp.int32, (rows, width), 0) // NO
    target_time = lax.broadcasted_iota(jnp.int32, (rows, width), 1) // NO + first_time
    inside = source_time <= target_time

    def weighted(part):
        part = (part.reshape(rows // NO, NO, width) * weights[None]).reshape(rows, width)
        return jnp.where(inside, part, 0.0).astype(jnp.bfloat16)

    return weighted(real), weighted(imag)


def mirrored(rounded):
    return [jnp.transpose(part.astype(jnp.float32)) for part in rounded]


def products(left_side, right_side):
    real = bf16_dot(left_side[0], right_side[0]) - bf16_dot(left_side[1], right_side[1])
    imag = bf16_dot(left_side[0], right_side[1]) + bf16_dot(left_side[1], right_side[0])
    return real, imag


def tables_of(hamiltonian, interaction, block_rows):
    def repeated(tile):
        return jnp.concatenate([tile] * (block_rows // NO), axis=1)

    weights = repeated(jnp.transpose(interaction[...] * interaction[...]))
    table = jnp.concatenate([repeated(jnp.transpose(hamiltonian[...]))] * (block_rows // NO))
    same_time = (
        lax.broadcasted_iota(jnp.int32, table.shape, 0) // NO
        == lax.broadcasted_iota(jnp.int32, table.shape, 1) // NO
    )
    return weights, halves(jnp.where(same_time, table, 0.0))


def one_body(values, high, low, table):
    turned = [
        bf16_dot(high[part], table[0])
        + bf16_dot(low[part], table[0])
        + bf16_dot(high[part], table[1])
        for part in range(2)
    ]
    return values[0] + 0.5 * turned[1], values[1] - 0.5 * turned[0]


def placed(tp_count, stripe, flip, mask):
    me = lax.axis_index("ta") * tp_count + lax.axis_index("tp")
    device = me ^ (flip ^ mask)
    return device // tp_count, pl.multiple_of((device % tp_count) * stripe, stripe)


def first_stage(masks, tp_count, stripe, block_rows, factor):
    offsets = offsets_of(masks)
    half_count = len(offsets) // 2

    def kernel(*refs):
        sources = refs[:4]
        hamiltonian, interaction, values, lows, bases, window = refs[4:]
        for flip in range(2):
            for index, mask in enumerate(offsets):
                late, slot = divmod(index, half_count)
                block, row = placed(tp_count, stripe, flip, mask)
                for part in range(2):
                    values[part, block, pl.ds(row, stripe), :] = sources[2 * flip + late][
                        slot, part
                    ]
        weights, table = tables_of(hamiltonian, interaction, block_rows)
        for block in range(2):
            current = [values[part, block] for part in range(2)]
            split = [halves(part) for part in current]
            high = [part[0] for part in split]
            base = one_body(current, high, [part[1] for part in split], table)
            for part in range(2):
                lows[part, :, block * block_rows : (block + 1) * block_rows] = high[part]
            if block == 0:
                made = window_of(current, mirrored(high), weights, 0)
                memory = products(high, made)
                scale = 0.5 * factor
                base = (base[0] + scale * memory[1], base[1] - scale * memory[0])
                window[0] = made[0]
                window[1] = made[1]
            bases[0, block] = base[0]
            bases[1, block] = base[1]

    block = jax.ShapeDtypeStruct((2, 2, block_rows, block_rows), jnp.float32)
    return pl.pallas_call(
        kernel,
        out_shape=[
            block,
            jax.ShapeDtypeStruct((2, block_rows, 2 * block_rows), jnp.bfloat16),
            block,
            jax.ShapeDtypeStruct((2, block_rows, block_rows), jnp.bfloat16),
        ],
        in_specs=[pl.BlockSpec(memory_space=pltpu.VMEM)] * 6,
        out_specs=[pl.BlockSpec(memory_space=pltpu.VMEM)] * 4,
        compiler_params=pltpu.CompilerParams(vmem_limit_bytes=16 << 20),
        name="first_stage",
    )


def second_stage(masks, tp_count, stripe, block_rows, factor):
    offsets = offsets_of(masks)
    half_count = len(offsets) // 2
    order_size = 2 * block_rows
    scale = 0.5 * factor

    def kernel(*refs):
        sources = refs[:4]
        hamiltonian, interaction, values, lows, bases, window = refs[4:10]
        out, highs, rests, nexts, low_next = refs[10:]
        ta_place = lax.axis_index("ta")
        tp_place = lax.axis_index("tp")
        for flip in range(2):
            for index, mask in enumerate(offsets):
                late, slot = divmod(index, half_count)
                block, row = placed(tp_count, stripe, flip, mask)
                source = sources[2 * flip + late]
                for part in range(2):
                    highs[part, block, pl.ds(row, stripe), :] = source[slot, 0, part]
                    highs[part, 1 - block, pl.ds(row, stripe), :] = source[slot, 1, part]
                    rests[part, block, pl.ds(row, stripe), :] = source[slot, 2, part]
                    rests[part, 1 - block, pl.ds(row, stripe), :] = jnp.zeros(
                        (stripe, block_rows), jnp.bfloat16
                    )
        weights, table = tables_of(hamiltonian, interaction, block_rows)
        high = [[highs[part, block] for part in range(2)] for block in range(2)]
        rest = [[rests[part, block] for part in range(2)] for block in range(2)]
        full = [
            [
                high[block][part].astype(jnp.float32) + rest[block][part].astype(jnp.float32)
                for part in range(2)
            ]
            for block in range(2)
        ]
        base = [one_body(full[block], high[block], rest[block], table) for block in range(2)]

        def stored(block, group, real, imag):
            for part, result in ((0, real), (1, imag)):
                nexts[part, block, group] = result
                low_next[part, group, :, block * block_rows : (block + 1) * block_rows] = (
                    result.astype(jnp.bfloat16)
                )

        stored(0, 0, bases[0, 0], bases[1, 0])
        memory = products(high[0], (window[0], window[1]))
        stored(0, 1, base[0][0] + scale * memory[1], base[0][1] - scale * memory[0])
        later = [
            window_of(
                [values[part, 1] for part in range(2)], mirrored(high[0]), weights, block_rows // NO
            ),
            window_of(full[1], mirrored(high[1]), weights, 0),
        ]
        rows = [[lows[part, :, :block_rows] for part in range(2)]]
        rows.append([lows[part, :, block_rows:] for part in range(2)])
        early_memory = [products(rows[0], later[0]), products(high[0], later[0])]
        late_memory = [products(rows[1], later[1]), products(high[1], later[1])]
        for group in range(2):
            start = (bases[0, 1], bases[1, 1]) if group == 0 else base[1]
            real = early_memory[group][0] + late_memory[group][0]
            imag = early_memory[group][1] + late_memory[group][1]
            stored(1, group, start[0] + scale * imag, start[1] - scale * real)

        current = [nexts[part, ta_place].reshape(order_size, block_rows) for part in range(2)]
        mirror = mirrored([low_next[part, ta_place] for part in range(2)])
        last = window_of(current, mirror, weights, ta_place * (block_rows // NO))
        row = pl.multiple_of(tp_place * stripe, stripe)
        own = [
            nexts[part, ta_place, :, pl.ds(row, stripe), :].reshape(2 * stripe, block_rows)
            for part in range(2)
        ]
        own_rounded = [
            low_next[part, :, pl.ds(row, stripe), :].reshape(2 * stripe, order_size)
            for part in range(2)
        ]
        memory = products(own_rounded, last)
        split = [halves(part) for part in own]
        real, imag = one_body(own, [part[0] for part in split], [part[1] for part in split], table)
        shape = (2, stripe, block_rows)
        out[0] = (real + scale * memory[1]).reshape(shape)
        out[1] = (imag - scale * memory[0]).reshape(shape)

    square = (2, 2, block_rows, block_rows)
    return pl.pallas_call(
        kernel,
        out_shape=jax.ShapeDtypeStruct((2, 2, stripe, block_rows), jnp.float32),
        in_specs=[pl.BlockSpec(memory_space=pltpu.VMEM)] * 10,
        out_specs=pl.BlockSpec(memory_space=pltpu.VMEM),
        scratch_shapes=[
            pltpu.VMEM(square, jnp.bfloat16),
            pltpu.VMEM(square, jnp.bfloat16),
            pltpu.VMEM((2,) + square, jnp.float32),
            pltpu.VMEM((2, 2, block_rows, order_size), jnp.bfloat16),
        ],
        compiler_params=pltpu.CompilerParams(vmem_limit_bytes=24 << 20),
        name="second_stage",
    )


def replicated(green, hamiltonian, interaction):
    tp_count = lax.axis_size("tp")
    count = 2 * tp_count
    stripe = green.shape[3]
    block_rows = green.shape[4]
    factor = 1.0 / math.sqrt(2 * block_rows)
    first_masks, second_masks = exchange_masks(2, tp_count)

    def exchanged(block, mask):
        return lax.ppermute(block, ("ta", "tp"), [(i, i ^ mask) for i in range(count)])

    first = green[:, 0, 0]
    second = green[:, 1, 0]
    high = lax.reduce_precision(second, 8, 7)
    low = (second - high).astype(jnp.bfloat16)
    high = high.astype(jnp.bfloat16)
    arriving = exchanged(first, first_masks[0])
    other_high = exchanged(high, tp_count)
    first = jnp.stack([first, arriving])
    second = jnp.stack([high, other_high, low])[None]
    for first_mask, second_mask in zip(first_masks[1:-1], second_masks[:-1]):
        arriving = exchanged(first, first_mask)
        second_arriving = exchanged(second, second_mask)
        first = jnp.concatenate([first, arriving])
        second = jnp.concatenate([second, second_arriving])
    first_parts = [first, exchanged(first, first_masks[-1])]
    second_parts = [second, exchanged(second, second_masks[-1])]
    first_parts += [exchanged(part, 1) for part in first_parts]
    second_parts += [exchanged(part, 1) for part in second_parts]
    early = first_stage(first_masks, tp_count, stripe, block_rows, factor)
    late = second_stage(second_masks, tp_count, stripe, block_rows, factor)
    known = early(*first_parts, hamiltonian, interaction)
    return late(*second_parts, hamiltonian, interaction, *known)[:, :, None]


def solution(mesh):
    in_specs = (P(None, None, "tp", None, "ta"), P(), P())
    out_specs = P(None, None, "tp", None, "ta")
    ta_count = mesh.shape["ta"]
    tp_count = mesh.shape["tp"]

    def shards(green, hamiltonian, interaction):
        whole_bytes = green.size * green.dtype.itemsize * ta_count * tp_count
        covered = ta_count == 2 and green.shape[1] == 2 and tp_count >= 8
        if covered and tp_count & (tp_count - 1) == 0 and whole_bytes <= 1 << 22:
            return replicated(green, hamiltonian, interaction)
        return windowed(green, hamiltonian, interaction)

    return jax.shard_map(shards, mesh=mesh, in_specs=in_specs, out_specs=out_specs, check_vma=False)
```

```python
import math

import jax
import jax.numpy as jnp
from jax import lax
from jax.experimental import pallas as pl
from jax.experimental.pallas import tpu as pltpu
from jax.sharding import PartitionSpec as P

NO = 32
ITERS = 2


highest = lax.Precision.HIGHEST


def shifted(block, axis, distance):
    devices = range(lax.axis_size(axis))
    route = [(i - distance, i) for i in devices if i - distance in devices]
    return lax.ppermute(block, axis, route)


def half_dot(left_side, right_side):
    return jnp.dot(left_side, right_side, preferred_element_type=jnp.float32)


def accumulate(left_side, right_side):
    product_real = half_dot(left_side[0], right_side[0]) - half_dot(left_side[1], right_side[1])
    product_imag = half_dot(left_side[0], right_side[1]) + half_dot(left_side[1], right_side[0])
    return (product_real, product_imag)


def self_energy(values, mirror_part, weights):
    real_square = values[0] * values[0] - values[1] * values[1]
    imag_square = 2.0 * values[0] * values[1]
    sigma_real = weights * (real_square * mirror_part[0] - imag_square * mirror_part[1])
    sigma_imag = weights * (real_square * mirror_part[1] + imag_square * mirror_part[0])
    return jnp.stack([sigma_real, sigma_imag])


def windowed(green, hamiltonian, interaction):
    tp_count = lax.axis_size("tp")
    ta_place = lax.axis_index("ta")
    tp_place = lax.axis_index("tp")
    groups = green.shape[1]
    stripe = green.shape[3]
    block_rows = green.shape[4]
    columns = groups * stripe
    factor = 1.0 / math.sqrt(2 * block_rows)
    current = green[:, :, 0].reshape(2, columns, block_rows)
    squared = interaction * interaction
    column_global = (
        jnp.arange(groups, dtype=jnp.int32)[:, None] * tp_count + tp_place
    ) * stripe + jnp.arange(stripe, dtype=jnp.int32)[None, :]
    column_orbital = (column_global % NO).reshape(columns)
    onehot = (column_orbital[:, None] == jnp.arange(NO, dtype=jnp.int32)[None, :]).astype(
        jnp.float32
    )
    lookup_table = jnp.dot(onehot, squared.T, precision=highest)
    coupling = jnp.tile(lookup_table, (1, block_rows // NO))
    row_time = jnp.arange(block_rows, dtype=jnp.int32) // NO
    column_time = (tp_place * stripe + jnp.arange(stripe, dtype=jnp.int32)) // NO
    is_later = column_time[:, None] > row_time[None, :]
    block_width = math.gcd(block_rows, 128)
    blocked = jnp.kron(jnp.eye(block_width // NO, dtype=jnp.float32), hamiltonian.T)
    zero_half = jnp.zeros((), jnp.bfloat16)
    for iteration in range(ITERS):
        rounded = current.astype(jnp.bfloat16)
        outgoing = rounded.reshape(2, groups, stripe, tp_count, stripe)
        previous = shifted(rounded, "ta", 1)
        earliest = shifted(rounded, "ta", 2)
        hamilton_term = jnp.dot(
            current.reshape(-1, block_width), blocked, precision=highest
        ).reshape(2, columns, block_rows)
        selected = []
        nearby = jnp.stack(
            [
                lax.dynamic_index_in_dim(
                    outgoing, jnp.minimum(ta_place + step_ahead, groups - 1), 1, keepdims=False
                )
                for step_ahead in range(3)
            ],
            1,
        )
        spread = lax.all_to_all(nearby, "tp", split_axis=3, concat_axis=3, tiled=True)
        from_one = shifted(spread[:, 1], "ta", 1)
        from_two = shifted(spread[:, 2], "ta", 2)
        received = (from_two, from_one, spread[:, 0])
        by_current = current.reshape(2, groups, stripe, block_rows)
        for window_index in range(3):
            group_pick = jnp.maximum(ta_place - 2 + window_index, 0)
            own_part = lax.dynamic_index_in_dim(by_current, group_pick, 1, keepdims=False)
            flipped = (
                jnp.transpose(received[window_index], (0, 3, 2, 1))
                .reshape(2, stripe, block_rows)
                .astype(jnp.float32)
            )
            selected.append(self_energy(own_part, flipped, coupling[:stripe]))
        oldest = jnp.where(is_later[None], selected[0], 0.0)
        middle = selected[1]
        newest = jnp.where(is_later[None], 0.0, selected[2])
        sending = jnp.stack([oldest + newest, middle], 1).astype(jnp.bfloat16)[:, :, None]
        portion = lax.all_gather(sending, "tp", axis=2, tiled=True)
        row_count = portion.shape[2] * stripe
        arriving_time = jnp.arange(row_count, dtype=jnp.int32) // NO
        later_here = (arriving_time[:, None] > row_time[None, :])[None]
        merged = portion[:, 0].reshape(2, row_count, block_rows)
        recent = portion[:, 1].reshape(2, row_count, block_rows)
        right_side = jnp.concatenate(
            [
                jnp.where(later_here, merged, zero_half),
                recent,
                jnp.where(later_here, zero_half, merged),
            ],
            1,
        )
        memory = accumulate(
            jnp.concatenate([source for source in (earliest, previous, rounded)], 2), right_side
        )
        next_real = current[0] + 0.5 * (hamilton_term[1] + factor * memory[1])
        next_imag = current[1] - 0.5 * (hamilton_term[0] + factor * memory[0])
        current = jnp.stack([next_real, next_imag])
    return current.reshape(2, groups, 1, stripe, block_rows)


def exchange_masks(ta_count, tp_count):
    bits = [1 << bit for bit in reversed(range(1, tp_count.bit_length() - 1))]
    first, middle, last = bits[0], bits[1:-1], bits[-1:]
    ta_bit = [ta_count * tp_count // 2]
    return first, middle + last + ta_bit, last + ta_bit + middle


def offsets_of(masks):
    offsets = [0]
    for mask in masks:
        offsets = offsets + [known ^ mask for known in offsets]
    return offsets


def bf16_dot(left_side, right_side):
    return lax.dot_general(
        left_side, right_side, (((1,), (0,)), ((), ())), preferred_element_type=jnp.float32
    )


def halves(values):
    high = values.astype(jnp.bfloat16)
    return high, (values - high.astype(jnp.float32)).astype(jnp.bfloat16)


def window_of(values, mirror, weights, first_time):
    rows, width = values[0].shape
    real_square = values[0] * values[0] - values[1] * values[1]
    imag_square = 2.0 * values[0] * values[1]
    real = real_square * mirror[0] - imag_square * mirror[1]
    imag = real_square * mirror[1] + imag_square * mirror[0]
    source_time = lax.broadcasted_iota(jnp.int32, (rows, width), 0) // NO
    target_time = lax.broadcasted_iota(jnp.int32, (rows, width), 1) // NO + first_time
    inside = source_time <= target_time

    def weighted(part):
        part = (part.reshape(rows // NO, NO, width) * weights[None]).reshape(rows, width)
        return jnp.where(inside, part, 0.0).astype(jnp.bfloat16)

    return weighted(real), weighted(imag)


def mirrored(rounded):
    return [jnp.transpose(part.astype(jnp.float32)) for part in rounded]


def products(left_side, right_side):
    real = bf16_dot(left_side[0], right_side[0]) - bf16_dot(left_side[1], right_side[1])
    imag = bf16_dot(left_side[0], right_side[1]) + bf16_dot(left_side[1], right_side[0])
    return real, imag


def tables_of(hamiltonian, interaction, block_rows):
    def repeated(tile):
        return jnp.concatenate([tile] * (block_rows // NO), axis=1)

    weights = repeated(jnp.transpose(interaction[...] * interaction[...]))
    table = jnp.concatenate([repeated(jnp.transpose(hamiltonian[...]))] * (block_rows // NO))
    same_time = (
        lax.broadcasted_iota(jnp.int32, table.shape, 0) // NO
        == lax.broadcasted_iota(jnp.int32, table.shape, 1) // NO
    )
    return weights, halves(jnp.where(same_time, table, 0.0))


def one_body(values, high, low, table):
    turned = [
        bf16_dot(high[part], table[0])
        + bf16_dot(low[part], table[0])
        + bf16_dot(high[part], table[1])
        for part in range(2)
    ]
    return values[0] + 0.5 * turned[1], values[1] - 0.5 * turned[0]


def first_stage(masks, tp_count, stripe, block_rows, factor):
    offsets = offsets_of(masks)
    half_count = len(offsets) // 2

    def kernel(*refs):
        sources = refs[:4]
        hamiltonian, interaction, values, lows, bases, window = refs[4:]
        me = lax.axis_index("ta") * tp_count + lax.axis_index("tp")
        for flip in range(2):
            for index, mask in enumerate(offsets):
                late, slot = divmod(index, half_count)
                device = me ^ (flip ^ mask)
                for part in range(2):
                    values[part, device] = sources[2 * flip + late][slot, part]
        weights, table = tables_of(hamiltonian, interaction, block_rows)
        for block in range(2):
            current = [
                values[part, block * tp_count : (block + 1) * tp_count].reshape(
                    block_rows, block_rows
                )
                for part in range(2)
            ]
            split = [halves(part) for part in current]
            high = [part[0] for part in split]
            base = one_body(current, high, [part[1] for part in split], table)
            for part in range(2):
                lows[part, :, block * block_rows : (block + 1) * block_rows] = high[part]
            if block == 0:
                made = window_of(current, mirrored(high), weights, 0)
                memory = products(high, made)
                scale = 0.5 * factor
                base = (base[0] + scale * memory[1], base[1] - scale * memory[0])
                window[0] = made[0]
                window[1] = made[1]
            bases[0, block] = base[0]
            bases[1, block] = base[1]

    block = jax.ShapeDtypeStruct((2, 2, block_rows, block_rows), jnp.float32)
    return pl.pallas_call(
        kernel,
        out_shape=[
            jax.ShapeDtypeStruct((2, 2 * tp_count, stripe, block_rows), jnp.float32),
            jax.ShapeDtypeStruct((2, block_rows, 2 * block_rows), jnp.bfloat16),
            block,
            jax.ShapeDtypeStruct((2, block_rows, block_rows), jnp.bfloat16),
        ],
        in_specs=[pl.BlockSpec(memory_space=pltpu.VMEM)] * 6,
        out_specs=[pl.BlockSpec(memory_space=pltpu.VMEM)] * 4,
        compiler_params=pltpu.CompilerParams(vmem_limit_bytes=16 << 20),
        name="first_stage",
    )


def second_stage(masks, tp_count, stripe, block_rows, factor):
    offsets = offsets_of(masks)
    half_count = len(offsets) // 2
    order_size = 2 * block_rows
    scale = 0.5 * factor

    def kernel(*refs):
        sources = refs[:4]
        hamiltonian, interaction, values, lows, bases, window = refs[4:10]
        out, highs, rests, nexts, low_next = refs[10:]
        ta_place = lax.axis_index("ta")
        tp_place = lax.axis_index("tp")
        me = ta_place * tp_count + tp_place
        blank = jnp.zeros((stripe, block_rows), jnp.bfloat16)
        for flip in range(2):
            for index, mask in enumerate(offsets):
                late, slot = divmod(index, half_count)
                device = me ^ (flip ^ mask)
                other = device ^ tp_count
                source = sources[2 * flip + late]
                for part in range(2):
                    highs[part, device] = source[slot, 0, part]
                    highs[part, other] = source[slot, 1, part]
                    rests[part, device] = source[slot, 2, part]
                    rests[part, other] = blank
        weights, table = tables_of(hamiltonian, interaction, block_rows)

        def whole(source, block):
            return [
                source[part, block * tp_count : (block + 1) * tp_count].reshape(
                    block_rows, block_rows
                )
                for part in range(2)
            ]

        high = [whole(highs, block) for block in range(2)]
        rest = [whole(rests, block) for block in range(2)]
        full = [
            [
                high[block][part].astype(jnp.float32) + rest[block][part].astype(jnp.float32)
                for part in range(2)
            ]
            for block in range(2)
        ]
        base = [one_body(full[block], high[block], rest[block], table) for block in range(2)]

        def stored(block, group, real, imag):
            for part, result in ((0, real), (1, imag)):
                nexts[part, block, group] = result
                low_next[part, group, :, block * block_rows : (block + 1) * block_rows] = (
                    result.astype(jnp.bfloat16)
                )

        stored(0, 0, bases[0, 0], bases[1, 0])
        memory = products(high[0], (window[0], window[1]))
        stored(0, 1, base[0][0] + scale * memory[1], base[0][1] - scale * memory[0])
        later = [
            window_of(whole(values, 1), mirrored(high[0]), weights, block_rows // NO),
            window_of(full[1], mirrored(high[1]), weights, 0),
        ]
        rows = [[lows[part, :, :block_rows] for part in range(2)]]
        rows.append([lows[part, :, block_rows:] for part in range(2)])
        early_memory = [products(rows[0], later[0]), products(high[0], later[0])]
        late_memory = [products(rows[1], later[1]), products(high[1], later[1])]
        for group in range(2):
            start = (bases[0, 1], bases[1, 1]) if group == 0 else base[1]
            real = early_memory[group][0] + late_memory[group][0]
            imag = early_memory[group][1] + late_memory[group][1]
            stored(1, group, start[0] + scale * imag, start[1] - scale * real)

        current = [nexts[part, ta_place].reshape(order_size, block_rows) for part in range(2)]
        mirror = mirrored([low_next[part, ta_place] for part in range(2)])
        last = window_of(current, mirror, weights, ta_place * (block_rows // NO))
        row = pl.multiple_of(tp_place * stripe, stripe)
        own = [
            nexts[part, ta_place, :, pl.ds(row, stripe), :].reshape(2 * stripe, block_rows)
            for part in range(2)
        ]
        own_rounded = [
            low_next[part, :, pl.ds(row, stripe), :].reshape(2 * stripe, order_size)
            for part in range(2)
        ]
        memory = products(own_rounded, last)
        split = [halves(part) for part in own]
        real, imag = one_body(own, [part[0] for part in split], [part[1] for part in split], table)
        shape = (2, stripe, block_rows)
        out[0] = (real + scale * memory[1]).reshape(shape)
        out[1] = (imag - scale * memory[0]).reshape(shape)

    square = (2, 2, block_rows, block_rows)
    return pl.pallas_call(
        kernel,
        out_shape=jax.ShapeDtypeStruct((2, 2, stripe, block_rows), jnp.float32),
        in_specs=[pl.BlockSpec(memory_space=pltpu.VMEM)] * 10,
        out_specs=pl.BlockSpec(memory_space=pltpu.VMEM),
        scratch_shapes=[
            pltpu.VMEM((2, 2 * tp_count, stripe, block_rows), jnp.bfloat16),
            pltpu.VMEM((2, 2 * tp_count, stripe, block_rows), jnp.bfloat16),
            pltpu.VMEM((2,) + square, jnp.float32),
            pltpu.VMEM((2, 2, block_rows, order_size), jnp.bfloat16),
        ],
        compiler_params=pltpu.CompilerParams(vmem_limit_bytes=24 << 20),
        name="second_stage",
    )


def replicated(green, hamiltonian, interaction):
    tp_count = lax.axis_size("tp")
    count = 2 * tp_count
    stripe = green.shape[3]
    block_rows = green.shape[4]
    factor = 1.0 / math.sqrt(2 * block_rows)
    mask, first_masks, second_masks = exchange_masks(2, tp_count)

    def exchanged(block, mask):
        return lax.ppermute(block, ("ta", "tp"), [(i, i ^ mask) for i in range(count)])

    arriving = exchanged(green.reshape(-1, block_rows), mask).reshape(green.shape)
    first = jnp.stack([green[:, 0, 0], arriving[:, 0, 0]])
    second = jnp.stack([green[:, 1, 0], arriving[:, 1, 0]])
    high = lax.reduce_precision(second, 8, 7)
    second = jnp.stack([high, second - high], 1).astype(jnp.bfloat16)
    first_parts = second_parts = ()
    for first_mask, second_mask in zip(first_masks, second_masks):
        first_parts = [first, exchanged(first, first_mask)]
        first = jnp.concatenate(first_parts)
        if second_mask == tp_count:
            other_high = exchanged(second[:, 0], second_mask)[:, None]
            second = jnp.concatenate([second[:, :1], other_high, second[:, 1:]], 1)
        else:
            second_parts = [second, exchanged(second, second_mask)]
            second = jnp.concatenate(second_parts)
    first_parts += [exchanged(part, 1) for part in first_parts]
    second_parts += [exchanged(part, 1) for part in second_parts]
    first_masks = [mask] + first_masks
    second_masks = [mask] + [later for later in second_masks if later != tp_count]
    early = first_stage(first_masks, tp_count, stripe, block_rows, factor)
    late = second_stage(second_masks, tp_count, stripe, block_rows, factor)
    known = early(*first_parts, hamiltonian, interaction)
    return late(*second_parts, hamiltonian, interaction, *known)[:, :, None]


def solution(mesh):
    in_specs = (P(None, None, "tp", None, "ta"), P(), P())
    out_specs = P(None, None, "tp", None, "ta")
    ta_count = mesh.shape["ta"]
    tp_count = mesh.shape["tp"]

    def shards(green, hamiltonian, interaction):
        whole_bytes = green.size * green.dtype.itemsize * ta_count * tp_count
        covered = ta_count == 2 and green.shape[1] == 2 and tp_count >= 16
        if covered and tp_count & (tp_count - 1) == 0 and whole_bytes <= 1 << 22:
            return replicated(green, hamiltonian, interaction)
        return windowed(green, hamiltonian, interaction)

    return jax.shard_map(shards, mesh=mesh, in_specs=in_specs, out_specs=out_specs, check_vma=False)
```

```python
import math

import jax
import jax.numpy as jnp
from jax import lax
from jax.experimental import pallas as pl
from jax.experimental.pallas import tpu as pltpu
from jax.sharding import PartitionSpec as P

NO = 32
ITERS = 2


highest = lax.Precision.HIGHEST


def shifted(block, axis, distance):
    devices = range(lax.axis_size(axis))
    route = [(i - distance, i) for i in devices if i - distance in devices]
    return lax.ppermute(block, axis, route)


def half_dot(left_side, right_side):
    return jnp.dot(left_side, right_side, preferred_element_type=jnp.float32)


def accumulate(left_side, right_side):
    product_real = half_dot(left_side[0], right_side[0]) - half_dot(left_side[1], right_side[1])
    product_imag = half_dot(left_side[0], right_side[1]) + half_dot(left_side[1], right_side[0])
    return (product_real, product_imag)


def self_energy(values, mirror_part, weights):
    real_square = values[0] * values[0] - values[1] * values[1]
    imag_square = 2.0 * values[0] * values[1]
    sigma_real = weights * (real_square * mirror_part[0] - imag_square * mirror_part[1])
    sigma_imag = weights * (real_square * mirror_part[1] + imag_square * mirror_part[0])
    return jnp.stack([sigma_real, sigma_imag])


def windowed(green, hamiltonian, interaction):
    tp_count = lax.axis_size("tp")
    ta_place = lax.axis_index("ta")
    tp_place = lax.axis_index("tp")
    groups = green.shape[1]
    stripe = green.shape[3]
    block_rows = green.shape[4]
    columns = groups * stripe
    factor = 1.0 / math.sqrt(2 * block_rows)
    current = green[:, :, 0].reshape(2, columns, block_rows)
    squared = interaction * interaction
    column_global = (
        jnp.arange(groups, dtype=jnp.int32)[:, None] * tp_count + tp_place
    ) * stripe + jnp.arange(stripe, dtype=jnp.int32)[None, :]
    column_orbital = (column_global % NO).reshape(columns)
    onehot = (column_orbital[:, None] == jnp.arange(NO, dtype=jnp.int32)[None, :]).astype(
        jnp.float32
    )
    lookup_table = jnp.dot(onehot, squared.T, precision=highest)
    coupling = jnp.tile(lookup_table, (1, block_rows // NO))
    row_time = jnp.arange(block_rows, dtype=jnp.int32) // NO
    column_time = (tp_place * stripe + jnp.arange(stripe, dtype=jnp.int32)) // NO
    is_later = column_time[:, None] > row_time[None, :]
    block_width = math.gcd(block_rows, 128)
    blocked = jnp.kron(jnp.eye(block_width // NO, dtype=jnp.float32), hamiltonian.T)
    zero_half = jnp.zeros((), jnp.bfloat16)
    for iteration in range(ITERS):
        rounded = current.astype(jnp.bfloat16)
        outgoing = rounded.reshape(2, groups, stripe, tp_count, stripe)
        previous = shifted(rounded, "ta", 1)
        earliest = shifted(rounded, "ta", 2)
        hamilton_term = jnp.dot(
            current.reshape(-1, block_width), blocked, precision=highest
        ).reshape(2, columns, block_rows)
        selected = []
        nearby = jnp.stack(
            [
                lax.dynamic_index_in_dim(
                    outgoing, jnp.minimum(ta_place + step_ahead, groups - 1), 1, keepdims=False
                )
                for step_ahead in range(3)
            ],
            1,
        )
        spread = lax.all_to_all(nearby, "tp", split_axis=3, concat_axis=3, tiled=True)
        from_one = shifted(spread[:, 1], "ta", 1)
        from_two = shifted(spread[:, 2], "ta", 2)
        received = (from_two, from_one, spread[:, 0])
        by_current = current.reshape(2, groups, stripe, block_rows)
        for window_index in range(3):
            group_pick = jnp.maximum(ta_place - 2 + window_index, 0)
            own_part = lax.dynamic_index_in_dim(by_current, group_pick, 1, keepdims=False)
            flipped = (
                jnp.transpose(received[window_index], (0, 3, 2, 1))
                .reshape(2, stripe, block_rows)
                .astype(jnp.float32)
            )
            selected.append(self_energy(own_part, flipped, coupling[:stripe]))
        oldest = jnp.where(is_later[None], selected[0], 0.0)
        middle = selected[1]
        newest = jnp.where(is_later[None], 0.0, selected[2])
        sending = jnp.stack([oldest + newest, middle], 1).astype(jnp.bfloat16)[:, :, None]
        portion = lax.all_gather(sending, "tp", axis=2, tiled=True)
        row_count = portion.shape[2] * stripe
        arriving_time = jnp.arange(row_count, dtype=jnp.int32) // NO
        later_here = (arriving_time[:, None] > row_time[None, :])[None]
        merged = portion[:, 0].reshape(2, row_count, block_rows)
        recent = portion[:, 1].reshape(2, row_count, block_rows)
        right_side = jnp.concatenate(
            [
                jnp.where(later_here, merged, zero_half),
                recent,
                jnp.where(later_here, zero_half, merged),
            ],
            1,
        )
        memory = accumulate(
            jnp.concatenate([source for source in (earliest, previous, rounded)], 2), right_side
        )
        next_real = current[0] + 0.5 * (hamilton_term[1] + factor * memory[1])
        next_imag = current[1] - 0.5 * (hamilton_term[0] + factor * memory[0])
        current = jnp.stack([next_real, next_imag])
    return current.reshape(2, groups, 1, stripe, block_rows)


def exchange_masks(tp_count):
    bits = [1 << bit for bit in reversed(range(1, tp_count.bit_length() - 1))]
    top, middle = bits[:1], bits[1:-1]
    return bits[-1], top + [tp_count] + middle, middle + top + [tp_count]


def offsets_of(masks):
    offsets = [0]
    for mask in masks:
        offsets = offsets + [known ^ mask for known in offsets]
    return offsets


def bf16_dot(left_side, right_side):
    return lax.dot_general(
        left_side, right_side, (((1,), (0,)), ((), ())), preferred_element_type=jnp.float32
    )


def halves(values):
    high = values.astype(jnp.bfloat16)
    return high, (values - high.astype(jnp.float32)).astype(jnp.bfloat16)


def window_of(values, mirror, weights, first_time):
    rows, width = values[0].shape
    real_square = values[0] * values[0] - values[1] * values[1]
    imag_square = 2.0 * values[0] * values[1]
    real = real_square * mirror[0] - imag_square * mirror[1]
    imag = real_square * mirror[1] + imag_square * mirror[0]
    source_time = lax.broadcasted_iota(jnp.int32, (rows, width), 0) // NO
    target_time = lax.broadcasted_iota(jnp.int32, (rows, width), 1) // NO + first_time
    inside = source_time <= target_time

    def weighted(part):
        part = (part.reshape(rows // NO, NO, width) * weights[None]).reshape(rows, width)
        return jnp.where(inside, part, 0.0).astype(jnp.bfloat16)

    return weighted(real), weighted(imag)


def mirrored(rounded):
    return [jnp.transpose(part.astype(jnp.float32)) for part in rounded]


def products(left_side, right_side):
    real = bf16_dot(left_side[0], right_side[0]) - bf16_dot(left_side[1], right_side[1])
    imag = bf16_dot(left_side[0], right_side[1]) + bf16_dot(left_side[1], right_side[0])
    return real, imag


def tables_of(hamiltonian, interaction, block_rows):
    def repeated(tile):
        return jnp.concatenate([tile] * (block_rows // NO), axis=1)

    weights = repeated(jnp.transpose(interaction[...] * interaction[...]))
    table = jnp.concatenate([repeated(jnp.transpose(hamiltonian[...]))] * (block_rows // NO))
    same_time = (
        lax.broadcasted_iota(jnp.int32, table.shape, 0) // NO
        == lax.broadcasted_iota(jnp.int32, table.shape, 1) // NO
    )
    return weights, halves(jnp.where(same_time, table, 0.0))


def one_body(values, high, low, table):
    turned = [
        bf16_dot(high[part], table[0])
        + bf16_dot(low[part], table[0])
        + bf16_dot(high[part], table[1])
        for part in range(2)
    ]
    return values[0] + 0.5 * turned[1], values[1] - 0.5 * turned[0]


def whole(source, block, tp_count, block_rows):
    return [
        source[part, block * tp_count : (block + 1) * tp_count].reshape(block_rows, block_rows)
        for part in range(2)
    ]


def second_group(masks, tp_count, stripe, block_rows, factor):
    offsets = offsets_of(masks)
    scale = 0.5 * factor

    def kernel(*refs):
        sources, hamiltonian, interaction = refs[:4], refs[4], refs[5]
        highs, bases, window, mirror, rests = refs[6:]
        me = lax.axis_index("ta") * tp_count + lax.axis_index("tp")
        blank = jnp.zeros((stripe, block_rows), jnp.bfloat16)
        for flip in range(2):
            both, opposite = sources[2 * flip], sources[2 * flip + 1]
            for index, mask in enumerate(offsets):
                device = me ^ (flip ^ mask)
                other = device ^ tp_count
                for part in range(2):
                    highs[part, device] = both[0, index, part]
                    rests[part, device] = both[1, index, part]
                    highs[part, other] = opposite[index, part]
                    rests[part, other] = blank
        weights, table = tables_of(hamiltonian, interaction, block_rows)
        for block in range(2):
            high = whole(highs, block, tp_count, block_rows)
            rest = whole(rests, block, tp_count, block_rows)
            full = [high[k].astype(jnp.float32) + rest[k].astype(jnp.float32) for k in range(2)]
            base = one_body(full, high, rest, table)
            turned = mirrored(high)
            if block == 0:
                mirror[0] = turned[0]
                mirror[1] = turned[1]
            else:
                made = window_of(full, turned, weights, 0)
                memory = products(high, made)
                base = (base[0] + scale * memory[1], base[1] - scale * memory[0])
                window[0] = made[0]
                window[1] = made[1]
            bases[0, block] = base[0]
            bases[1, block] = base[1]

    square = (2, block_rows, block_rows)
    pieces = (2, 2 * tp_count, stripe, block_rows)
    return pl.pallas_call(
        kernel,
        out_shape=[
            jax.ShapeDtypeStruct(pieces, jnp.bfloat16),
            jax.ShapeDtypeStruct((2,) + square, jnp.float32),
            jax.ShapeDtypeStruct(square, jnp.bfloat16),
            jax.ShapeDtypeStruct(square, jnp.float32),
        ],
        in_specs=[pl.BlockSpec(memory_space=pltpu.VMEM)] * 6,
        out_specs=[pl.BlockSpec(memory_space=pltpu.VMEM)] * 4,
        scratch_shapes=[pltpu.VMEM(pieces, jnp.bfloat16)],
        compiler_params=pltpu.CompilerParams(vmem_limit_bytes=16 << 20),
        name="second_group",
    )


def both_groups(masks, tp_count, stripe, block_rows, factor):
    offsets = offsets_of(masks)
    half_count = len(offsets) // 2
    order_size = 2 * block_rows
    scale = 0.5 * factor

    def kernel(*refs):
        sources, hamiltonian, interaction = refs[:4], refs[4], refs[5]
        highs, bases, window, mirror, out, values, nexts, low_next = refs[6:]
        ta_place = lax.axis_index("ta")
        tp_place = lax.axis_index("tp")
        me = ta_place * tp_count + tp_place
        for flip in range(2):
            for index, mask in enumerate(offsets):
                late, slot = divmod(index, half_count)
                device = me ^ (flip ^ mask)
                for part in range(2):
                    values[part, device] = sources[2 * flip + late][slot, part]
        weights, table = tables_of(hamiltonian, interaction, block_rows)

        def stored(block, group, real, imag):
            for part, result in ((0, real), (1, imag)):
                nexts[part, block, group] = result
                low_next[part, group, :, block * block_rows : (block + 1) * block_rows] = (
                    result.astype(jnp.bfloat16)
                )

        second_high = whole(highs, 0, tp_count, block_rows)
        current = [whole(values, block, tp_count, block_rows) for block in range(2)]
        split = [[halves(part) for part in current[block]] for block in range(2)]
        high = [[part[0] for part in split[block]] for block in range(2)]
        base = [
            one_body(current[block], high[block], [part[1] for part in split[block]], table)
            for block in range(2)
        ]
        early = window_of(current[0], mirrored(high[0]), weights, 0)
        for group, rows in ((0, high[0]), (1, second_high)):
            start = base[0] if group == 0 else (bases[0, 0], bases[1, 0])
            memory = products(rows, early)
            stored(0, group, start[0] + scale * memory[1], start[1] - scale * memory[0])
        cross = window_of(
            current[1], [mirror[0], mirror[1]], weights, block_rows // NO
        )
        memory = products(second_high, cross)
        stored(1, 1, bases[0, 1] + scale * memory[1], bases[1, 1] - scale * memory[0])
        memory = products(high[0], cross)
        late = products(high[1], [window[0], window[1]])
        real = memory[0] + late[0]
        imag = memory[1] + late[1]
        stored(1, 0, base[1][0] + scale * imag, base[1][1] - scale * real)

        present = [nexts[part, ta_place].reshape(order_size, block_rows) for part in range(2)]
        turned = mirrored([low_next[part, ta_place] for part in range(2)])
        last = window_of(present, turned, weights, ta_place * (block_rows // NO))
        row = pl.multiple_of(tp_place * stripe, stripe)
        own = [
            nexts[part, ta_place, :, pl.ds(row, stripe), :].reshape(2 * stripe, block_rows)
            for part in range(2)
        ]
        own_rounded = [
            low_next[part, :, pl.ds(row, stripe), :].reshape(2 * stripe, order_size)
            for part in range(2)
        ]
        memory = products(own_rounded, last)
        split = [halves(part) for part in own]
        real, imag = one_body(own, [part[0] for part in split], [part[1] for part in split], table)
        shape = (2, stripe, block_rows)
        out[0] = (real + scale * memory[1]).reshape(shape)
        out[1] = (imag - scale * memory[0]).reshape(shape)

    square = (2, 2, block_rows, block_rows)
    return pl.pallas_call(
        kernel,
        out_shape=jax.ShapeDtypeStruct((2, 2, stripe, block_rows), jnp.float32),
        in_specs=[pl.BlockSpec(memory_space=pltpu.VMEM)] * 10,
        out_specs=pl.BlockSpec(memory_space=pltpu.VMEM),
        scratch_shapes=[
            pltpu.VMEM((2, 2 * tp_count, stripe, block_rows), jnp.float32),
            pltpu.VMEM((2,) + square, jnp.float32),
            pltpu.VMEM((2, 2, block_rows, order_size), jnp.bfloat16),
        ],
        compiler_params=pltpu.CompilerParams(vmem_limit_bytes=24 << 20),
        name="both_groups",
    )


def replicated(green, hamiltonian, interaction):
    tp_count = lax.axis_size("tp")
    count = 2 * tp_count
    stripe = green.shape[3]
    block_rows = green.shape[4]
    factor = 1.0 / math.sqrt(2 * block_rows)
    mask, first_masks, second_masks = exchange_masks(tp_count)

    def exchanged(block, mask):
        return lax.ppermute(block, ("ta", "tp"), [(i, i ^ mask) for i in range(count)])

    arriving = exchanged(green.reshape(-1, block_rows), mask).reshape(green.shape)
    first = jnp.stack([green[:, 0, 0], arriving[:, 0, 0]])
    second = jnp.stack([green[:, 1, 0], arriving[:, 1, 0]])
    high = lax.reduce_precision(second, 8, 7)
    second = jnp.stack([high, second - high]).astype(jnp.bfloat16)
    first_parts = second_parts = ()
    for first_mask, second_mask in zip(first_masks, second_masks):
        first_parts = [first, exchanged(first, first_mask)]
        first = jnp.concatenate(first_parts)
        if second_mask == tp_count:
            second_parts = [second, exchanged(second[0], second_mask)]
        else:
            second = jnp.concatenate([second, exchanged(second, second_mask)], 1)
    first_parts += [exchanged(part, 1) for part in first_parts]
    second_parts += [exchanged(part, 1) for part in second_parts]
    sizes = (tp_count, stripe, block_rows, factor)
    known = second_group([mask] + second_masks[:-1], *sizes)(
        *second_parts, hamiltonian, interaction
    )
    result = both_groups([mask] + first_masks, *sizes)(
        *first_parts, hamiltonian, interaction, *known
    )
    return result[:, :, None]


def solution(mesh):
    in_specs = (P(None, None, "tp", None, "ta"), P(), P())
    out_specs = P(None, None, "tp", None, "ta")
    ta_count = mesh.shape["ta"]
    tp_count = mesh.shape["tp"]

    def shards(green, hamiltonian, interaction):
        whole_bytes = green.size * green.dtype.itemsize * ta_count * tp_count
        covered = ta_count == 2 and green.shape[1] == 2 and tp_count >= 16
        if covered and tp_count & (tp_count - 1) == 0 and whole_bytes <= 1 << 22:
            return replicated(green, hamiltonian, interaction)
        return windowed(green, hamiltonian, interaction)

    return jax.shard_map(shards, mesh=mesh, in_specs=in_specs, out_specs=out_specs, check_vma=False)
```

```python
import math

import jax
import jax.numpy as jnp
from jax import lax
from jax.experimental import pallas as pl
from jax.experimental.pallas import tpu as pltpu
from jax.sharding import PartitionSpec as P

NO = 32
ITERS = 2


highest = lax.Precision.HIGHEST


def shifted(block, axis, distance):
    devices = range(lax.axis_size(axis))
    route = [(i - distance, i) for i in devices if i - distance in devices]
    return lax.ppermute(block, axis, route)


def half_dot(left_side, right_side):
    return jnp.dot(left_side, right_side, preferred_element_type=jnp.float32)


def accumulate(left_side, right_side):
    product_real = half_dot(left_side[0], right_side[0]) - half_dot(left_side[1], right_side[1])
    product_imag = half_dot(left_side[0], right_side[1]) + half_dot(left_side[1], right_side[0])
    return (product_real, product_imag)


def self_energy(values, mirror_part, weights):
    real_square = values[0] * values[0] - values[1] * values[1]
    imag_square = 2.0 * values[0] * values[1]
    sigma_real = weights * (real_square * mirror_part[0] - imag_square * mirror_part[1])
    sigma_imag = weights * (real_square * mirror_part[1] + imag_square * mirror_part[0])
    return jnp.stack([sigma_real, sigma_imag])


def windowed(green, hamiltonian, interaction):
    tp_count = lax.axis_size("tp")
    ta_place = lax.axis_index("ta")
    tp_place = lax.axis_index("tp")
    groups = green.shape[1]
    stripe = green.shape[3]
    block_rows = green.shape[4]
    columns = groups * stripe
    factor = 1.0 / math.sqrt(2 * block_rows)
    current = green[:, :, 0].reshape(2, columns, block_rows)
    squared = interaction * interaction
    column_global = (
        jnp.arange(groups, dtype=jnp.int32)[:, None] * tp_count + tp_place
    ) * stripe + jnp.arange(stripe, dtype=jnp.int32)[None, :]
    column_orbital = (column_global % NO).reshape(columns)
    onehot = (column_orbital[:, None] == jnp.arange(NO, dtype=jnp.int32)[None, :]).astype(
        jnp.float32
    )
    lookup_table = jnp.dot(onehot, squared.T, precision=highest)
    coupling = jnp.tile(lookup_table, (1, block_rows // NO))
    row_time = jnp.arange(block_rows, dtype=jnp.int32) // NO
    column_time = (tp_place * stripe + jnp.arange(stripe, dtype=jnp.int32)) // NO
    is_later = column_time[:, None] > row_time[None, :]
    block_width = math.gcd(block_rows, 128)
    blocked = jnp.kron(jnp.eye(block_width // NO, dtype=jnp.float32), hamiltonian.T)
    zero_half = jnp.zeros((), jnp.bfloat16)
    for iteration in range(ITERS):
        rounded = current.astype(jnp.bfloat16)
        outgoing = rounded.reshape(2, groups, stripe, tp_count, stripe)
        previous = shifted(rounded, "ta", 1)
        earliest = shifted(rounded, "ta", 2)
        hamilton_term = jnp.dot(
            current.reshape(-1, block_width), blocked, precision=highest
        ).reshape(2, columns, block_rows)
        selected = []
        nearby = jnp.stack(
            [
                lax.dynamic_index_in_dim(
                    outgoing, jnp.minimum(ta_place + step_ahead, groups - 1), 1, keepdims=False
                )
                for step_ahead in range(3)
            ],
            1,
        )
        spread = lax.all_to_all(nearby, "tp", split_axis=3, concat_axis=3, tiled=True)
        from_one = shifted(spread[:, 1], "ta", 1)
        from_two = shifted(spread[:, 2], "ta", 2)
        received = (from_two, from_one, spread[:, 0])
        by_current = current.reshape(2, groups, stripe, block_rows)
        for window_index in range(3):
            group_pick = jnp.maximum(ta_place - 2 + window_index, 0)
            own_part = lax.dynamic_index_in_dim(by_current, group_pick, 1, keepdims=False)
            flipped = (
                jnp.transpose(received[window_index], (0, 3, 2, 1))
                .reshape(2, stripe, block_rows)
                .astype(jnp.float32)
            )
            selected.append(self_energy(own_part, flipped, coupling[:stripe]))
        oldest = jnp.where(is_later[None], selected[0], 0.0)
        middle = selected[1]
        newest = jnp.where(is_later[None], 0.0, selected[2])
        sending = jnp.stack([oldest + newest, middle], 1).astype(jnp.bfloat16)[:, :, None]
        portion = lax.all_gather(sending, "tp", axis=2, tiled=True)
        row_count = portion.shape[2] * stripe
        arriving_time = jnp.arange(row_count, dtype=jnp.int32) // NO
        later_here = (arriving_time[:, None] > row_time[None, :])[None]
        merged = portion[:, 0].reshape(2, row_count, block_rows)
        recent = portion[:, 1].reshape(2, row_count, block_rows)
        right_side = jnp.concatenate(
            [
                jnp.where(later_here, merged, zero_half),
                recent,
                jnp.where(later_here, zero_half, merged),
            ],
            1,
        )
        memory = accumulate(
            jnp.concatenate([source for source in (earliest, previous, rounded)], 2), right_side
        )
        next_real = current[0] + 0.5 * (hamilton_term[1] + factor * memory[1])
        next_imag = current[1] - 0.5 * (hamilton_term[0] + factor * memory[0])
        current = jnp.stack([next_real, next_imag])
    return current.reshape(2, groups, 1, stripe, block_rows)


def exchange_masks(tp_count):
    bits = [1 << bit for bit in reversed(range(1, tp_count.bit_length() - 1))]
    middle, low, ta_bit = bits[1:-1], bits[-1:], [tp_count]
    even, odd = ta_bit + middle + low, low + middle + ta_bit
    return bits[0], (even, odd), ta_bit + low + middle


def offsets_of(masks):
    offsets = [0]
    for mask in masks:
        offsets = offsets + [known ^ mask for known in offsets]
    return offsets


def bf16_dot(left_side, right_side):
    return lax.dot_general(
        left_side, right_side, (((1,), (0,)), ((), ())), preferred_element_type=jnp.float32
    )


def halves(values):
    high = values.astype(jnp.bfloat16)
    return high, (values - high.astype(jnp.float32)).astype(jnp.bfloat16)


def window_of(values, mirror, weights, first_time):
    rows, width = values[0].shape
    real_square = values[0] * values[0] - values[1] * values[1]
    imag_square = 2.0 * values[0] * values[1]
    real = real_square * mirror[0] - imag_square * mirror[1]
    imag = real_square * mirror[1] + imag_square * mirror[0]
    source_time = lax.broadcasted_iota(jnp.int32, (rows, width), 0) // NO
    target_time = lax.broadcasted_iota(jnp.int32, (rows, width), 1) // NO + first_time
    inside = source_time <= target_time

    def weighted(part):
        part = (part.reshape(rows // NO, NO, width) * weights[None]).reshape(rows, width)
        return jnp.where(inside, part, 0.0).astype(jnp.bfloat16)

    return weighted(real), weighted(imag)


def mirrored(rounded):
    return [jnp.transpose(part.astype(jnp.float32)) for part in rounded]


def products(left_side, right_side):
    real = bf16_dot(left_side[0], right_side[0]) - bf16_dot(left_side[1], right_side[1])
    imag = bf16_dot(left_side[0], right_side[1]) + bf16_dot(left_side[1], right_side[0])
    return real, imag


def tables_of(hamiltonian, interaction, block_rows):
    def repeated(tile):
        return jnp.concatenate([tile] * (block_rows // NO), axis=1)

    weights = repeated(jnp.transpose(interaction[...] * interaction[...]))
    table = jnp.concatenate([repeated(jnp.transpose(hamiltonian[...]))] * (block_rows // NO))
    same_time = (
        lax.broadcasted_iota(jnp.int32, table.shape, 0) // NO
        == lax.broadcasted_iota(jnp.int32, table.shape, 1) // NO
    )
    return weights, halves(jnp.where(same_time, table, 0.0))


def one_body(values, high, low, table):
    turned = [
        bf16_dot(high[part], table[0])
        + bf16_dot(low[part], table[0])
        + bf16_dot(high[part], table[1])
        for part in range(2)
    ]
    return values[0] + 0.5 * turned[1], values[1] - 0.5 * turned[0]


def first_stage(masks, tp_count, stripe, block_rows, factor):
    offsets = [offsets_of(each) for each in masks]
    half_count = len(offsets[0]) // 2

    def kernel(*refs):
        sources = refs[:4]
        hamiltonian, interaction, values, lows, bases, window = refs[4:]
        me = lax.axis_index("ta") * tp_count + lax.axis_index("tp")
        for flip in range(2):
            for index in range(2 * half_count):
                late, slot = divmod(index, half_count)
                mask = jnp.where(me % 2 == flip, offsets[0][index], offsets[1][index])
                device = me ^ (flip ^ mask)
                for part in range(2):
                    values[part, device] = sources[2 * flip + late][slot, part]
        weights, table = tables_of(hamiltonian, interaction, block_rows)
        for block in range(2):
            current = [
                values[part, block * tp_count : (block + 1) * tp_count].reshape(
                    block_rows, block_rows
                )
                for part in range(2)
            ]
            split = [halves(part) for part in current]
            high = [part[0] for part in split]
            base = one_body(current, high, [part[1] for part in split], table)
            for part in range(2):
                lows[part, :, block * block_rows : (block + 1) * block_rows] = high[part]
            if block == 0:
                made = window_of(current, mirrored(high), weights, 0)
                memory = products(high, made)
                scale = 0.5 * factor
                base = (base[0] + scale * memory[1], base[1] - scale * memory[0])
                window[0] = made[0]
                window[1] = made[1]
            bases[0, block] = base[0]
            bases[1, block] = base[1]

    block = jax.ShapeDtypeStruct((2, 2, block_rows, block_rows), jnp.float32)
    return pl.pallas_call(
        kernel,
        out_shape=[
            jax.ShapeDtypeStruct((2, 2 * tp_count, stripe, block_rows), jnp.float32),
            jax.ShapeDtypeStruct((2, block_rows, 2 * block_rows), jnp.bfloat16),
            block,
            jax.ShapeDtypeStruct((2, block_rows, block_rows), jnp.bfloat16),
        ],
        in_specs=[pl.BlockSpec(memory_space=pltpu.VMEM)] * 6,
        out_specs=[pl.BlockSpec(memory_space=pltpu.VMEM)] * 4,
        compiler_params=pltpu.CompilerParams(vmem_limit_bytes=16 << 20),
        name="first_stage",
    )


def second_stage(masks, tp_count, stripe, block_rows, factor):
    offsets = offsets_of(masks)
    half_count = len(offsets) // 2
    order_size = 2 * block_rows
    scale = 0.5 * factor

    def kernel(*refs):
        sources = refs[:4]
        hamiltonian, interaction, values, lows, bases, window = refs[4:10]
        out, highs, rests, nexts, low_next = refs[10:]
        ta_place = lax.axis_index("ta")
        tp_place = lax.axis_index("tp")
        me = ta_place * tp_count + tp_place
        blank = jnp.zeros((stripe, block_rows), jnp.bfloat16)
        for flip in range(2):
            for index, mask in enumerate(offsets):
                late, slot = divmod(index, half_count)
                device = me ^ (flip ^ mask)
                other = device ^ tp_count
                source = sources[2 * flip + late]
                for part in range(2):
                    highs[part, device] = source[slot, 0, part]
                    highs[part, other] = source[slot, 1, part]
                    rests[part, device] = source[slot, 2, part]
                    rests[part, other] = blank
        weights, table = tables_of(hamiltonian, interaction, block_rows)

        def whole(source, block):
            return [
                source[part, block * tp_count : (block + 1) * tp_count].reshape(
                    block_rows, block_rows
                )
                for part in range(2)
            ]

        high = [whole(highs, block) for block in range(2)]
        rest = [whole(rests, block) for block in range(2)]
        full = [
            [
                high[block][part].astype(jnp.float32) + rest[block][part].astype(jnp.float32)
                for part in range(2)
            ]
            for block in range(2)
        ]
        base = [one_body(full[block], high[block], rest[block], table) for block in range(2)]

        def stored(block, group, real, imag):
            for part, result in ((0, real), (1, imag)):
                nexts[part, block, group] = result
                low_next[part, group, :, block * block_rows : (block + 1) * block_rows] = (
                    result.astype(jnp.bfloat16)
                )

        stored(0, 0, bases[0, 0], bases[1, 0])
        memory = products(high[0], (window[0], window[1]))
        stored(0, 1, base[0][0] + scale * memory[1], base[0][1] - scale * memory[0])
        later = [
            window_of(whole(values, 1), mirrored(high[0]), weights, block_rows // NO),
            window_of(full[1], mirrored(high[1]), weights, 0),
        ]
        rows = [[lows[part, :, :block_rows] for part in range(2)]]
        rows.append([lows[part, :, block_rows:] for part in range(2)])
        early_memory = [products(rows[0], later[0]), products(high[0], later[0])]
        late_memory = [products(rows[1], later[1]), products(high[1], later[1])]
        for group in range(2):
            start = (bases[0, 1], bases[1, 1]) if group == 0 else base[1]
            real = early_memory[group][0] + late_memory[group][0]
            imag = early_memory[group][1] + late_memory[group][1]
            stored(1, group, start[0] + scale * imag, start[1] - scale * real)

        current = [nexts[part, ta_place].reshape(order_size, block_rows) for part in range(2)]
        mirror = mirrored([low_next[part, ta_place] for part in range(2)])
        last = window_of(current, mirror, weights, ta_place * (block_rows // NO))
        row = pl.multiple_of(tp_place * stripe, stripe)
        own = [
            nexts[part, ta_place, :, pl.ds(row, stripe), :].reshape(2 * stripe, block_rows)
            for part in range(2)
        ]
        own_rounded = [
            low_next[part, :, pl.ds(row, stripe), :].reshape(2 * stripe, order_size)
            for part in range(2)
        ]
        memory = products(own_rounded, last)
        split = [halves(part) for part in own]
        real, imag = one_body(own, [part[0] for part in split], [part[1] for part in split], table)
        shape = (2, stripe, block_rows)
        out[0] = (real + scale * memory[1]).reshape(shape)
        out[1] = (imag - scale * memory[0]).reshape(shape)

    square = (2, 2, block_rows, block_rows)
    return pl.pallas_call(
        kernel,
        out_shape=jax.ShapeDtypeStruct((2, 2, stripe, block_rows), jnp.float32),
        in_specs=[pl.BlockSpec(memory_space=pltpu.VMEM)] * 10,
        out_specs=pl.BlockSpec(memory_space=pltpu.VMEM),
        scratch_shapes=[
            pltpu.VMEM((2, 2 * tp_count, stripe, block_rows), jnp.bfloat16),
            pltpu.VMEM((2, 2 * tp_count, stripe, block_rows), jnp.bfloat16),
            pltpu.VMEM((2,) + square, jnp.float32),
            pltpu.VMEM((2, 2, block_rows, order_size), jnp.bfloat16),
        ],
        compiler_params=pltpu.CompilerParams(vmem_limit_bytes=24 << 20),
        name="second_stage",
    )


def replicated(green, hamiltonian, interaction):
    tp_count = lax.axis_size("tp")
    count = 2 * tp_count
    stripe = green.shape[3]
    block_rows = green.shape[4]
    factor = 1.0 / math.sqrt(2 * block_rows)
    mask, first_masks, second_masks = exchange_masks(tp_count)

    def exchanged(block, mask):
        masks = (mask, mask) if isinstance(mask, int) else mask
        return lax.ppermute(block, ("ta", "tp"), [(i, i ^ masks[i % 2]) for i in range(count)])

    arriving = exchanged(green.reshape(-1, block_rows), mask).reshape(green.shape)
    first = jnp.stack([green[:, 0, 0], arriving[:, 0, 0]])
    second = jnp.stack([green[:, 1, 0], arriving[:, 1, 0]])
    high = lax.reduce_precision(second, 8, 7)
    second = jnp.stack([high, second - high], 1).astype(jnp.bfloat16)
    first_parts = second_parts = ()
    for first_mask, second_mask in zip(zip(*first_masks), second_masks):
        first_parts = [first, exchanged(first, first_mask)]
        first = jnp.concatenate(first_parts)
        if second_mask == tp_count:
            other_high = exchanged(second[:, 0], second_mask)[:, None]
            second = jnp.concatenate([second[:, :1], other_high, second[:, 1:]], 1)
        else:
            second_parts = [second, exchanged(second, second_mask)]
            second = jnp.concatenate(second_parts)
    first_parts += [exchanged(part, 1) for part in first_parts]
    second_parts += [exchanged(part, 1) for part in second_parts]
    first_masks = [[mask] + each for each in first_masks]
    second_masks = [mask] + [later for later in second_masks if later != tp_count]
    early = first_stage(first_masks, tp_count, stripe, block_rows, factor)
    late = second_stage(second_masks, tp_count, stripe, block_rows, factor)
    known = early(*first_parts, hamiltonian, interaction)
    return late(*second_parts, hamiltonian, interaction, *known)[:, :, None]


def solution(mesh):
    in_specs = (P(None, None, "tp", None, "ta"), P(), P())
    out_specs = P(None, None, "tp", None, "ta")
    ta_count = mesh.shape["ta"]
    tp_count = mesh.shape["tp"]

    def shards(green, hamiltonian, interaction):
        whole_bytes = green.size * green.dtype.itemsize * ta_count * tp_count
        covered = ta_count == 2 and green.shape[1] == 2 and tp_count >= 16
        if covered and tp_count & (tp_count - 1) == 0 and whole_bytes <= 1 << 22:
            return replicated(green, hamiltonian, interaction)
        return windowed(green, hamiltonian, interaction)

    return jax.shard_map(shards, mesh=mesh, in_specs=in_specs, out_specs=out_specs, check_vma=False)
```

```python
import math

import jax
import jax.numpy as jnp
from jax import lax
from jax.experimental import pallas as pl
from jax.experimental.pallas import tpu as pltpu
from jax.sharding import PartitionSpec as P

NO = 32
ITERS = 2


highest = lax.Precision.HIGHEST


def shifted(block, axis, distance):
    devices = range(lax.axis_size(axis))
    route = [(i - distance, i) for i in devices if i - distance in devices]
    return lax.ppermute(block, axis, route)


def half_dot(left_side, right_side):
    return jnp.dot(left_side, right_side, preferred_element_type=jnp.float32)


def accumulate(left_side, right_side):
    product_real = half_dot(left_side[0], right_side[0]) - half_dot(left_side[1], right_side[1])
    product_imag = half_dot(left_side[0], right_side[1]) + half_dot(left_side[1], right_side[0])
    return (product_real, product_imag)


def self_energy(values, mirror_part, weights):
    real_square = values[0] * values[0] - values[1] * values[1]
    imag_square = 2.0 * values[0] * values[1]
    sigma_real = weights * (real_square * mirror_part[0] - imag_square * mirror_part[1])
    sigma_imag = weights * (real_square * mirror_part[1] + imag_square * mirror_part[0])
    return jnp.stack([sigma_real, sigma_imag])


def windowed(green, hamiltonian, interaction):
    tp_count = lax.axis_size("tp")
    ta_place = lax.axis_index("ta")
    tp_place = lax.axis_index("tp")
    groups = green.shape[1]
    stripe = green.shape[3]
    block_rows = green.shape[4]
    columns = groups * stripe
    factor = 1.0 / math.sqrt(2 * block_rows)
    current = green[:, :, 0].reshape(2, columns, block_rows)
    squared = interaction * interaction
    column_global = (
        jnp.arange(groups, dtype=jnp.int32)[:, None] * tp_count + tp_place
    ) * stripe + jnp.arange(stripe, dtype=jnp.int32)[None, :]
    column_orbital = (column_global % NO).reshape(columns)
    onehot = (column_orbital[:, None] == jnp.arange(NO, dtype=jnp.int32)[None, :]).astype(
        jnp.float32
    )
    lookup_table = jnp.dot(onehot, squared.T, precision=highest)
    coupling = jnp.tile(lookup_table, (1, block_rows // NO))
    row_time = jnp.arange(block_rows, dtype=jnp.int32) // NO
    column_time = (tp_place * stripe + jnp.arange(stripe, dtype=jnp.int32)) // NO
    is_later = column_time[:, None] > row_time[None, :]
    block_width = math.gcd(block_rows, 128)
    blocked = jnp.kron(jnp.eye(block_width // NO, dtype=jnp.float32), hamiltonian.T)
    zero_half = jnp.zeros((), jnp.bfloat16)
    for _ in range(ITERS):
        rounded = current.astype(jnp.bfloat16)
        outgoing = rounded.reshape(2, groups, stripe, tp_count, stripe)
        previous = shifted(rounded, "ta", 1)
        earliest = shifted(rounded, "ta", 2)
        hamilton_term = jnp.dot(
            current.reshape(-1, block_width), blocked, precision=highest
        ).reshape(2, columns, block_rows)
        selected = []
        nearby = jnp.stack(
            [
                lax.dynamic_index_in_dim(
                    outgoing, jnp.minimum(ta_place + step_ahead, groups - 1), 1, keepdims=False
                )
                for step_ahead in range(3)
            ],
            1,
        )
        spread = lax.all_to_all(nearby, "tp", split_axis=3, concat_axis=3, tiled=True)
        from_one = shifted(spread[:, 1], "ta", 1)
        from_two = shifted(spread[:, 2], "ta", 2)
        received = (from_two, from_one, spread[:, 0])
        by_current = current.reshape(2, groups, stripe, block_rows)
        for window_index in range(3):
            group_pick = jnp.maximum(ta_place - 2 + window_index, 0)
            own_part = lax.dynamic_index_in_dim(by_current, group_pick, 1, keepdims=False)
            flipped = (
                jnp.transpose(received[window_index], (0, 3, 2, 1))
                .reshape(2, stripe, block_rows)
                .astype(jnp.float32)
            )
            selected.append(self_energy(own_part, flipped, coupling[:stripe]))
        oldest = jnp.where(is_later[None], selected[0], 0.0)
        middle = selected[1]
        newest = jnp.where(is_later[None], 0.0, selected[2])
        sending = jnp.stack([oldest + newest, middle], 1).astype(jnp.bfloat16)[:, :, None]
        portion = lax.all_gather(sending, "tp", axis=2, tiled=True)
        row_count = portion.shape[2] * stripe
        arriving_time = jnp.arange(row_count, dtype=jnp.int32) // NO
        later_here = (arriving_time[:, None] > row_time[None, :])[None]
        merged = portion[:, 0].reshape(2, row_count, block_rows)
        recent = portion[:, 1].reshape(2, row_count, block_rows)
        right_side = jnp.concatenate(
            [
                jnp.where(later_here, merged, zero_half),
                recent,
                jnp.where(later_here, zero_half, merged),
            ],
            1,
        )
        memory = accumulate(
            jnp.concatenate([source for source in (earliest, previous, rounded)], 2), right_side
        )
        next_real = current[0] + 0.5 * (hamilton_term[1] + factor * memory[1])
        next_imag = current[1] - 0.5 * (hamilton_term[0] + factor * memory[0])
        current = jnp.stack([next_real, next_imag])
    return current.reshape(2, groups, 1, stripe, block_rows)


def exchange_masks(tp_count):
    bits = [1 << bit for bit in reversed(range(1, tp_count.bit_length() - 1))]
    middle, low, ta_bit = bits[1:-1], bits[-1:], [tp_count]
    even, odd = ta_bit + middle + low, low + middle + ta_bit
    return bits[0], (even, odd), ta_bit + low + middle


def offsets_of(masks):
    offsets = [0]
    for mask in masks:
        offsets = offsets + [known ^ mask for known in offsets]
    return offsets


def bf16_dot(left_side, right_side):
    return lax.dot_general(
        left_side, right_side, (((1,), (0,)), ((), ())), preferred_element_type=jnp.float32
    )


def halves(values):
    high = values.astype(jnp.bfloat16)
    return high, (values - high.astype(jnp.float32)).astype(jnp.bfloat16)


def window_of(values, mirror, weights, first_time):
    rows, width = values[0].shape
    real_square = values[0] * values[0] - values[1] * values[1]
    imag_square = 2.0 * values[0] * values[1]
    real = real_square * mirror[0] - imag_square * mirror[1]
    imag = real_square * mirror[1] + imag_square * mirror[0]
    source_time = lax.broadcasted_iota(jnp.int32, (rows, width), 0) // NO
    target_time = lax.broadcasted_iota(jnp.int32, (rows, width), 1) // NO + first_time
    inside = source_time <= target_time

    def weighted(part):
        part = (part.reshape(rows // NO, NO, width) * weights[None]).reshape(rows, width)
        return jnp.where(inside, part, 0.0).astype(jnp.bfloat16)

    return weighted(real), weighted(imag)


def mirrored(rounded):
    return [jnp.transpose(part.astype(jnp.float32)) for part in rounded]


def products(left_side, right_side):
    real = bf16_dot(left_side[0], right_side[0]) - bf16_dot(left_side[1], right_side[1])
    imag = bf16_dot(left_side[0], right_side[1]) + bf16_dot(left_side[1], right_side[0])
    return real, imag


def tables_of(hamiltonian, interaction, block_rows):
    def repeated(tile):
        return jnp.concatenate([tile] * (block_rows // NO), axis=1)

    weights = repeated(jnp.transpose(interaction[...] * interaction[...]))
    table = jnp.concatenate([repeated(jnp.transpose(hamiltonian[...]))] * (block_rows // NO))
    same_time = (
        lax.broadcasted_iota(jnp.int32, table.shape, 0) // NO
        == lax.broadcasted_iota(jnp.int32, table.shape, 1) // NO
    )
    return weights, halves(jnp.where(same_time, table, 0.0))


def turned_by(table, high, low=None):
    result = bf16_dot(high, table[0]) + bf16_dot(high, table[1])
    return result if low is None else result + bf16_dot(low, table[0])


def started(values, turned):
    return values[0] + 0.5 * turned[1], values[1] - 0.5 * turned[0]


def rows_of(pieces):
    return pieces.reshape(pieces.shape[0] * pieces.shape[1], pieces.shape[2])


def whole(source, block):
    tp_count, stripe, block_rows = source.shape[1] // 2, source.shape[2], source.shape[3]
    return [
        source[part, block * tp_count : (block + 1) * tp_count].reshape(
            tp_count * stripe, block_rows
        )
        for part in range(2)
    ]


def put(device, targets, results, index, stripe):
    for target, result in zip(targets, results):
        for part in range(2):
            target[part, device] = result[part][index * stripe : (index + 1) * stripe]


def take_first(sources, late, me, offsets, stripe, table, targets):
    count = len(offsets[0]) // 2
    for flip in range(2):
        values = [rows_of(sources[flip][:, part]) for part in range(2)]
        split = [halves(part) for part in values]
        base = started(values, [turned_by(table, high, low) for high, low in split])
        highs = [high for high, _ in split]
        for index in range(count):
            place = late * count + index
            mask = jnp.where(me % 2 == flip, offsets[0][place], offsets[1][place])
            put(me ^ (flip ^ mask), targets, (values, highs, base), index, stripe)


def take_second(sources, late, me, offsets, tp_count, stripe, table, targets):
    count = len(offsets) // 2
    for flip in range(2):
        for plane in range(2):
            highs = [rows_of(sources[flip][:, plane, part]) for part in range(2)]
            values = [high.astype(jnp.float32) for high in highs]
            if plane == 0:
                lows = [rows_of(sources[flip][:, 2, part]) for part in range(2)]
                values = [values[part] + lows[part].astype(jnp.float32) for part in range(2)]
                turned = [turned_by(table, highs[part], lows[part]) for part in range(2)]
            else:
                turned = [turned_by(table, high) for high in highs]
            base = started(values, turned)
            for index in range(count):
                device = me ^ (flip ^ offsets[late * count + index] ^ (plane * tp_count))
                put(device, targets, (values, highs, base), index, stripe)


def own_place(tp_count):
    return lax.axis_index("ta") * tp_count + lax.axis_index("tp")


def kept_shapes(tp_count, stripe, block_rows):
    pieces = (2, 2 * tp_count, stripe, block_rows)
    return [jax.ShapeDtypeStruct(pieces, each) for each in (jnp.float32, jnp.bfloat16, jnp.float32)]


def in_vmem(count):
    return [pl.BlockSpec(memory_space=pltpu.VMEM)] * count


def early_stage(first_masks, second_masks, tp_count, stripe, block_rows, factor):
    first_offsets = [offsets_of(each) for each in first_masks]
    second_offsets = offsets_of(second_masks)

    def kernel(*refs):
        hamiltonian, interaction, weights_out, table_out = refs[4:6] + refs[12:]
        me = own_place(tp_count)
        weights, table = tables_of(hamiltonian, interaction, block_rows)
        weights_out[...] = weights
        table_out[0] = table[0]
        table_out[1] = table[1]
        take_first(refs[:2], 0, me, first_offsets, stripe, table, refs[6:9])
        take_second(refs[2:4], 0, me, second_offsets, tp_count, stripe, table, refs[9:12])

    shapes = kept_shapes(tp_count, stripe, block_rows)
    tables = [
        jax.ShapeDtypeStruct((NO, block_rows), jnp.float32),
        jax.ShapeDtypeStruct((2, block_rows, block_rows), jnp.bfloat16),
    ]
    return pl.pallas_call(
        kernel,
        out_shape=shapes + shapes + tables,
        in_specs=in_vmem(6),
        out_specs=in_vmem(8),
        compiler_params=pltpu.CompilerParams(vmem_limit_bytes=16 << 20),
        name="early_stage",
    )


def first_stage(masks, tp_count, stripe, block_rows, factor):
    offsets = [offsets_of(each) for each in masks]
    scale = 0.5 * factor

    def kernel(*refs):
        weights, table = refs[2], (refs[3][0], refs[3][1])
        targets, window = refs[7:10], refs[10]
        take_first(refs[:2], 1, own_place(tp_count), offsets, stripe, table, targets)
        values, highs, bases = targets
        high = whole(highs, 0)
        made = window_of(whole(values, 0), mirrored(high), weights[...], 0)
        memory = products(high, made)
        window[0] = made[0]
        window[1] = made[1]
        half = (tp_count, stripe, block_rows)
        bases[0, :tp_count] = bases[0, :tp_count] + scale * memory[1].reshape(half)
        bases[1, :tp_count] = bases[1, :tp_count] - scale * memory[0].reshape(half)

    square = jax.ShapeDtypeStruct((2, block_rows, block_rows), jnp.bfloat16)
    return pl.pallas_call(
        kernel,
        out_shape=kept_shapes(tp_count, stripe, block_rows) + [square],
        in_specs=in_vmem(7),
        out_specs=in_vmem(4),
        input_output_aliases={4: 0, 5: 1, 6: 2},
        compiler_params=pltpu.CompilerParams(vmem_limit_bytes=16 << 20),
        name="first_stage",
    )


def second_stage(masks, tp_count, stripe, block_rows, factor):
    offsets = offsets_of(masks)
    order_size = 2 * block_rows
    scale = 0.5 * factor

    def kernel(*refs):
        weights, table = refs[2][...], (refs[3][0], refs[3][1])
        values, lows, bases, window = refs[4:8]
        out, targets, nexts, low_next = refs[11], refs[12:15], refs[15], refs[16]
        ta_place = lax.axis_index("ta")
        tp_place = lax.axis_index("tp")
        take_second(
            refs[:2], 1, own_place(tp_count), offsets, tp_count, stripe, table, targets
        )
        second_values, second_highs, second_bases = targets
        high = [whole(second_highs, block) for block in range(2)]

        def stored(block, group, real, imag):
            for part, result in ((0, real), (1, imag)):
                nexts[part, block, group] = result
                low_next[part, group, :, block * block_rows : (block + 1) * block_rows] = (
                    result.astype(jnp.bfloat16)
                )

        stored(0, 0, *whole(bases, 0))
        memory = products(high[0], (window[0], window[1]))
        base = whole(second_bases, 0)
        stored(0, 1, base[0] + scale * memory[1], base[1] - scale * memory[0])
        later = [
            window_of(whole(values, 1), mirrored(high[0]), weights, block_rows // NO),
            window_of(whole(second_values, 1), mirrored(high[1]), weights, 0),
        ]
        rows = [whole(lows, block) for block in range(2)]
        early_memory = [products(rows[0], later[0]), products(high[0], later[0])]
        late_memory = [products(rows[1], later[1]), products(high[1], later[1])]
        for group in range(2):
            start = whole(bases if group == 0 else second_bases, 1)
            real = early_memory[group][0] + late_memory[group][0]
            imag = early_memory[group][1] + late_memory[group][1]
            stored(1, group, start[0] + scale * imag, start[1] - scale * real)

        current = [nexts[part, ta_place].reshape(order_size, block_rows) for part in range(2)]
        mirror = mirrored([low_next[part, ta_place] for part in range(2)])
        last = window_of(current, mirror, weights, ta_place * (block_rows // NO))
        row = pl.multiple_of(tp_place * stripe, stripe)
        own = [
            nexts[part, ta_place, :, pl.ds(row, stripe), :].reshape(2 * stripe, block_rows)
            for part in range(2)
        ]
        own_rounded = [
            low_next[part, :, pl.ds(row, stripe), :].reshape(2 * stripe, order_size)
            for part in range(2)
        ]
        memory = products(own_rounded, last)
        real, imag = started(own, [turned_by(table, *halves(part)) for part in own])
        shape = (2, stripe, block_rows)
        out[0] = (real + scale * memory[1]).reshape(shape)
        out[1] = (imag - scale * memory[0]).reshape(shape)

    return pl.pallas_call(
        kernel,
        out_shape=[jax.ShapeDtypeStruct((2, 2, stripe, block_rows), jnp.float32)]
        + kept_shapes(tp_count, stripe, block_rows),
        in_specs=in_vmem(11),
        out_specs=in_vmem(4),
        input_output_aliases={8: 1, 9: 2, 10: 3},
        scratch_shapes=[
            pltpu.VMEM((2, 2, 2, block_rows, block_rows), jnp.float32),
            pltpu.VMEM((2, 2, block_rows, order_size), jnp.bfloat16),
        ],
        compiler_params=pltpu.CompilerParams(vmem_limit_bytes=24 << 20),
        name="second_stage",
    )


def replicated(green, hamiltonian, interaction):
    tp_count = lax.axis_size("tp")
    count = 2 * tp_count
    stripe = green.shape[3]
    block_rows = green.shape[4]
    factor = 1.0 / math.sqrt(2 * block_rows)
    mask, first_masks, second_masks = exchange_masks(tp_count)

    def exchanged(block, mask):
        masks = (mask, mask) if isinstance(mask, int) else mask
        return lax.ppermute(block, ("ta", "tp"), [(i, i ^ masks[i % 2]) for i in range(count)])

    arriving = exchanged(green.reshape(-1, block_rows), mask).reshape(green.shape)
    first = jnp.stack([green[:, 0, 0], arriving[:, 0, 0]])
    second = jnp.stack([green[:, 1, 0], arriving[:, 1, 0]])
    high = lax.reduce_precision(second, 8, 7)
    second = jnp.stack([high, second - high], 1).astype(jnp.bfloat16)
    first_parts = second_parts = ()
    for first_mask, second_mask in zip(zip(*first_masks), second_masks):
        first_parts = [first, exchanged(first, first_mask)]
        first = jnp.concatenate(first_parts)
        if second_mask == tp_count:
            other_high = exchanged(second[:, 0], second_mask)[:, None]
            second = jnp.concatenate([second[:, :1], other_high, second[:, 1:]], 1)
        else:
            second_parts = [second, exchanged(second, second_mask)]
            second = jnp.concatenate(second_parts)
    first_parts += [exchanged(part, 1) for part in first_parts]
    second_parts += [exchanged(part, 1) for part in second_parts]
    first_masks = [[mask] + each for each in first_masks]
    second_masks = [mask] + [later for later in second_masks if later != tp_count]
    sizes = (tp_count, stripe, block_rows, factor)
    *kept, weights, table = early_stage(first_masks, second_masks, *sizes)(
        *first_parts[::2], *second_parts[::2], hamiltonian, interaction
    )
    known = first_stage(first_masks, *sizes)(*first_parts[1::2], weights, table, *kept[:3])
    result = second_stage(second_masks, *sizes)(
        *second_parts[1::2], weights, table, *known, *kept[3:]
    )
    return result[0][:, :, None]


def solution(mesh):
    in_specs = (P(None, None, "tp", None, "ta"), P(), P())
    out_specs = P(None, None, "tp", None, "ta")
    ta_count = mesh.shape["ta"]
    tp_count = mesh.shape["tp"]

    def shards(green, hamiltonian, interaction):
        whole_bytes = green.size * green.dtype.itemsize * ta_count * tp_count
        covered = ta_count == 2 and green.shape[1] == 2 and tp_count >= 16
        if covered and tp_count & (tp_count - 1) == 0 and whole_bytes <= 1 << 22:
            return replicated(green, hamiltonian, interaction)
        return windowed(green, hamiltonian, interaction)

    return jax.shard_map(shards, mesh=mesh, in_specs=in_specs, out_specs=out_specs, check_vma=False)
```

```python
import math

import jax
import jax.numpy as jnp
from jax import lax
from jax.experimental import pallas as pl
from jax.experimental.pallas import tpu as pltpu
from jax.sharding import PartitionSpec as P

NO = 32
ITERS = 2


highest = lax.Precision.HIGHEST


def shifted(block, axis, distance):
    devices = range(lax.axis_size(axis))
    route = [(i - distance, i) for i in devices if i - distance in devices]
    return lax.ppermute(block, axis, route)


def half_dot(left_side, right_side):
    return jnp.dot(left_side, right_side, preferred_element_type=jnp.float32)


def accumulate(left_side, right_side):
    product_real = half_dot(left_side[0], right_side[0]) - half_dot(left_side[1], right_side[1])
    product_imag = half_dot(left_side[0], right_side[1]) + half_dot(left_side[1], right_side[0])
    return (product_real, product_imag)


def self_energy(values, mirror_part, weights):
    real_square = values[0] * values[0] - values[1] * values[1]
    imag_square = 2.0 * values[0] * values[1]
    sigma_real = weights * (real_square * mirror_part[0] - imag_square * mirror_part[1])
    sigma_imag = weights * (real_square * mirror_part[1] + imag_square * mirror_part[0])
    return jnp.stack([sigma_real, sigma_imag])


def windowed(green, hamiltonian, interaction):
    tp_count = lax.axis_size("tp")
    ta_place = lax.axis_index("ta")
    tp_place = lax.axis_index("tp")
    groups = green.shape[1]
    stripe = green.shape[3]
    block_rows = green.shape[4]
    columns = groups * stripe
    factor = 1.0 / math.sqrt(2 * block_rows)
    current = green[:, :, 0].reshape(2, columns, block_rows)
    squared = interaction * interaction
    column_global = (
        jnp.arange(groups, dtype=jnp.int32)[:, None] * tp_count + tp_place
    ) * stripe + jnp.arange(stripe, dtype=jnp.int32)[None, :]
    column_orbital = (column_global % NO).reshape(columns)
    onehot = (column_orbital[:, None] == jnp.arange(NO, dtype=jnp.int32)[None, :]).astype(
        jnp.float32
    )
    lookup_table = jnp.dot(onehot, squared.T, precision=highest)
    coupling = jnp.tile(lookup_table, (1, block_rows // NO))
    row_time = jnp.arange(block_rows, dtype=jnp.int32) // NO
    column_time = (tp_place * stripe + jnp.arange(stripe, dtype=jnp.int32)) // NO
    is_later = column_time[:, None] > row_time[None, :]
    block_width = math.gcd(block_rows, 128)
    blocked = jnp.kron(jnp.eye(block_width // NO, dtype=jnp.float32), hamiltonian.T)
    zero_half = jnp.zeros((), jnp.bfloat16)
    for _ in range(ITERS):
        rounded = current.astype(jnp.bfloat16)
        outgoing = rounded.reshape(2, groups, stripe, tp_count, stripe)
        previous = shifted(rounded, "ta", 1)
        earliest = shifted(rounded, "ta", 2)
        hamilton_term = jnp.dot(
            current.reshape(-1, block_width), blocked, precision=highest
        ).reshape(2, columns, block_rows)
        selected = []
        nearby = jnp.stack(
            [
                lax.dynamic_index_in_dim(
                    outgoing, jnp.minimum(ta_place + step_ahead, groups - 1), 1, keepdims=False
                )
                for step_ahead in range(3)
            ],
            1,
        )
        spread = lax.all_to_all(nearby, "tp", split_axis=3, concat_axis=3, tiled=True)
        from_one = shifted(spread[:, 1], "ta", 1)
        from_two = shifted(spread[:, 2], "ta", 2)
        received = (from_two, from_one, spread[:, 0])
        by_current = current.reshape(2, groups, stripe, block_rows)
        for window_index in range(3):
            group_pick = jnp.maximum(ta_place - 2 + window_index, 0)
            own_part = lax.dynamic_index_in_dim(by_current, group_pick, 1, keepdims=False)
            flipped = (
                jnp.transpose(received[window_index], (0, 3, 2, 1))
                .reshape(2, stripe, block_rows)
                .astype(jnp.float32)
            )
            selected.append(self_energy(own_part, flipped, coupling[:stripe]))
        oldest = jnp.where(is_later[None], selected[0], 0.0)
        middle = selected[1]
        newest = jnp.where(is_later[None], 0.0, selected[2])
        sending = jnp.stack([oldest + newest, middle], 1).astype(jnp.bfloat16)[:, :, None]
        portion = lax.all_gather(sending, "tp", axis=2, tiled=True)
        row_count = portion.shape[2] * stripe
        arriving_time = jnp.arange(row_count, dtype=jnp.int32) // NO
        later_here = (arriving_time[:, None] > row_time[None, :])[None]
        merged = portion[:, 0].reshape(2, row_count, block_rows)
        recent = portion[:, 1].reshape(2, row_count, block_rows)
        right_side = jnp.concatenate(
            [
                jnp.where(later_here, merged, zero_half),
                recent,
                jnp.where(later_here, zero_half, merged),
            ],
            1,
        )
        memory = accumulate(
            jnp.concatenate([source for source in (earliest, previous, rounded)], 2), right_side
        )
        next_real = current[0] + 0.5 * (hamilton_term[1] + factor * memory[1])
        next_imag = current[1] - 0.5 * (hamilton_term[0] + factor * memory[0])
        current = jnp.stack([next_real, next_imag])
    return current.reshape(2, groups, 1, stripe, block_rows)


def exchange_masks(tp_count):
    bits = [1 << bit for bit in reversed(range(1, tp_count.bit_length() - 1))]
    middle, low, ta_bit = bits[1:-1], bits[-1:], [tp_count]
    even, odd = ta_bit + middle + low, low + middle + ta_bit
    return bits[0], (even, odd), ta_bit + low + middle


def offsets_of(masks):
    offsets = [0]
    for mask in masks:
        offsets = offsets + [known ^ mask for known in offsets]
    return offsets


def bf16_dot(left_side, right_side):
    return lax.dot_general(
        left_side, right_side, (((1,), (0,)), ((), ())), preferred_element_type=jnp.float32
    )


def halves(values):
    high = values.astype(jnp.bfloat16)
    return high, (values - high.astype(jnp.float32)).astype(jnp.bfloat16)


def window_of(values, mirror, weights, first_time):
    rows, width = values[0].shape
    real_square = values[0] * values[0] - values[1] * values[1]
    imag_square = 2.0 * values[0] * values[1]
    real = real_square * mirror[0] - imag_square * mirror[1]
    imag = real_square * mirror[1] + imag_square * mirror[0]
    source_time = lax.broadcasted_iota(jnp.int32, (rows, width), 0) // NO
    target_time = lax.broadcasted_iota(jnp.int32, (rows, width), 1) // NO + first_time
    inside = source_time <= target_time

    def weighted(part):
        part = (part.reshape(rows // NO, NO, width) * weights[None]).reshape(rows, width)
        return jnp.where(inside, part, 0.0).astype(jnp.bfloat16)

    return weighted(real), weighted(imag)


def mirrored(rounded):
    return [jnp.transpose(part.astype(jnp.float32)) for part in rounded]


def products(left_side, right_side):
    real = bf16_dot(left_side[0], right_side[0]) - bf16_dot(left_side[1], right_side[1])
    imag = bf16_dot(left_side[0], right_side[1]) + bf16_dot(left_side[1], right_side[0])
    return real, imag


def tables_of(hamiltonian, interaction, block_rows):
    def repeated(tile):
        return jnp.concatenate([tile] * (block_rows // NO), axis=1)

    weights = repeated(jnp.transpose(interaction[...] * interaction[...]))
    table = jnp.concatenate([repeated(jnp.transpose(hamiltonian[...]))] * (block_rows // NO))
    same_time = (
        lax.broadcasted_iota(jnp.int32, table.shape, 0) // NO
        == lax.broadcasted_iota(jnp.int32, table.shape, 1) // NO
    )
    return weights, halves(jnp.where(same_time, table, 0.0))


def turned_by(table, high, low=None):
    result = bf16_dot(high, table[0]) + bf16_dot(high, table[1])
    return result if low is None else result + bf16_dot(low, table[0])


def started(values, turned):
    return values[0] + 0.5 * turned[1], values[1] - 0.5 * turned[0]


def rows_of(pieces):
    return pieces.reshape(pieces.shape[0] * pieces.shape[1], pieces.shape[2])


def whole(source, block):
    tp_count, stripe, block_rows = source.shape[1] // 2, source.shape[2], source.shape[3]
    return [
        source[part, block * tp_count : (block + 1) * tp_count].reshape(
            tp_count * stripe, block_rows
        )
        for part in range(2)
    ]


def put(device, targets, results, index, stripe):
    for target, result in zip(targets, results):
        for part in range(2):
            target[part, device] = result[part][index * stripe : (index + 1) * stripe]


def take_first(sources, late, me, offsets, stripe, table, targets):
    count = len(offsets[0]) // 2
    for flip in range(2):
        values = [rows_of(sources[flip][:, part]) for part in range(2)]
        split = [halves(part) for part in values]
        base = started(values, [turned_by(table, high, low) for high, low in split])
        highs = [high for high, _ in split]
        for index in range(count):
            place = late * count + index
            mask = jnp.where(me % 2 == flip, offsets[0][place], offsets[1][place])
            put(me ^ (flip ^ mask), targets, (values, highs, base), index, stripe)


def take_second(sources, late, me, offsets, tp_count, stripe, table, targets):
    count = len(offsets) // 2
    for flip in range(2):
        for plane in range(2):
            highs = [rows_of(sources[flip][:, plane, part]) for part in range(2)]
            values = [high.astype(jnp.float32) for high in highs]
            if plane == 0:
                lows = [rows_of(sources[flip][:, 2, part]) for part in range(2)]
                values = [values[part] + lows[part].astype(jnp.float32) for part in range(2)]
                turned = [turned_by(table, highs[part], lows[part]) for part in range(2)]
            else:
                turned = [turned_by(table, high) for high in highs]
            base = started(values, turned)
            for index in range(count):
                device = me ^ (flip ^ offsets[late * count + index] ^ (plane * tp_count))
                put(device, targets, (values, highs, base), index, stripe)


def own_place(tp_count):
    return lax.axis_index("ta") * tp_count + lax.axis_index("tp")


def kept_shapes(tp_count, stripe, block_rows):
    pieces = (2, 2 * tp_count, stripe, block_rows)
    return [jax.ShapeDtypeStruct(pieces, each) for each in (jnp.float32, jnp.bfloat16, jnp.float32)]


def in_vmem(count):
    return [pl.BlockSpec(memory_space=pltpu.VMEM)] * count


def early_stage(masks, tp_count, stripe, block_rows, factor):
    offsets = [offsets_of(each) for each in masks]

    def kernel(*refs):
        hamiltonian, interaction, weights_out, table_out = refs[2:4] + refs[7:]
        me = own_place(tp_count)
        weights, table = tables_of(hamiltonian, interaction, block_rows)
        weights_out[...] = weights
        table_out[0] = table[0]
        table_out[1] = table[1]
        take_first(refs[:2], 0, me, offsets, stripe, table, refs[4:7])

    shapes = kept_shapes(tp_count, stripe, block_rows)
    tables = [
        jax.ShapeDtypeStruct((NO, block_rows), jnp.float32),
        jax.ShapeDtypeStruct((2, block_rows, block_rows), jnp.bfloat16),
    ]
    return pl.pallas_call(
        kernel,
        out_shape=shapes + tables,
        in_specs=in_vmem(4),
        out_specs=in_vmem(5),
        compiler_params=pltpu.CompilerParams(vmem_limit_bytes=16 << 20),
        name="early_stage",
    )


def first_stage(masks, tp_count, stripe, block_rows, factor):
    offsets = [offsets_of(each) for each in masks]
    scale = 0.5 * factor

    def kernel(*refs):
        weights, table = refs[2], (refs[3][0], refs[3][1])
        targets, window = refs[7:10], refs[10]
        take_first(refs[:2], 1, own_place(tp_count), offsets, stripe, table, targets)
        values, highs, bases = targets
        high = whole(highs, 0)
        made = window_of(whole(values, 0), mirrored(high), weights[...], 0)
        memory = products(high, made)
        window[0] = made[0]
        window[1] = made[1]
        half = (tp_count, stripe, block_rows)
        bases[0, :tp_count] = bases[0, :tp_count] + scale * memory[1].reshape(half)
        bases[1, :tp_count] = bases[1, :tp_count] - scale * memory[0].reshape(half)

    square = jax.ShapeDtypeStruct((2, block_rows, block_rows), jnp.bfloat16)
    return pl.pallas_call(
        kernel,
        out_shape=kept_shapes(tp_count, stripe, block_rows) + [square],
        in_specs=in_vmem(7),
        out_specs=in_vmem(4),
        input_output_aliases={4: 0, 5: 1, 6: 2},
        compiler_params=pltpu.CompilerParams(vmem_limit_bytes=16 << 20),
        name="first_stage",
    )


def second_stage(masks, tp_count, stripe, block_rows, factor):
    offsets = offsets_of(masks)
    order_size = 2 * block_rows
    scale = 0.5 * factor

    def kernel(*refs):
        weights, table = refs[4][...], (refs[5][0], refs[5][1])
        values, lows, bases, window = refs[6:10]
        out, targets, nexts, low_next = refs[10], refs[11:14], refs[14], refs[15]
        ta_place = lax.axis_index("ta")
        tp_place = lax.axis_index("tp")
        me = own_place(tp_count)
        for late in range(2):
            sources = refs[late:4:2]
            take_second(sources, late, me, offsets, tp_count, stripe, table, targets)
        second_values, second_highs, second_bases = targets
        high = [whole(second_highs, block) for block in range(2)]

        def stored(block, group, real, imag):
            for part, result in ((0, real), (1, imag)):
                nexts[part, block, group] = result
                low_next[part, group, :, block * block_rows : (block + 1) * block_rows] = (
                    result.astype(jnp.bfloat16)
                )

        stored(0, 0, *whole(bases, 0))
        memory = products(high[0], (window[0], window[1]))
        base = whole(second_bases, 0)
        stored(0, 1, base[0] + scale * memory[1], base[1] - scale * memory[0])
        later = [
            window_of(whole(values, 1), mirrored(high[0]), weights, block_rows // NO),
            window_of(whole(second_values, 1), mirrored(high[1]), weights, 0),
        ]
        rows = [whole(lows, block) for block in range(2)]
        early_memory = [products(rows[0], later[0]), products(high[0], later[0])]
        late_memory = [products(rows[1], later[1]), products(high[1], later[1])]
        for group in range(2):
            start = whole(bases if group == 0 else second_bases, 1)
            real = early_memory[group][0] + late_memory[group][0]
            imag = early_memory[group][1] + late_memory[group][1]
            stored(1, group, start[0] + scale * imag, start[1] - scale * real)

        current = [nexts[part, ta_place].reshape(order_size, block_rows) for part in range(2)]
        mirror = mirrored([low_next[part, ta_place] for part in range(2)])
        last = window_of(current, mirror, weights, ta_place * (block_rows // NO))
        row = pl.multiple_of(tp_place * stripe, stripe)
        own = [
            nexts[part, ta_place, :, pl.ds(row, stripe), :].reshape(2 * stripe, block_rows)
            for part in range(2)
        ]
        own_rounded = [
            low_next[part, :, pl.ds(row, stripe), :].reshape(2 * stripe, order_size)
            for part in range(2)
        ]
        memory = products(own_rounded, last)
        real, imag = started(own, [turned_by(table, *halves(part)) for part in own])
        shape = (2, stripe, block_rows)
        out[0] = (real + scale * memory[1]).reshape(shape)
        out[1] = (imag - scale * memory[0]).reshape(shape)

    return pl.pallas_call(
        kernel,
        out_shape=jax.ShapeDtypeStruct((2, 2, stripe, block_rows), jnp.float32),
        in_specs=in_vmem(10),
        out_specs=in_vmem(1)[0],
        scratch_shapes=[
            pltpu.VMEM(each.shape, each.dtype)
            for each in kept_shapes(tp_count, stripe, block_rows)
        ]
        + [
            pltpu.VMEM((2, 2, 2, block_rows, block_rows), jnp.float32),
            pltpu.VMEM((2, 2, block_rows, order_size), jnp.bfloat16),
        ],
        compiler_params=pltpu.CompilerParams(vmem_limit_bytes=24 << 20),
        name="second_stage",
    )


def replicated(green, hamiltonian, interaction):
    tp_count = lax.axis_size("tp")
    count = 2 * tp_count
    stripe = green.shape[3]
    block_rows = green.shape[4]
    factor = 1.0 / math.sqrt(2 * block_rows)
    mask, first_masks, second_masks = exchange_masks(tp_count)

    def exchanged(block, mask):
        masks = (mask, mask) if isinstance(mask, int) else mask
        return lax.ppermute(block, ("ta", "tp"), [(i, i ^ masks[i % 2]) for i in range(count)])

    arriving = exchanged(green.reshape(-1, block_rows), mask).reshape(green.shape)
    first = jnp.stack([green[:, 0, 0], arriving[:, 0, 0]])
    second = jnp.stack([green[:, 1, 0], arriving[:, 1, 0]])
    high = lax.reduce_precision(second, 8, 7)
    second = jnp.stack([high, second - high], 1).astype(jnp.bfloat16)
    first_parts = second_parts = ()
    for first_mask, second_mask in zip(zip(*first_masks), second_masks):
        first_parts = [first, exchanged(first, first_mask)]
        first = jnp.concatenate(first_parts)
        if second_mask == tp_count:
            other_high = exchanged(second[:, 0], second_mask)[:, None]
            second = jnp.concatenate([second[:, :1], other_high, second[:, 1:]], 1)
        else:
            second_parts = [second, exchanged(second, second_mask)]
            second = jnp.concatenate(second_parts)
    first_parts += [exchanged(first_parts[0], 1)]
    first_parts += [exchanged(first_parts[1], 1)]
    second_parts += [exchanged(part, 1) for part in second_parts]
    first_masks = [[mask] + each for each in first_masks]
    second_masks = [mask] + [later for later in second_masks if later != tp_count]
    sizes = (tp_count, stripe, block_rows, factor)
    *kept, weights, table = early_stage(first_masks, *sizes)(
        *first_parts[::2], hamiltonian, interaction
    )
    known = first_stage(first_masks, *sizes)(*first_parts[1::2], weights, table, *kept)
    result = second_stage(second_masks, *sizes)(*second_parts, weights, table, *known)
    return result[:, :, None]


def solution(mesh):
    in_specs = (P(None, None, "tp", None, "ta"), P(), P())
    out_specs = P(None, None, "tp", None, "ta")
    ta_count = mesh.shape["ta"]
    tp_count = mesh.shape["tp"]

    def shards(green, hamiltonian, interaction):
        whole_bytes = green.size * green.dtype.itemsize * ta_count * tp_count
        covered = ta_count == 2 and green.shape[1] == 2 and tp_count >= 16
        if covered and tp_count & (tp_count - 1) == 0 and whole_bytes <= 1 << 22:
            return replicated(green, hamiltonian, interaction)
        return windowed(green, hamiltonian, interaction)

    return jax.shard_map(shards, mesh=mesh, in_specs=in_specs, out_specs=out_specs, check_vma=False)
```

```python
import math

import jax
import jax.numpy as jnp
from jax import lax
from jax.experimental import pallas as pl
from jax.experimental.pallas import tpu as pltpu
from jax.sharding import PartitionSpec as P

NO = 32
ITERS = 2


highest = lax.Precision.HIGHEST


def shifted(block, axis, distance):
    devices = range(lax.axis_size(axis))
    route = [(i - distance, i) for i in devices if i - distance in devices]
    return lax.ppermute(block, axis, route)


def half_dot(left_side, right_side):
    return jnp.dot(left_side, right_side, preferred_element_type=jnp.float32)


def accumulate(left_side, right_side):
    product_real = half_dot(left_side[0], right_side[0]) - half_dot(left_side[1], right_side[1])
    product_imag = half_dot(left_side[0], right_side[1]) + half_dot(left_side[1], right_side[0])
    return (product_real, product_imag)


def self_energy(values, mirror_part, weights):
    real_square = values[0] * values[0] - values[1] * values[1]
    imag_square = 2.0 * values[0] * values[1]
    sigma_real = weights * (real_square * mirror_part[0] - imag_square * mirror_part[1])
    sigma_imag = weights * (real_square * mirror_part[1] + imag_square * mirror_part[0])
    return jnp.stack([sigma_real, sigma_imag])


def windowed(green, hamiltonian, interaction):
    tp_count = lax.axis_size("tp")
    ta_place = lax.axis_index("ta")
    tp_place = lax.axis_index("tp")
    groups = green.shape[1]
    stripe = green.shape[3]
    block_rows = green.shape[4]
    columns = groups * stripe
    factor = 1.0 / math.sqrt(2 * block_rows)
    current = green[:, :, 0].reshape(2, columns, block_rows)
    squared = interaction * interaction
    column_global = (
        jnp.arange(groups, dtype=jnp.int32)[:, None] * tp_count + tp_place
    ) * stripe + jnp.arange(stripe, dtype=jnp.int32)[None, :]
    column_orbital = (column_global % NO).reshape(columns)
    onehot = (column_orbital[:, None] == jnp.arange(NO, dtype=jnp.int32)[None, :]).astype(
        jnp.float32
    )
    lookup_table = jnp.dot(onehot, squared.T, precision=highest)
    coupling = jnp.tile(lookup_table, (1, block_rows // NO))
    row_time = jnp.arange(block_rows, dtype=jnp.int32) // NO
    column_time = (tp_place * stripe + jnp.arange(stripe, dtype=jnp.int32)) // NO
    is_later = column_time[:, None] > row_time[None, :]
    block_width = math.gcd(block_rows, 128)
    blocked = jnp.kron(jnp.eye(block_width // NO, dtype=jnp.float32), hamiltonian.T)
    zero_half = jnp.zeros((), jnp.bfloat16)
    for _ in range(ITERS):
        rounded = current.astype(jnp.bfloat16)
        outgoing = rounded.reshape(2, groups, stripe, tp_count, stripe)
        previous = shifted(rounded, "ta", 1)
        earliest = shifted(rounded, "ta", 2)
        hamilton_term = jnp.dot(
            current.reshape(-1, block_width), blocked, precision=highest
        ).reshape(2, columns, block_rows)
        selected = []
        nearby = jnp.stack(
            [
                lax.dynamic_index_in_dim(
                    outgoing, jnp.minimum(ta_place + step_ahead, groups - 1), 1, keepdims=False
                )
                for step_ahead in range(3)
            ],
            1,
        )
        spread = lax.all_to_all(nearby, "tp", split_axis=3, concat_axis=3, tiled=True)
        from_one = shifted(spread[:, 1], "ta", 1)
        from_two = shifted(spread[:, 2], "ta", 2)
        received = (from_two, from_one, spread[:, 0])
        by_current = current.reshape(2, groups, stripe, block_rows)
        for window_index in range(3):
            group_pick = jnp.maximum(ta_place - 2 + window_index, 0)
            own_part = lax.dynamic_index_in_dim(by_current, group_pick, 1, keepdims=False)
            flipped = (
                jnp.transpose(received[window_index], (0, 3, 2, 1))
                .reshape(2, stripe, block_rows)
                .astype(jnp.float32)
            )
            selected.append(self_energy(own_part, flipped, coupling[:stripe]))
        oldest = jnp.where(is_later[None], selected[0], 0.0)
        middle = selected[1]
        newest = jnp.where(is_later[None], 0.0, selected[2])
        sending = jnp.stack([oldest + newest, middle], 1).astype(jnp.bfloat16)[:, :, None]
        portion = lax.all_gather(sending, "tp", axis=2, tiled=True)
        row_count = portion.shape[2] * stripe
        arriving_time = jnp.arange(row_count, dtype=jnp.int32) // NO
        later_here = (arriving_time[:, None] > row_time[None, :])[None]
        merged = portion[:, 0].reshape(2, row_count, block_rows)
        recent = portion[:, 1].reshape(2, row_count, block_rows)
        right_side = jnp.concatenate(
            [
                jnp.where(later_here, merged, zero_half),
                recent,
                jnp.where(later_here, zero_half, merged),
            ],
            1,
        )
        memory = accumulate(
            jnp.concatenate([source for source in (earliest, previous, rounded)], 2), right_side
        )
        next_real = current[0] + 0.5 * (hamilton_term[1] + factor * memory[1])
        next_imag = current[1] - 0.5 * (hamilton_term[0] + factor * memory[0])
        current = jnp.stack([next_real, next_imag])
    return current.reshape(2, groups, 1, stripe, block_rows)


def exchange_masks(tp_count):
    bits = [1 << bit for bit in reversed(range(1, tp_count.bit_length() - 1))]
    middle, low, ta_bit = bits[1:-1], bits[-1:], [tp_count]
    even, odd = ta_bit + middle + low, low + middle + ta_bit
    return bits[0], (even, odd), ta_bit + low + middle


def offsets_of(masks):
    offsets = [0]
    for mask in masks:
        offsets = offsets + [known ^ mask for known in offsets]
    return offsets


def bf16_dot(left_side, right_side):
    return lax.dot_general(
        left_side, right_side, (((1,), (0,)), ((), ())), preferred_element_type=jnp.float32
    )


def halves(values):
    high = values.astype(jnp.bfloat16)
    return high, (values - high.astype(jnp.float32)).astype(jnp.bfloat16)


def window_of(values, mirror, weights, first_time=None):
    rows, width = values[0].shape
    real_square = values[0] * values[0] - values[1] * values[1]
    imag_square = 2.0 * values[0] * values[1]
    real = real_square * mirror[0] - imag_square * mirror[1]
    imag = real_square * mirror[1] + imag_square * mirror[0]
    inside = None
    if first_time is not None:
        source_time = lax.broadcasted_iota(jnp.int32, (rows, width), 0) // NO
        target_time = lax.broadcasted_iota(jnp.int32, (rows, width), 1) // NO + first_time
        inside = source_time <= target_time

    def weighted(part):
        part = (part.reshape(rows // NO, NO, width) * weights[None]).reshape(rows, width)
        part = part if inside is None else jnp.where(inside, part, 0.0)
        return part.astype(jnp.bfloat16)

    real, imag = weighted(real), weighted(imag)
    return [jnp.concatenate([real, -imag]), jnp.concatenate([imag, real])]


def mirrored(rounded):
    return [jnp.transpose(part.astype(jnp.float32)) for part in rounded]


def products(left_side, right_side):
    left_side = jnp.concatenate(left_side, axis=1)
    return [bf16_dot(left_side, part) for part in right_side]


def tables_of(hamiltonian, interaction, block_rows):
    def repeated(tile):
        return jnp.concatenate([tile] * (block_rows // NO), axis=1)

    weights = repeated(jnp.transpose(interaction[...] * interaction[...]))
    table = jnp.concatenate([repeated(jnp.transpose(hamiltonian[...]))] * (block_rows // NO))
    same_time = (
        lax.broadcasted_iota(jnp.int32, table.shape, 0) // NO
        == lax.broadcasted_iota(jnp.int32, table.shape, 1) // NO
    )
    high, low = halves(jnp.where(same_time, table, 0.0))
    return weights, jnp.concatenate([high, high, low])


def turned_by(table, high, low):
    return bf16_dot(jnp.concatenate([low, high, high], axis=1), table)


def started(values, turned):
    return values[0] + 0.5 * turned[1], values[1] - 0.5 * turned[0]


def rows_of(pieces):
    return pieces.reshape(pieces.shape[0] * pieces.shape[1], pieces.shape[2])


def whole(source, block):
    tp_count, stripe, block_rows = source.shape[1] // 2, source.shape[2], source.shape[3]
    return [
        source[part, block * tp_count : (block + 1) * tp_count].reshape(
            tp_count * stripe, block_rows
        )
        for part in range(2)
    ]


def put(device, targets, results, index, stripe):
    for target, result in zip(targets, results):
        for part in range(2):
            target[part, device] = result[part][index * stripe : (index + 1) * stripe]


def take_first(sources, late, me, offsets, stripe, table, targets):
    count = len(offsets[0]) // 2
    for flip in range(2):
        values = [rows_of(sources[flip][:, part]) for part in range(2)]
        split = [halves(part) for part in values]
        base = started(values, [turned_by(table, high, low) for high, low in split])
        highs = [high for high, _ in split]
        for index in range(count):
            place = late * count + index
            mask = jnp.where(me % 2 == flip, offsets[0][place], offsets[1][place])
            put(me ^ (flip ^ mask), targets, (values, highs, base), index, stripe)


def own_place(tp_count):
    return lax.axis_index("ta") * tp_count + lax.axis_index("tp")


def kept_shapes(tp_count, stripe, block_rows):
    pieces = (2, 2 * tp_count, stripe, block_rows)
    return [jax.ShapeDtypeStruct(pieces, each) for each in (jnp.float32, jnp.bfloat16, jnp.float32)]


def in_vmem(count):
    return [pl.BlockSpec(memory_space=pltpu.VMEM)] * count


def early_stage(masks, tp_count, stripe, block_rows, factor):
    offsets = [offsets_of(each) for each in masks]

    def kernel(*refs):
        hamiltonian, interaction, weights_out, table_out = refs[2:4] + refs[7:]
        me = own_place(tp_count)
        weights, table = tables_of(hamiltonian, interaction, block_rows)
        weights_out[...] = weights
        table_out[...] = table
        take_first(refs[:2], 0, me, offsets, stripe, table, refs[4:7])

    shapes = kept_shapes(tp_count, stripe, block_rows)
    tables = [
        jax.ShapeDtypeStruct((NO, block_rows), jnp.float32),
        jax.ShapeDtypeStruct((3 * block_rows, block_rows), jnp.bfloat16),
    ]
    return pl.pallas_call(
        kernel,
        out_shape=shapes + tables,
        in_specs=in_vmem(4),
        out_specs=in_vmem(5),
        compiler_params=pltpu.CompilerParams(vmem_limit_bytes=16 << 20),
        name="early_stage",
    )


def first_stage(masks, tp_count, stripe, block_rows, factor):
    offsets = [offsets_of(each) for each in masks]
    scale = 0.5 * factor

    def kernel(*refs):
        weights, table = refs[2], refs[3][...]
        targets, window = refs[7:10], refs[10]
        take_first(refs[:2], 1, own_place(tp_count), offsets, stripe, table, targets)
        values, highs, bases = targets
        high = whole(highs, 0)
        made = window_of(whole(values, 0), mirrored(high), weights[...], 0)
        memory = products(high, made)
        window[0] = made[0]
        window[1] = made[1]
        half = (tp_count, stripe, block_rows)
        bases[0, :tp_count] = bases[0, :tp_count] + scale * memory[1].reshape(half)
        bases[1, :tp_count] = bases[1, :tp_count] - scale * memory[0].reshape(half)

    square = jax.ShapeDtypeStruct((2, 2 * block_rows, block_rows), jnp.bfloat16)
    return pl.pallas_call(
        kernel,
        out_shape=kept_shapes(tp_count, stripe, block_rows) + [square],
        in_specs=in_vmem(7),
        out_specs=in_vmem(4),
        input_output_aliases={4: 0, 5: 1, 6: 2},
        compiler_params=pltpu.CompilerParams(vmem_limit_bytes=16 << 20),
        name="first_stage",
    )


def second_stage(masks, tp_count, stripe, block_rows, factor):
    offsets = offsets_of(masks)
    half_count = len(offsets) // 2
    order_size = 2 * block_rows
    scale = 0.5 * factor

    def kernel(*refs):
        weights, table = refs[4][...], refs[5][...]
        values, lows, bases, window = refs[6:10]
        out, highs, rests, nexts, low_next = refs[10:]
        ta_place = lax.axis_index("ta")
        tp_place = lax.axis_index("tp")
        me = own_place(tp_count)
        blank = jnp.zeros((stripe, block_rows), jnp.bfloat16)
        for flip in range(2):
            for index, mask in enumerate(offsets):
                late, slot = divmod(index, half_count)
                device = me ^ (flip ^ mask)
                other = device ^ tp_count
                source = refs[2 * flip + late]
                for part in range(2):
                    highs[part, device] = source[slot, 0, part]
                    highs[part, other] = source[slot, 1, part]
                    rests[part, device] = source[slot, 2, part]
                    rests[part, other] = blank
        high = [whole(highs, block) for block in range(2)]
        rest = [whole(rests, block) for block in range(2)]
        full = [
            [high[block][k].astype(jnp.float32) + rest[block][k].astype(jnp.float32) for k in range(2)]
            for block in range(2)
        ]
        base = [
            started(full[block], [turned_by(table, high[block][k], rest[block][k]) for k in range(2)])
            for block in range(2)
        ]

        def stored(block, group, real, imag):
            for part, result in ((0, real), (1, imag)):
                nexts[part, block, group] = result
                low_next[part, group, :, block * block_rows : (block + 1) * block_rows] = (
                    result.astype(jnp.bfloat16)
                )

        stored(0, 0, *whole(bases, 0))
        memory = products(high[0], [window[0], window[1]])
        stored(0, 1, base[0][0] + scale * memory[1], base[0][1] - scale * memory[0])
        later = [
            window_of(whole(values, 1), mirrored(high[0]), weights),
            window_of(full[1], mirrored(high[1]), weights, 0),
        ]
        later = [jnp.concatenate([later[0][k], later[1][k]]) for k in range(2)]
        for group in range(2):
            start = whole(bases, 1) if group == 0 else base[1]
            rows = whole(lows, 0) + whole(lows, 1) if group == 0 else high[0] + high[1]
            memory = products(rows, later)
            stored(1, group, start[0] + scale * memory[1], start[1] - scale * memory[0])

        current = [nexts[part, ta_place].reshape(order_size, block_rows) for part in range(2)]
        mirror = mirrored([low_next[part, ta_place] for part in range(2)])
        last = window_of(current, mirror, weights, ta_place * (block_rows // NO))
        row = pl.multiple_of(tp_place * stripe, stripe)
        own = [
            nexts[part, ta_place, :, pl.ds(row, stripe), :].reshape(2 * stripe, block_rows)
            for part in range(2)
        ]
        own_rounded = [
            low_next[part, :, pl.ds(row, stripe), :].reshape(2 * stripe, order_size)
            for part in range(2)
        ]
        memory = products(own_rounded, last)
        real, imag = started(own, [turned_by(table, *halves(part)) for part in own])
        shape = (2, stripe, block_rows)
        out[0] = (real + scale * memory[1]).reshape(shape)
        out[1] = (imag - scale * memory[0]).reshape(shape)

    return pl.pallas_call(
        kernel,
        out_shape=jax.ShapeDtypeStruct((2, 2, stripe, block_rows), jnp.float32),
        in_specs=in_vmem(10),
        out_specs=in_vmem(1)[0],
        scratch_shapes=[pltpu.VMEM((2, 2 * tp_count, stripe, block_rows), jnp.bfloat16)] * 2
        + [
            pltpu.VMEM((2, 2, 2, block_rows, block_rows), jnp.float32),
            pltpu.VMEM((2, 2, block_rows, order_size), jnp.bfloat16),
        ],
        compiler_params=pltpu.CompilerParams(vmem_limit_bytes=24 << 20),
        name="second_stage",
    )


def replicated(green, hamiltonian, interaction):
    tp_count = lax.axis_size("tp")
    count = 2 * tp_count
    stripe = green.shape[3]
    block_rows = green.shape[4]
    factor = 1.0 / math.sqrt(2 * block_rows)
    mask, first_masks, second_masks = exchange_masks(tp_count)

    def exchanged(block, mask):
        masks = (mask, mask) if isinstance(mask, int) else mask
        return lax.ppermute(block, ("ta", "tp"), [(i, i ^ masks[i % 2]) for i in range(count)])

    arriving = exchanged(green.reshape(-1, block_rows), mask).reshape(green.shape)
    first = jnp.stack([green[:, 0, 0], arriving[:, 0, 0]])
    second = jnp.stack([green[:, 1, 0], arriving[:, 1, 0]])
    high = lax.reduce_precision(second, 8, 7)
    second = jnp.stack([high, second - high], 1).astype(jnp.bfloat16)
    first_parts = second_parts = ()
    for first_mask, second_mask in zip(zip(*first_masks), second_masks):
        first_parts = [first, exchanged(first, first_mask)]
        first = jnp.concatenate(first_parts)
        if second_mask == tp_count:
            other_high = exchanged(second[:, 0], second_mask)[:, None]
            second = jnp.concatenate([second[:, :1], other_high, second[:, 1:]], 1)
        else:
            second_parts = [second, exchanged(second, second_mask)]
            second = jnp.concatenate(second_parts)
    first_parts += [exchanged(first_parts[0], 1)]
    first_parts += [exchanged(first_parts[1], 1)]
    second_parts += [exchanged(part, 1) for part in second_parts]
    first_masks = [[mask] + each for each in first_masks]
    second_masks = [mask] + [later for later in second_masks if later != tp_count]
    sizes = (tp_count, stripe, block_rows, factor)
    *kept, weights, table = early_stage(first_masks, *sizes)(
        *first_parts[::2], hamiltonian, interaction
    )
    known = first_stage(first_masks, *sizes)(*first_parts[1::2], weights, table, *kept)
    result = second_stage(second_masks, *sizes)(*second_parts, weights, table, *known)
    return result[:, :, None]


def solution(mesh):
    in_specs = (P(None, None, "tp", None, "ta"), P(), P())
    out_specs = P(None, None, "tp", None, "ta")
    ta_count = mesh.shape["ta"]
    tp_count = mesh.shape["tp"]

    def shards(green, hamiltonian, interaction):
        whole_bytes = green.size * green.dtype.itemsize * ta_count * tp_count
        covered = ta_count == 2 and green.shape[1] == 2 and tp_count >= 16
        if covered and tp_count & (tp_count - 1) == 0 and whole_bytes <= 1 << 22:
            return replicated(green, hamiltonian, interaction)
        return windowed(green, hamiltonian, interaction)

    return jax.shard_map(shards, mesh=mesh, in_specs=in_specs, out_specs=out_specs, check_vma=False)
```

```python
import math

import jax
import jax.numpy as jnp
from jax import lax
from jax.experimental import pallas as pl
from jax.experimental.pallas import tpu as pltpu
from jax.sharding import PartitionSpec as P

NO = 32
ITERS = 2


highest = lax.Precision.HIGHEST


def shifted(block, axis, distance):
    devices = range(lax.axis_size(axis))
    route = [(i - distance, i) for i in devices if i - distance in devices]
    return lax.ppermute(block, axis, route)


def half_dot(left_side, right_side):
    return jnp.dot(left_side, right_side, preferred_element_type=jnp.float32)


def accumulate(left_side, right_side):
    product_real = half_dot(left_side[0], right_side[0]) - half_dot(left_side[1], right_side[1])
    product_imag = half_dot(left_side[0], right_side[1]) + half_dot(left_side[1], right_side[0])
    return (product_real, product_imag)


def self_energy(values, mirror_part, weights):
    real_square = values[0] * values[0] - values[1] * values[1]
    imag_square = 2.0 * values[0] * values[1]
    sigma_real = weights * (real_square * mirror_part[0] - imag_square * mirror_part[1])
    sigma_imag = weights * (real_square * mirror_part[1] + imag_square * mirror_part[0])
    return jnp.stack([sigma_real, sigma_imag])


def windowed(green, hamiltonian, interaction):
    tp_count = lax.axis_size("tp")
    ta_place = lax.axis_index("ta")
    tp_place = lax.axis_index("tp")
    groups = green.shape[1]
    stripe = green.shape[3]
    block_rows = green.shape[4]
    columns = groups * stripe
    factor = 1.0 / math.sqrt(2 * block_rows)
    current = green[:, :, 0].reshape(2, columns, block_rows)
    squared = interaction * interaction
    column_global = (
        jnp.arange(groups, dtype=jnp.int32)[:, None] * tp_count + tp_place
    ) * stripe + jnp.arange(stripe, dtype=jnp.int32)[None, :]
    column_orbital = (column_global % NO).reshape(columns)
    onehot = (column_orbital[:, None] == jnp.arange(NO, dtype=jnp.int32)[None, :]).astype(
        jnp.float32
    )
    lookup_table = jnp.dot(onehot, squared.T, precision=highest)
    coupling = jnp.tile(lookup_table, (1, block_rows // NO))
    row_time = jnp.arange(block_rows, dtype=jnp.int32) // NO
    column_time = (tp_place * stripe + jnp.arange(stripe, dtype=jnp.int32)) // NO
    is_later = column_time[:, None] > row_time[None, :]
    block_width = math.gcd(block_rows, 128)
    blocked = jnp.kron(jnp.eye(block_width // NO, dtype=jnp.float32), hamiltonian.T)
    zero_half = jnp.zeros((), jnp.bfloat16)
    for _ in range(ITERS):
        rounded = current.astype(jnp.bfloat16)
        outgoing = rounded.reshape(2, groups, stripe, tp_count, stripe)
        previous = shifted(rounded, "ta", 1)
        earliest = shifted(rounded, "ta", 2)
        hamilton_term = jnp.dot(
            current.reshape(-1, block_width), blocked, precision=highest
        ).reshape(2, columns, block_rows)
        selected = []
        nearby = jnp.stack(
            [
                lax.dynamic_index_in_dim(
                    outgoing, jnp.minimum(ta_place + step_ahead, groups - 1), 1, keepdims=False
                )
                for step_ahead in range(3)
            ],
            1,
        )
        spread = lax.all_to_all(nearby, "tp", split_axis=3, concat_axis=3, tiled=True)
        from_one = shifted(spread[:, 1], "ta", 1)
        from_two = shifted(spread[:, 2], "ta", 2)
        received = (from_two, from_one, spread[:, 0])
        by_current = current.reshape(2, groups, stripe, block_rows)
        for window_index in range(3):
            group_pick = jnp.maximum(ta_place - 2 + window_index, 0)
            own_part = lax.dynamic_index_in_dim(by_current, group_pick, 1, keepdims=False)
            flipped = (
                jnp.transpose(received[window_index], (0, 3, 2, 1))
                .reshape(2, stripe, block_rows)
                .astype(jnp.float32)
            )
            selected.append(self_energy(own_part, flipped, coupling[:stripe]))
        oldest = jnp.where(is_later[None], selected[0], 0.0)
        middle = selected[1]
        newest = jnp.where(is_later[None], 0.0, selected[2])
        sending = jnp.stack([oldest + newest, middle], 1).astype(jnp.bfloat16)[:, :, None]
        portion = lax.all_gather(sending, "tp", axis=2, tiled=True)
        row_count = portion.shape[2] * stripe
        arriving_time = jnp.arange(row_count, dtype=jnp.int32) // NO
        later_here = (arriving_time[:, None] > row_time[None, :])[None]
        merged = portion[:, 0].reshape(2, row_count, block_rows)
        recent = portion[:, 1].reshape(2, row_count, block_rows)
        right_side = jnp.concatenate(
            [
                jnp.where(later_here, merged, zero_half),
                recent,
                jnp.where(later_here, zero_half, merged),
            ],
            1,
        )
        memory = accumulate(
            jnp.concatenate([source for source in (earliest, previous, rounded)], 2), right_side
        )
        next_real = current[0] + 0.5 * (hamilton_term[1] + factor * memory[1])
        next_imag = current[1] - 0.5 * (hamilton_term[0] + factor * memory[0])
        current = jnp.stack([next_real, next_imag])
    return current.reshape(2, groups, 1, stripe, block_rows)


def exchange_masks(tp_count):
    bits = [1 << bit for bit in reversed(range(1, tp_count.bit_length() - 1))]
    middle, low, ta_bit = bits[1:-1], bits[-1:], [tp_count]
    even, odd = ta_bit + middle + low, low + middle + ta_bit
    return bits[0], (even, odd), ta_bit + low + middle


def offsets_of(masks):
    offsets = [0]
    for mask in masks:
        offsets = offsets + [known ^ mask for known in offsets]
    return offsets


def bf16_dot(left_side, right_side):
    return lax.dot_general(
        left_side, right_side, (((1,), (0,)), ((), ())), preferred_element_type=jnp.float32
    )


def halves(values):
    high = values.astype(jnp.bfloat16)
    return high, (values - high.astype(jnp.float32)).astype(jnp.bfloat16)


def squares_of(values, weights):
    real = values[0] * values[0] - values[1] * values[1]
    imag = 2.0 * values[0] * values[1]
    return real * weights, imag * weights


def window_of(squares, mirror):
    real = squares[0] * mirror[0] - squares[1] * mirror[1]
    imag = squares[0] * mirror[1] + squares[1] * mirror[0]
    real, imag = real.astype(jnp.bfloat16), imag.astype(jnp.bfloat16)
    return [jnp.concatenate([real, -imag]), jnp.concatenate([imag, real])]


def inside_only(weights, first_time):
    source_time = lax.broadcasted_iota(jnp.int32, weights.shape, 0) // NO
    target_time = lax.broadcasted_iota(jnp.int32, weights.shape, 1) // NO + first_time
    return jnp.where(source_time <= target_time, weights, 0.0)


def mirrored(rounded):
    return [jnp.transpose(part.astype(jnp.float32)) for part in rounded]


def products(left_side, right_side):
    left_side = jnp.concatenate(left_side, axis=1)
    return [bf16_dot(left_side, part) for part in right_side]


def tables_of(hamiltonian, interaction, block_rows):
    def repeated(tile):
        return jnp.concatenate([tile] * (block_rows // NO), axis=1)

    weights = repeated(jnp.transpose(interaction[...] * interaction[...]))
    table = jnp.concatenate([repeated(jnp.transpose(hamiltonian[...]))] * (block_rows // NO))
    same_time = (
        lax.broadcasted_iota(jnp.int32, table.shape, 0) // NO
        == lax.broadcasted_iota(jnp.int32, table.shape, 1) // NO
    )
    high, low = halves(jnp.where(same_time, table, 0.0))
    return weights, jnp.concatenate([high, high, low])


def turned_by(table, high, low):
    return bf16_dot(jnp.concatenate([low, high, high], axis=1), table)


def started(values, turned):
    return values[0] + 0.5 * turned[1], values[1] - 0.5 * turned[0]


def rows_of(pieces):
    return pieces.reshape(pieces.shape[0] * pieces.shape[1], pieces.shape[2])


def whole(source, block):
    tp_count, stripe, block_rows = source.shape[1] // 2, source.shape[2], source.shape[3]
    return [
        source[part, block * tp_count : (block + 1) * tp_count].reshape(
            tp_count * stripe, block_rows
        )
        for part in range(2)
    ]


def put(device, targets, results, index, stripe):
    for target, result in zip(targets, results):
        for part in range(2):
            target[part, device] = result[part][index * stripe : (index + 1) * stripe]


def take_first(sources, late, me, offsets, stripe, table, targets):
    count = len(offsets[0]) // 2
    for flip in range(2):
        values = [rows_of(sources[flip][:, part]) for part in range(2)]
        split = [halves(part) for part in values]
        base = started(values, [turned_by(table, high, low) for high, low in split])
        highs = [high for high, _ in split]
        for index in range(count):
            place = late * count + index
            mask = jnp.where(me % 2 == flip, offsets[0][place], offsets[1][place])
            put(me ^ (flip ^ mask), targets, (values, highs, base), index, stripe)


def own_place(tp_count):
    return lax.axis_index("ta") * tp_count + lax.axis_index("tp")


def kept_shapes(tp_count, stripe, block_rows):
    pieces = (2, 2 * tp_count, stripe, block_rows)
    return [jax.ShapeDtypeStruct(pieces, each) for each in (jnp.float32, jnp.bfloat16, jnp.float32)]


def in_vmem(count):
    return [pl.BlockSpec(memory_space=pltpu.VMEM)] * count


def early_stage(masks, tp_count, stripe, block_rows, factor):
    offsets = [offsets_of(each) for each in masks]

    def kernel(*refs):
        hamiltonian, interaction, diagonal, last, table_out = refs[2:4] + refs[7:]
        me = own_place(tp_count)
        weights, table = tables_of(hamiltonian, interaction, block_rows)
        weights = jnp.concatenate([weights] * (block_rows // NO))
        diagonal[0] = weights
        diagonal[1] = inside_only(weights, 0)
        last[...] = inside_only(
            jnp.concatenate([weights] * 2), lax.axis_index("ta") * (block_rows // NO)
        )
        table_out[...] = table
        take_first(refs[:2], 0, me, offsets, stripe, table, refs[4:7])

    shapes = kept_shapes(tp_count, stripe, block_rows)
    tables = [
        jax.ShapeDtypeStruct((2, block_rows, block_rows), jnp.float32),
        jax.ShapeDtypeStruct((2 * block_rows, block_rows), jnp.float32),
        jax.ShapeDtypeStruct((3 * block_rows, block_rows), jnp.bfloat16),
    ]
    return pl.pallas_call(
        kernel,
        out_shape=shapes + tables,
        in_specs=in_vmem(4),
        out_specs=in_vmem(6),
        compiler_params=pltpu.CompilerParams(vmem_limit_bytes=16 << 20),
        name="early_stage",
    )


def first_stage(masks, tp_count, stripe, block_rows, factor):
    offsets = [offsets_of(each) for each in masks]
    scale = 0.5 * factor

    def kernel(*refs):
        weights, table = refs[2], refs[3][...]
        targets, window, squares = refs[7:10], refs[10], refs[11]
        take_first(refs[:2], 1, own_place(tp_count), offsets, stripe, table, targets)
        values, highs, bases = targets
        high = whole(highs, 0)
        made = window_of(squares_of(whole(values, 0), weights[1]), mirrored(high))
        squares[0], squares[1] = squares_of(whole(values, 1), weights[0])
        memory = products(high, made)
        window[0] = made[0]
        window[1] = made[1]
        half = (tp_count, stripe, block_rows)
        bases[0, :tp_count] = bases[0, :tp_count] + scale * memory[1].reshape(half)
        bases[1, :tp_count] = bases[1, :tp_count] - scale * memory[0].reshape(half)

    square = jax.ShapeDtypeStruct((2, 2 * block_rows, block_rows), jnp.bfloat16)
    return pl.pallas_call(
        kernel,
        out_shape=kept_shapes(tp_count, stripe, block_rows)
        + [square, jax.ShapeDtypeStruct((2, block_rows, block_rows), jnp.float32)],
        in_specs=in_vmem(7),
        out_specs=in_vmem(5),
        input_output_aliases={4: 0, 5: 1, 6: 2},
        compiler_params=pltpu.CompilerParams(vmem_limit_bytes=16 << 20),
        name="first_stage",
    )


def second_stage(masks, tp_count, stripe, block_rows, factor):
    offsets = offsets_of(masks)
    half_count = len(offsets) // 2
    order_size = 2 * block_rows
    scale = 0.5 * factor

    def kernel(*refs):
        diagonal, last_weights, table = refs[4], refs[5], refs[6][...]
        lows, bases, window, squares = refs[7:11]
        out, highs, rests, nexts, low_next = refs[11:]
        ta_place = lax.axis_index("ta")
        tp_place = lax.axis_index("tp")
        me = own_place(tp_count)
        blank = jnp.zeros((stripe, block_rows), jnp.bfloat16)
        for flip in range(2):
            for index, mask in enumerate(offsets):
                late, slot = divmod(index, half_count)
                device = me ^ (flip ^ mask)
                other = device ^ tp_count
                source = refs[2 * flip + late]
                for part in range(2):
                    highs[part, device] = source[slot, 0, part]
                    highs[part, other] = source[slot, 1, part]
                    rests[part, device] = source[slot, 2, part]
                    rests[part, other] = blank
        high = [whole(highs, block) for block in range(2)]
        rest = [whole(rests, block) for block in range(2)]
        full = [
            [high[block][k].astype(jnp.float32) + rest[block][k].astype(jnp.float32) for k in range(2)]
            for block in range(2)
        ]
        base = [
            started(full[block], [turned_by(table, high[block][k], rest[block][k]) for k in range(2)])
            for block in range(2)
        ]

        def stored(block, group, real, imag):
            for part, result in ((0, real), (1, imag)):
                nexts[part, block, group] = result
                low_next[part, group, :, block * block_rows : (block + 1) * block_rows] = (
                    result.astype(jnp.bfloat16)
                )

        stored(0, 0, *whole(bases, 0))
        memory = products(high[0], [window[0], window[1]])
        stored(0, 1, base[0][0] + scale * memory[1], base[0][1] - scale * memory[0])
        later = [
            window_of([squares[0], squares[1]], mirrored(high[0])),
            window_of(squares_of(full[1], diagonal[1]), mirrored(high[1])),
        ]
        later = [jnp.concatenate([later[0][k], later[1][k]]) for k in range(2)]
        for group in range(2):
            start = whole(bases, 1) if group == 0 else base[1]
            rows = whole(lows, 0) + whole(lows, 1) if group == 0 else high[0] + high[1]
            memory = products(rows, later)
            stored(1, group, start[0] + scale * memory[1], start[1] - scale * memory[0])

        current = [nexts[part, ta_place].reshape(order_size, block_rows) for part in range(2)]
        mirror = mirrored([low_next[part, ta_place] for part in range(2)])
        last = window_of(squares_of(current, last_weights[...]), mirror)
        row = pl.multiple_of(tp_place * stripe, stripe)
        own = [
            nexts[part, ta_place, :, pl.ds(row, stripe), :].reshape(2 * stripe, block_rows)
            for part in range(2)
        ]
        own_rounded = [
            low_next[part, :, pl.ds(row, stripe), :].reshape(2 * stripe, order_size)
            for part in range(2)
        ]
        memory = products(own_rounded, last)
        real, imag = started(own, [turned_by(table, *halves(part)) for part in own])
        shape = (2, stripe, block_rows)
        out[0] = (real + scale * memory[1]).reshape(shape)
        out[1] = (imag - scale * memory[0]).reshape(shape)

    return pl.pallas_call(
        kernel,
        out_shape=jax.ShapeDtypeStruct((2, 2, stripe, block_rows), jnp.float32),
        in_specs=in_vmem(11),
        out_specs=in_vmem(1)[0],
        scratch_shapes=[pltpu.VMEM((2, 2 * tp_count, stripe, block_rows), jnp.bfloat16)] * 2
        + [
            pltpu.VMEM((2, 2, 2, block_rows, block_rows), jnp.float32),
            pltpu.VMEM((2, 2, block_rows, order_size), jnp.bfloat16),
        ],
        compiler_params=pltpu.CompilerParams(vmem_limit_bytes=24 << 20),
        name="second_stage",
    )


def replicated(green, hamiltonian, interaction):
    tp_count = lax.axis_size("tp")
    count = 2 * tp_count
    stripe = green.shape[3]
    block_rows = green.shape[4]
    factor = 1.0 / math.sqrt(2 * block_rows)
    mask, first_masks, second_masks = exchange_masks(tp_count)

    def exchanged(block, mask):
        masks = (mask, mask) if isinstance(mask, int) else mask
        return lax.ppermute(block, ("ta", "tp"), [(i, i ^ masks[i % 2]) for i in range(count)])

    arriving = exchanged(green.reshape(-1, block_rows), mask).reshape(green.shape)
    first = jnp.stack([green[:, 0, 0], arriving[:, 0, 0]])
    second = jnp.stack([green[:, 1, 0], arriving[:, 1, 0]])
    high = lax.reduce_precision(second, 8, 7)
    second = jnp.stack([high, second - high], 1).astype(jnp.bfloat16)
    first_parts = second_parts = ()
    for first_mask, second_mask in zip(zip(*first_masks), second_masks):
        first_parts = [first, exchanged(first, first_mask)]
        first = jnp.concatenate(first_parts)
        if second_mask == tp_count:
            other_high = exchanged(second[:, 0], second_mask)[:, None]
            second = jnp.concatenate([second[:, :1], other_high, second[:, 1:]], 1)
        else:
            second_parts = [second, exchanged(second, second_mask)]
            second = jnp.concatenate(second_parts)
    first_parts += [exchanged(first_parts[0], 1)]
    first_parts += [exchanged(first_parts[1], 1)]
    second_parts += [exchanged(part, 1) for part in second_parts]
    first_masks = [[mask] + each for each in first_masks]
    second_masks = [mask] + [later for later in second_masks if later != tp_count]
    sizes = (tp_count, stripe, block_rows, factor)
    *kept, weights, last, table = early_stage(first_masks, *sizes)(
        *first_parts[::2], hamiltonian, interaction
    )
    _, *known = first_stage(first_masks, *sizes)(*first_parts[1::2], weights, table, *kept)
    result = second_stage(second_masks, *sizes)(*second_parts, weights, last, table, *known)
    return result[:, :, None]


def solution(mesh):
    in_specs = (P(None, None, "tp", None, "ta"), P(), P())
    out_specs = P(None, None, "tp", None, "ta")
    ta_count = mesh.shape["ta"]
    tp_count = mesh.shape["tp"]

    def shards(green, hamiltonian, interaction):
        whole_bytes = green.size * green.dtype.itemsize * ta_count * tp_count
        covered = ta_count == 2 and green.shape[1] == 2 and tp_count >= 16
        if covered and tp_count & (tp_count - 1) == 0 and whole_bytes <= 1 << 22:
            return replicated(green, hamiltonian, interaction)
        return windowed(green, hamiltonian, interaction)

    return jax.shard_map(shards, mesh=mesh, in_specs=in_specs, out_specs=out_specs, check_vma=False)
```

```python
import math

import jax
import jax.numpy as jnp
from jax import lax
from jax.experimental import pallas as pl
from jax.experimental.pallas import tpu as pltpu
from jax.sharding import PartitionSpec as P

NO = 32
ITERS = 2


highest = lax.Precision.HIGHEST


def shifted(block, axis, distance):
    devices = range(lax.axis_size(axis))
    route = [(i - distance, i) for i in devices if i - distance in devices]
    return lax.ppermute(block, axis, route)


def half_dot(left_side, right_side):
    return jnp.dot(left_side, right_side, preferred_element_type=jnp.float32)


def accumulate(left_side, right_side):
    product_real = half_dot(left_side[0], right_side[0]) - half_dot(left_side[1], right_side[1])
    product_imag = half_dot(left_side[0], right_side[1]) + half_dot(left_side[1], right_side[0])
    return (product_real, product_imag)


def self_energy(values, mirror_part, weights):
    real_square = values[0] * values[0] - values[1] * values[1]
    imag_square = 2.0 * values[0] * values[1]
    sigma_real = weights * (real_square * mirror_part[0] - imag_square * mirror_part[1])
    sigma_imag = weights * (real_square * mirror_part[1] + imag_square * mirror_part[0])
    return jnp.stack([sigma_real, sigma_imag])


def windowed(green, hamiltonian, interaction):
    tp_count = lax.axis_size("tp")
    ta_place = lax.axis_index("ta")
    tp_place = lax.axis_index("tp")
    groups = green.shape[1]
    stripe = green.shape[3]
    block_rows = green.shape[4]
    columns = groups * stripe
    factor = 1.0 / math.sqrt(2 * block_rows)
    current = green[:, :, 0].reshape(2, columns, block_rows)
    squared = interaction * interaction
    column_global = (
        jnp.arange(groups, dtype=jnp.int32)[:, None] * tp_count + tp_place
    ) * stripe + jnp.arange(stripe, dtype=jnp.int32)[None, :]
    column_orbital = (column_global % NO).reshape(columns)
    onehot = (column_orbital[:, None] == jnp.arange(NO, dtype=jnp.int32)[None, :]).astype(
        jnp.float32
    )
    lookup_table = jnp.dot(onehot, squared.T, precision=highest)
    coupling = jnp.tile(lookup_table, (1, block_rows // NO))
    row_time = jnp.arange(block_rows, dtype=jnp.int32) // NO
    column_time = (tp_place * stripe + jnp.arange(stripe, dtype=jnp.int32)) // NO
    is_later = column_time[:, None] > row_time[None, :]
    block_width = math.gcd(block_rows, 128)
    blocked = jnp.kron(jnp.eye(block_width // NO, dtype=jnp.float32), hamiltonian.T)
    zero_half = jnp.zeros((), jnp.bfloat16)
    for _ in range(ITERS):
        rounded = current.astype(jnp.bfloat16)
        outgoing = rounded.reshape(2, groups, stripe, tp_count, stripe)
        previous = shifted(rounded, "ta", 1)
        earliest = shifted(rounded, "ta", 2)
        hamilton_term = jnp.dot(
            current.reshape(-1, block_width), blocked, precision=highest
        ).reshape(2, columns, block_rows)
        selected = []
        nearby = jnp.stack(
            [
                lax.dynamic_index_in_dim(
                    outgoing, jnp.minimum(ta_place + step_ahead, groups - 1), 1, keepdims=False
                )
                for step_ahead in range(3)
            ],
            1,
        )
        spread = lax.all_to_all(nearby, "tp", split_axis=3, concat_axis=3, tiled=True)
        from_one = shifted(spread[:, 1], "ta", 1)
        from_two = shifted(spread[:, 2], "ta", 2)
        received = (from_two, from_one, spread[:, 0])
        by_current = current.reshape(2, groups, stripe, block_rows)
        for window_index in range(3):
            group_pick = jnp.maximum(ta_place - 2 + window_index, 0)
            own_part = lax.dynamic_index_in_dim(by_current, group_pick, 1, keepdims=False)
            flipped = (
                jnp.transpose(received[window_index], (0, 3, 2, 1))
                .reshape(2, stripe, block_rows)
                .astype(jnp.float32)
            )
            selected.append(self_energy(own_part, flipped, coupling[:stripe]))
        oldest = jnp.where(is_later[None], selected[0], 0.0)
        middle = selected[1]
        newest = jnp.where(is_later[None], 0.0, selected[2])
        sending = jnp.stack([oldest + newest, middle], 1).astype(jnp.bfloat16)[:, :, None]
        portion = lax.all_gather(sending, "tp", axis=2, tiled=True)
        row_count = portion.shape[2] * stripe
        arriving_time = jnp.arange(row_count, dtype=jnp.int32) // NO
        later_here = (arriving_time[:, None] > row_time[None, :])[None]
        merged = portion[:, 0].reshape(2, row_count, block_rows)
        recent = portion[:, 1].reshape(2, row_count, block_rows)
        right_side = jnp.concatenate(
            [
                jnp.where(later_here, merged, zero_half),
                recent,
                jnp.where(later_here, zero_half, merged),
            ],
            1,
        )
        memory = accumulate(
            jnp.concatenate([source for source in (earliest, previous, rounded)], 2), right_side
        )
        next_real = current[0] + 0.5 * (hamilton_term[1] + factor * memory[1])
        next_imag = current[1] - 0.5 * (hamilton_term[0] + factor * memory[0])
        current = jnp.stack([next_real, next_imag])
    return current.reshape(2, groups, 1, stripe, block_rows)


def exchange_masks(tp_count):
    bits = [1 << bit for bit in reversed(range(1, tp_count.bit_length() - 1))]
    middle, low, ta_bit = bits[1:-1], bits[-1:], [tp_count]
    even, odd = ta_bit + middle + low, low + middle + ta_bit
    return bits[0], (even, odd), ta_bit + low + middle


def offsets_of(masks):
    offsets = [0]
    for mask in masks:
        offsets = offsets + [known ^ mask for known in offsets]
    return offsets


def bf16_dot(left_side, right_side):
    return lax.dot_general(
        left_side, right_side, (((1,), (0,)), ((), ())), preferred_element_type=jnp.float32
    )


def halves(values):
    high = values.astype(jnp.bfloat16)
    return high, (values - high.astype(jnp.float32)).astype(jnp.bfloat16)


def squares_of(values, weights):
    real = values[0] * values[0] - values[1] * values[1]
    imag = 2.0 * values[0] * values[1]
    return real * weights, imag * weights


def window_of(squares, mirror):
    real = squares[0] * mirror[0] - squares[1] * mirror[1]
    imag = squares[0] * mirror[1] + squares[1] * mirror[0]
    real, imag = real.astype(jnp.bfloat16), imag.astype(jnp.bfloat16)
    return [jnp.concatenate([real, -imag]), jnp.concatenate([imag, real])]


def inside_only(weights, first_time):
    source_time = lax.broadcasted_iota(jnp.int32, weights.shape, 0) // NO
    target_time = lax.broadcasted_iota(jnp.int32, weights.shape, 1) // NO + first_time
    return jnp.where(source_time <= target_time, weights, 0.0)


def mirrored(rounded):
    return [jnp.transpose(part.astype(jnp.float32)) for part in rounded]


def products(left_side, right_side):
    left_side = jnp.concatenate(left_side, axis=1)
    return [bf16_dot(left_side, part) for part in right_side]


def tables_of(hamiltonian, interaction, block_rows):
    def repeated(tile):
        return jnp.concatenate([tile] * (block_rows // NO), axis=1)

    weights = repeated(jnp.transpose(interaction[...] * interaction[...]))
    table = jnp.concatenate([repeated(jnp.transpose(hamiltonian[...]))] * (block_rows // NO))
    same_time = (
        lax.broadcasted_iota(jnp.int32, table.shape, 0) // NO
        == lax.broadcasted_iota(jnp.int32, table.shape, 1) // NO
    )
    high, low = halves(jnp.where(same_time, table, 0.0))
    return weights, jnp.concatenate([high, high, low])


def turned_by(table, high, low=None):
    if low is None:
        return bf16_dot(jnp.concatenate([high, high], axis=1), table[high.shape[1] :])
    return bf16_dot(jnp.concatenate([low, high, high], axis=1), table)


def started(values, turned):
    return values[0] + 0.5 * turned[1], values[1] - 0.5 * turned[0]


def rows_of(pieces):
    return pieces.reshape(pieces.shape[0] * pieces.shape[1], pieces.shape[2])


def whole(source, block):
    tp_count, stripe, block_rows = source.shape[1] // 2, source.shape[2], source.shape[3]
    return [
        source[part, block * tp_count : (block + 1) * tp_count].reshape(
            tp_count * stripe, block_rows
        )
        for part in range(2)
    ]


def put(device, targets, results, index, stripe):
    for target, result in zip(targets, results):
        for part in range(2):
            target[part, device] = result[part][index * stripe : (index + 1) * stripe]


def take_first(sources, late, me, offsets, stripe, table, targets):
    count = len(offsets[0]) // 2
    for flip in range(2):
        values = [rows_of(sources[flip][:, part]) for part in range(2)]
        split = [halves(part) for part in values]
        base = started(values, [turned_by(table, high, low) for high, low in split])
        highs = [high for high, _ in split]
        for index in range(count):
            place = late * count + index
            mask = jnp.where(me % 2 == flip, offsets[0][place], offsets[1][place])
            put(me ^ (flip ^ mask), targets, (values, highs, base), index, stripe)


def take_second(sources, late, me, offsets, tp_count, stripe, table, targets):
    count = len(offsets) // 2
    for flip in range(2):
        for plane in range(2):
            highs = [rows_of(sources[flip][:, plane, part]) for part in range(2)]
            values = [high.astype(jnp.float32) for high in highs]
            if plane == 0:
                lows = [rows_of(sources[flip][:, 2, part]) for part in range(2)]
                values = [values[part] + lows[part].astype(jnp.float32) for part in range(2)]
                turned = [turned_by(table, highs[part], lows[part]) for part in range(2)]
            else:
                turned = [turned_by(table, high) for high in highs]
            base = started(values, turned)
            for index in range(count):
                device = me ^ (flip ^ offsets[late * count + index] ^ (plane * tp_count))
                put(device, targets, (values, highs, base), index, stripe)


def own_place(tp_count):
    return lax.axis_index("ta") * tp_count + lax.axis_index("tp")


def kept_shapes(tp_count, stripe, block_rows):
    pieces = (2, 2 * tp_count, stripe, block_rows)
    return [jax.ShapeDtypeStruct(pieces, each) for each in (jnp.float32, jnp.bfloat16, jnp.float32)]


def in_vmem(count):
    return [pl.BlockSpec(memory_space=pltpu.VMEM)] * count


def early_stage(first_masks, second_masks, tp_count, stripe, block_rows, factor):
    offsets = [offsets_of(each) for each in first_masks]
    second_offsets = offsets_of(second_masks)

    def kernel(*refs):
        hamiltonian, interaction, diagonal, last, table_out = refs[4:6] + refs[12:]
        me = own_place(tp_count)
        weights, table = tables_of(hamiltonian, interaction, block_rows)
        weights = jnp.concatenate([weights] * (block_rows // NO))
        diagonal[0] = weights
        diagonal[1] = inside_only(weights, 0)
        last[...] = inside_only(
            jnp.concatenate([weights] * 2), lax.axis_index("ta") * (block_rows // NO)
        )
        table_out[...] = table
        take_first(refs[:2], 0, me, offsets, stripe, table, refs[6:9])
        take_second(refs[2:4], 0, me, second_offsets, tp_count, stripe, table, refs[9:12])

    shapes = kept_shapes(tp_count, stripe, block_rows)
    tables = [
        jax.ShapeDtypeStruct((2, block_rows, block_rows), jnp.float32),
        jax.ShapeDtypeStruct((2 * block_rows, block_rows), jnp.float32),
        jax.ShapeDtypeStruct((3 * block_rows, block_rows), jnp.bfloat16),
    ]
    return pl.pallas_call(
        kernel,
        out_shape=shapes + shapes + tables,
        in_specs=in_vmem(6),
        out_specs=in_vmem(9),
        compiler_params=pltpu.CompilerParams(vmem_limit_bytes=16 << 20),
        name="early_stage",
    )


def first_stage(masks, tp_count, stripe, block_rows, factor):
    offsets = [offsets_of(each) for each in masks]
    scale = 0.5 * factor

    def kernel(*refs):
        weights, table = refs[2], refs[3][...]
        targets, window, squares = refs[7:10], refs[10], refs[11]
        take_first(refs[:2], 1, own_place(tp_count), offsets, stripe, table, targets)
        values, highs, bases = targets
        high = whole(highs, 0)
        made = window_of(squares_of(whole(values, 0), weights[1]), mirrored(high))
        squares[0], squares[1] = squares_of(whole(values, 1), weights[0])
        memory = products(high, made)
        window[0] = made[0]
        window[1] = made[1]
        half = (tp_count, stripe, block_rows)
        bases[0, :tp_count] = bases[0, :tp_count] + scale * memory[1].reshape(half)
        bases[1, :tp_count] = bases[1, :tp_count] - scale * memory[0].reshape(half)

    square = jax.ShapeDtypeStruct((2, 2 * block_rows, block_rows), jnp.bfloat16)
    return pl.pallas_call(
        kernel,
        out_shape=kept_shapes(tp_count, stripe, block_rows)
        + [square, jax.ShapeDtypeStruct((2, block_rows, block_rows), jnp.float32)],
        in_specs=in_vmem(7),
        out_specs=in_vmem(5),
        input_output_aliases={4: 0, 5: 1, 6: 2},
        compiler_params=pltpu.CompilerParams(vmem_limit_bytes=16 << 20),
        name="first_stage",
    )


def second_stage(masks, tp_count, stripe, block_rows, factor):
    offsets = offsets_of(masks)
    order_size = 2 * block_rows
    scale = 0.5 * factor

    def kernel(*refs):
        diagonal, last_weights, table = refs[2], refs[3], refs[4][...]
        lows, bases, window, squares = refs[5:9]
        out, targets, nexts, low_next = refs[12], refs[13:16], refs[16], refs[17]
        ta_place = lax.axis_index("ta")
        tp_place = lax.axis_index("tp")
        me = own_place(tp_count)
        take_second(refs[:2], 1, me, offsets, tp_count, stripe, table, targets)
        second_values, second_highs, second_bases = targets
        high = [whole(second_highs, block) for block in range(2)]

        def stored(block, group, real, imag):
            for part, result in ((0, real), (1, imag)):
                nexts[part, block, group] = result
                low_next[part, group, :, block * block_rows : (block + 1) * block_rows] = (
                    result.astype(jnp.bfloat16)
                )

        stored(0, 0, *whole(bases, 0))
        memory = products(high[0], [window[0], window[1]])
        start = whole(second_bases, 0)
        stored(0, 1, start[0] + scale * memory[1], start[1] - scale * memory[0])
        later = [
            window_of([squares[0], squares[1]], mirrored(high[0])),
            window_of(squares_of(whole(second_values, 1), diagonal[1]), mirrored(high[1])),
        ]
        later = [jnp.concatenate([later[0][k], later[1][k]]) for k in range(2)]
        for group in range(2):
            start = whole(bases if group == 0 else second_bases, 1)
            rows = whole(lows, 0) + whole(lows, 1) if group == 0 else high[0] + high[1]
            memory = products(rows, later)
            stored(1, group, start[0] + scale * memory[1], start[1] - scale * memory[0])

        current = [nexts[part, ta_place].reshape(order_size, block_rows) for part in range(2)]
        mirror = mirrored([low_next[part, ta_place] for part in range(2)])
        last = window_of(squares_of(current, last_weights[...]), mirror)
        row = pl.multiple_of(tp_place * stripe, stripe)
        own = [
            nexts[part, ta_place, :, pl.ds(row, stripe), :].reshape(2 * stripe, block_rows)
            for part in range(2)
        ]
        own_rounded = [
            low_next[part, :, pl.ds(row, stripe), :].reshape(2 * stripe, order_size)
            for part in range(2)
        ]
        memory = products(own_rounded, last)
        real, imag = started(own, [turned_by(table, *halves(part)) for part in own])
        shape = (2, stripe, block_rows)
        out[0] = (real + scale * memory[1]).reshape(shape)
        out[1] = (imag - scale * memory[0]).reshape(shape)

    return pl.pallas_call(
        kernel,
        out_shape=[jax.ShapeDtypeStruct((2, 2, stripe, block_rows), jnp.float32)]
        + kept_shapes(tp_count, stripe, block_rows),
        in_specs=in_vmem(12),
        out_specs=in_vmem(4),
        input_output_aliases={9: 1, 10: 2, 11: 3},
        scratch_shapes=[
            pltpu.VMEM((2, 2, 2, block_rows, block_rows), jnp.float32),
            pltpu.VMEM((2, 2, block_rows, order_size), jnp.bfloat16),
        ],
        compiler_params=pltpu.CompilerParams(vmem_limit_bytes=24 << 20),
        name="second_stage",
    )


def replicated(green, hamiltonian, interaction):
    tp_count = lax.axis_size("tp")
    count = 2 * tp_count
    stripe = green.shape[3]
    block_rows = green.shape[4]
    factor = 1.0 / math.sqrt(2 * block_rows)
    mask, first_masks, second_masks = exchange_masks(tp_count)

    def exchanged(block, mask):
        masks = (mask, mask) if isinstance(mask, int) else mask
        return lax.ppermute(block, ("ta", "tp"), [(i, i ^ masks[i % 2]) for i in range(count)])

    arriving = exchanged(green.reshape(-1, block_rows), mask).reshape(green.shape)
    first = jnp.stack([green[:, 0, 0], arriving[:, 0, 0]])
    second = jnp.stack([green[:, 1, 0], arriving[:, 1, 0]])
    high = lax.reduce_precision(second, 8, 7)
    second = jnp.stack([high, second - high], 1).astype(jnp.bfloat16)
    first_parts = second_parts = ()
    for first_mask, second_mask in zip(zip(*first_masks), second_masks):
        first_parts = [first, exchanged(first, first_mask)]
        first = jnp.concatenate(first_parts)
        if second_mask == tp_count:
            other_high = exchanged(second[:, 0], second_mask)[:, None]
            second = jnp.concatenate([second[:, :1], other_high, second[:, 1:]], 1)
        else:
            second_parts = [second, exchanged(second, second_mask)]
            second = jnp.concatenate(second_parts)
    first_parts += [exchanged(first_parts[0], 1)]
    first_parts += [exchanged(first_parts[1], 1)]
    second_parts += [exchanged(second_parts[0], 1)]
    second_parts += [exchanged(second_parts[1], 1)]
    first_masks = [[mask] + each for each in first_masks]
    second_masks = [mask] + [later for later in second_masks if later != tp_count]
    sizes = (tp_count, stripe, block_rows, factor)
    *kept, weights, last, table = early_stage(first_masks, second_masks, *sizes)(
        *first_parts[::2], *second_parts[::2], hamiltonian, interaction
    )
    _, *known = first_stage(first_masks, *sizes)(*first_parts[1::2], weights, table, *kept[:3])
    result = second_stage(second_masks, *sizes)(
        *second_parts[1::2], weights, last, table, *known, *kept[3:]
    )
    return result[0][:, :, None]


def solution(mesh):
    in_specs = (P(None, None, "tp", None, "ta"), P(), P())
    out_specs = P(None, None, "tp", None, "ta")
    ta_count = mesh.shape["ta"]
    tp_count = mesh.shape["tp"]

    def shards(green, hamiltonian, interaction):
        whole_bytes = green.size * green.dtype.itemsize * ta_count * tp_count
        covered = ta_count == 2 and green.shape[1] == 2 and tp_count >= 16
        if covered and tp_count & (tp_count - 1) == 0 and whole_bytes <= 1 << 22:
            return replicated(green, hamiltonian, interaction)
        return windowed(green, hamiltonian, interaction)

    return jax.shard_map(shards, mesh=mesh, in_specs=in_specs, out_specs=out_specs, check_vma=False)
```

```python
import math

import jax
import jax.numpy as jnp
from jax import lax
from jax.experimental import pallas as pl
from jax.experimental.pallas import tpu as pltpu
from jax.sharding import PartitionSpec as P

NO = 32
ITERS = 2


highest = lax.Precision.HIGHEST


def shifted(block, axis, distance):
    devices = range(lax.axis_size(axis))
    route = [(i - distance, i) for i in devices if i - distance in devices]
    return lax.ppermute(block, axis, route)


def half_dot(left_side, right_side):
    return jnp.dot(left_side, right_side, preferred_element_type=jnp.float32)


def accumulate(left_side, right_side):
    product_real = half_dot(left_side[0], right_side[0]) - half_dot(left_side[1], right_side[1])
    product_imag = half_dot(left_side[0], right_side[1]) + half_dot(left_side[1], right_side[0])
    return (product_real, product_imag)


def self_energy(values, mirror_part, weights):
    real_square = values[0] * values[0] - values[1] * values[1]
    imag_square = 2.0 * values[0] * values[1]
    sigma_real = weights * (real_square * mirror_part[0] - imag_square * mirror_part[1])
    sigma_imag = weights * (real_square * mirror_part[1] + imag_square * mirror_part[0])
    return jnp.stack([sigma_real, sigma_imag])


def windowed(green, hamiltonian, interaction):
    tp_count = lax.axis_size("tp")
    ta_place = lax.axis_index("ta")
    tp_place = lax.axis_index("tp")
    groups = green.shape[1]
    stripe = green.shape[3]
    block_rows = green.shape[4]
    columns = groups * stripe
    factor = 1.0 / math.sqrt(2 * block_rows)
    current = green[:, :, 0].reshape(2, columns, block_rows)
    squared = interaction * interaction
    column_global = (
        jnp.arange(groups, dtype=jnp.int32)[:, None] * tp_count + tp_place
    ) * stripe + jnp.arange(stripe, dtype=jnp.int32)[None, :]
    column_orbital = (column_global % NO).reshape(columns)
    onehot = (column_orbital[:, None] == jnp.arange(NO, dtype=jnp.int32)[None, :]).astype(
        jnp.float32
    )
    lookup_table = jnp.dot(onehot, squared.T, precision=highest)
    coupling = jnp.tile(lookup_table, (1, block_rows // NO))
    row_time = jnp.arange(block_rows, dtype=jnp.int32) // NO
    column_time = (tp_place * stripe + jnp.arange(stripe, dtype=jnp.int32)) // NO
    is_later = column_time[:, None] > row_time[None, :]
    block_width = math.gcd(block_rows, 128)
    blocked = jnp.kron(jnp.eye(block_width // NO, dtype=jnp.float32), hamiltonian.T)
    zero_half = jnp.zeros((), jnp.bfloat16)
    for _ in range(ITERS):
        rounded = current.astype(jnp.bfloat16)
        outgoing = rounded.reshape(2, groups, stripe, tp_count, stripe)
        previous = shifted(rounded, "ta", 1)
        earliest = shifted(rounded, "ta", 2)
        hamilton_term = jnp.dot(
            current.reshape(-1, block_width), blocked, precision=highest
        ).reshape(2, columns, block_rows)
        selected = []
        nearby = jnp.stack(
            [
                lax.dynamic_index_in_dim(
                    outgoing, jnp.minimum(ta_place + step_ahead, groups - 1), 1, keepdims=False
                )
                for step_ahead in range(3)
            ],
            1,
        )
        spread = lax.all_to_all(nearby, "tp", split_axis=3, concat_axis=3, tiled=True)
        from_one = shifted(spread[:, 1], "ta", 1)
        from_two = shifted(spread[:, 2], "ta", 2)
        received = (from_two, from_one, spread[:, 0])
        by_current = current.reshape(2, groups, stripe, block_rows)
        for window_index in range(3):
            group_pick = jnp.maximum(ta_place - 2 + window_index, 0)
            own_part = lax.dynamic_index_in_dim(by_current, group_pick, 1, keepdims=False)
            flipped = (
                jnp.transpose(received[window_index], (0, 3, 2, 1))
                .reshape(2, stripe, block_rows)
                .astype(jnp.float32)
            )
            selected.append(self_energy(own_part, flipped, coupling[:stripe]))
        oldest = jnp.where(is_later[None], selected[0], 0.0)
        middle = selected[1]
        newest = jnp.where(is_later[None], 0.0, selected[2])
        sending = jnp.stack([oldest + newest, middle], 1).astype(jnp.bfloat16)[:, :, None]
        portion = lax.all_gather(sending, "tp", axis=2, tiled=True)
        row_count = portion.shape[2] * stripe
        arriving_time = jnp.arange(row_count, dtype=jnp.int32) // NO
        later_here = (arriving_time[:, None] > row_time[None, :])[None]
        merged = portion[:, 0].reshape(2, row_count, block_rows)
        recent = portion[:, 1].reshape(2, row_count, block_rows)
        right_side = jnp.concatenate(
            [
                jnp.where(later_here, merged, zero_half),
                recent,
                jnp.where(later_here, zero_half, merged),
            ],
            1,
        )
        memory = accumulate(
            jnp.concatenate([source for source in (earliest, previous, rounded)], 2), right_side
        )
        next_real = current[0] + 0.5 * (hamilton_term[1] + factor * memory[1])
        next_imag = current[1] - 0.5 * (hamilton_term[0] + factor * memory[0])
        current = jnp.stack([next_real, next_imag])
    return current.reshape(2, groups, 1, stripe, block_rows)


def exchange_masks(tp_count):
    bits = [1 << bit for bit in reversed(range(1, tp_count.bit_length() - 1))]
    middle, low, ta_bit = bits[1:-1], bits[-1:], [tp_count]
    even, odd = ta_bit + middle + low, low + middle + ta_bit
    return bits[0], (even, odd), ta_bit + low + middle


def offsets_of(masks):
    offsets = [0]
    for mask in masks:
        offsets = offsets + [known ^ mask for known in offsets]
    return offsets


def bf16_dot(left_side, right_side):
    return lax.dot_general(
        left_side, right_side, (((1,), (0,)), ((), ())), preferred_element_type=jnp.float32
    )


def halves(values):
    high = values.astype(jnp.bfloat16)
    return high, (values - high.astype(jnp.float32)).astype(jnp.bfloat16)


def squares_of(values, weights):
    real = values[0] * values[0] - values[1] * values[1]
    imag = 2.0 * values[0] * values[1]
    return real * weights, imag * weights


def window_of(squares, mirror):
    real = squares[0] * mirror[0] - squares[1] * mirror[1]
    imag = squares[0] * mirror[1] + squares[1] * mirror[0]
    real, imag = real.astype(jnp.bfloat16), imag.astype(jnp.bfloat16)
    return [jnp.concatenate([real, -imag]), jnp.concatenate([imag, real])]


def inside_only(weights, first_time):
    source_time = lax.broadcasted_iota(jnp.int32, weights.shape, 0) // NO
    target_time = lax.broadcasted_iota(jnp.int32, weights.shape, 1) // NO + first_time
    return jnp.where(source_time <= target_time, weights, 0.0)


def mirrored(rounded):
    return [jnp.transpose(part.astype(jnp.float32)) for part in rounded]


def products(left_side, right_side):
    left_side = jnp.concatenate(left_side, axis=1)
    return [bf16_dot(left_side, part) for part in right_side]


def tables_of(hamiltonian, interaction, block_rows):
    def repeated(tile):
        return jnp.concatenate([tile] * (block_rows // NO), axis=1)

    weights = repeated(jnp.transpose(interaction[...] * interaction[...]))
    table = jnp.concatenate([repeated(jnp.transpose(hamiltonian[...]))] * (block_rows // NO))
    same_time = (
        lax.broadcasted_iota(jnp.int32, table.shape, 0) // NO
        == lax.broadcasted_iota(jnp.int32, table.shape, 1) // NO
    )
    high, low = halves(jnp.where(same_time, table, 0.0))
    return weights, jnp.concatenate([high, high, low])


def turned_by(table, high, low=None):
    if low is None:
        return bf16_dot(jnp.concatenate([high, high], axis=1), table[high.shape[1] :])
    return bf16_dot(jnp.concatenate([low, high, high], axis=1), table)


def started(values, turned):
    return values[0] + 0.5 * turned[1], values[1] - 0.5 * turned[0]


def rows_of(pieces):
    return pieces.reshape(pieces.shape[0] * pieces.shape[1], pieces.shape[2])


def whole(source, block):
    tp_count, stripe, block_rows = source.shape[1] // 2, source.shape[2], source.shape[3]
    return [
        source[part, block * tp_count : (block + 1) * tp_count].reshape(
            tp_count * stripe, block_rows
        )
        for part in range(2)
    ]


def put(device, targets, results, index, stripe):
    for target, result in zip(targets, results):
        for part in range(2):
            target[part, device] = result[part][index * stripe : (index + 1) * stripe]


def take_first(sources, late, me, offsets, stripe, table, targets):
    count = len(offsets[0]) // 2
    for flip in range(2):
        values = [rows_of(sources[flip][:, part]) for part in range(2)]
        split = [halves(part) for part in values]
        base = started(values, [turned_by(table, high, low) for high, low in split])
        highs = [high for high, _ in split]
        for index in range(count):
            place = late * count + index
            mask = jnp.where(me % 2 == flip, offsets[0][place], offsets[1][place])
            put(me ^ (flip ^ mask), targets, (values, highs, base), index, stripe)


def take_second(sources, late, me, offsets, tp_count, stripe, table, targets):
    count = len(offsets) // 2
    for flip, (source, low_source, low_plane) in enumerate(sources):
        for plane in range(2):
            highs = [rows_of(source[:, plane, part]) for part in range(2)]
            values = [high.astype(jnp.float32) for high in highs]
            if plane == 0:
                lows = [rows_of(low_source[:, low_plane, part]) for part in range(2)]
                values = [values[part] + lows[part].astype(jnp.float32) for part in range(2)]
                turned = [turned_by(table, highs[part], lows[part]) for part in range(2)]
            else:
                turned = [turned_by(table, high) for high in highs]
            base = started(values, turned)
            for index in range(count):
                device = me ^ (flip ^ offsets[late * count + index] ^ (plane * tp_count))
                put(device, targets, (values, highs, base), index, stripe)


def own_place(tp_count):
    return lax.axis_index("ta") * tp_count + lax.axis_index("tp")


def kept_shapes(tp_count, stripe, block_rows):
    pieces = (2, 2 * tp_count, stripe, block_rows)
    return [jax.ShapeDtypeStruct(pieces, each) for each in (jnp.float32, jnp.bfloat16, jnp.float32)]


def in_vmem(count):
    return [pl.BlockSpec(memory_space=pltpu.VMEM)] * count


def early_stage(first_masks, second_masks, tp_count, stripe, block_rows, factor):
    offsets = [offsets_of(each) for each in first_masks]
    second_offsets = offsets_of(second_masks)

    def kernel(*refs):
        hamiltonian, interaction, diagonal, last, table_out = refs[4:6] + refs[12:]
        me = own_place(tp_count)
        weights, table = tables_of(hamiltonian, interaction, block_rows)
        weights = jnp.concatenate([weights] * (block_rows // NO))
        diagonal[0] = weights
        diagonal[1] = inside_only(weights, 0)
        last[...] = inside_only(
            jnp.concatenate([weights] * 2), lax.axis_index("ta") * (block_rows // NO)
        )
        table_out[...] = table
        take_first(refs[:2], 0, me, offsets, stripe, table, refs[6:9])
        pieces = [(source, source, 2) for source in refs[2:4]]
        take_second(pieces, 0, me, second_offsets, tp_count, stripe, table, refs[9:12])

    shapes = kept_shapes(tp_count, stripe, block_rows)
    tables = [
        jax.ShapeDtypeStruct((2, block_rows, block_rows), jnp.float32),
        jax.ShapeDtypeStruct((2 * block_rows, block_rows), jnp.float32),
        jax.ShapeDtypeStruct((3 * block_rows, block_rows), jnp.bfloat16),
    ]
    return pl.pallas_call(
        kernel,
        out_shape=shapes + shapes + tables,
        in_specs=in_vmem(6),
        out_specs=in_vmem(9),
        compiler_params=pltpu.CompilerParams(vmem_limit_bytes=16 << 20),
        name="early_stage",
    )


def first_stage(masks, tp_count, stripe, block_rows, factor):
    offsets = [offsets_of(each) for each in masks]
    scale = 0.5 * factor

    def kernel(*refs):
        weights, table = refs[2], refs[3][...]
        targets, window, squares = refs[7:10], refs[10], refs[11]
        take_first(refs[:2], 1, own_place(tp_count), offsets, stripe, table, targets)
        values, highs, bases = targets
        high = whole(highs, 0)
        made = window_of(squares_of(whole(values, 0), weights[1]), mirrored(high))
        squares[0], squares[1] = squares_of(whole(values, 1), weights[0])
        memory = products(high, made)
        window[0] = made[0]
        window[1] = made[1]
        half = (tp_count, stripe, block_rows)
        bases[0, :tp_count] = bases[0, :tp_count] + scale * memory[1].reshape(half)
        bases[1, :tp_count] = bases[1, :tp_count] - scale * memory[0].reshape(half)

    square = jax.ShapeDtypeStruct((2, 2 * block_rows, block_rows), jnp.bfloat16)
    return pl.pallas_call(
        kernel,
        out_shape=kept_shapes(tp_count, stripe, block_rows)
        + [square, jax.ShapeDtypeStruct((2, block_rows, block_rows), jnp.float32)],
        in_specs=in_vmem(7),
        out_specs=in_vmem(5),
        input_output_aliases={4: 0, 5: 1, 6: 2},
        compiler_params=pltpu.CompilerParams(vmem_limit_bytes=16 << 20),
        name="first_stage",
    )


def second_stage(masks, tp_count, stripe, block_rows, factor):
    offsets = offsets_of(masks)
    order_size = 2 * block_rows
    scale = 0.5 * factor

    def kernel(*refs):
        diagonal, last_weights, table = refs[4], refs[5], refs[6][...]
        lows, bases, window, squares = refs[7:11]
        out, targets, nexts, low_next = refs[14], refs[15:18], refs[18], refs[19]
        ta_place = lax.axis_index("ta")
        tp_place = lax.axis_index("tp")
        me = own_place(tp_count)
        pieces = [(refs[0], refs[1], 0), (refs[2], refs[3], 0)]
        take_second(pieces, 1, me, offsets, tp_count, stripe, table, targets)
        second_values, second_highs, second_bases = targets
        high = [whole(second_highs, block) for block in range(2)]

        def stored(block, group, real, imag):
            for part, result in ((0, real), (1, imag)):
                nexts[part, block, group] = result
                low_next[part, group, :, block * block_rows : (block + 1) * block_rows] = (
                    result.astype(jnp.bfloat16)
                )

        stored(0, 0, *whole(bases, 0))
        memory = products(high[0], [window[0], window[1]])
        start = whole(second_bases, 0)
        stored(0, 1, start[0] + scale * memory[1], start[1] - scale * memory[0])
        later = [
            window_of([squares[0], squares[1]], mirrored(high[0])),
            window_of(squares_of(whole(second_values, 1), diagonal[1]), mirrored(high[1])),
        ]
        later = [jnp.concatenate([later[0][k], later[1][k]]) for k in range(2)]
        for group in range(2):
            start = whole(bases if group == 0 else second_bases, 1)
            rows = whole(lows, 0) + whole(lows, 1) if group == 0 else high[0] + high[1]
            memory = products(rows, later)
            stored(1, group, start[0] + scale * memory[1], start[1] - scale * memory[0])

        current = [nexts[part, ta_place].reshape(order_size, block_rows) for part in range(2)]
        mirror = mirrored([low_next[part, ta_place] for part in range(2)])
        last = window_of(squares_of(current, last_weights[...]), mirror)
        row = pl.multiple_of(tp_place * stripe, stripe)
        own = [
            nexts[part, ta_place, :, pl.ds(row, stripe), :].reshape(2 * stripe, block_rows)
            for part in range(2)
        ]
        own_rounded = [
            low_next[part, :, pl.ds(row, stripe), :].reshape(2 * stripe, order_size)
            for part in range(2)
        ]
        memory = products(own_rounded, last)
        real, imag = started(own, [turned_by(table, *halves(part)) for part in own])
        shape = (2, stripe, block_rows)
        out[0] = (real + scale * memory[1]).reshape(shape)
        out[1] = (imag - scale * memory[0]).reshape(shape)

    return pl.pallas_call(
        kernel,
        out_shape=[jax.ShapeDtypeStruct((2, 2, stripe, block_rows), jnp.float32)]
        + kept_shapes(tp_count, stripe, block_rows),
        in_specs=in_vmem(14),
        out_specs=in_vmem(4),
        input_output_aliases={11: 1, 12: 2, 13: 3},
        scratch_shapes=[
            pltpu.VMEM((2, 2, 2, block_rows, block_rows), jnp.float32),
            pltpu.VMEM((2, 2, block_rows, order_size), jnp.bfloat16),
        ],
        compiler_params=pltpu.CompilerParams(vmem_limit_bytes=24 << 20),
        name="second_stage",
    )


def replicated(green, hamiltonian, interaction):
    tp_count = lax.axis_size("tp")
    count = 2 * tp_count
    stripe = green.shape[3]
    block_rows = green.shape[4]
    factor = 1.0 / math.sqrt(2 * block_rows)
    mask, first_masks, second_masks = exchange_masks(tp_count)

    def exchanged(block, mask):
        masks = (mask, mask) if isinstance(mask, int) else mask
        return lax.ppermute(block, ("ta", "tp"), [(i, i ^ masks[i % 2]) for i in range(count)])

    arriving = exchanged(green.reshape(-1, block_rows), mask).reshape(green.shape)
    first = jnp.stack([green[:, 0, 0], arriving[:, 0, 0]])
    second = jnp.stack([green[:, 1, 0], arriving[:, 1, 0]])
    high = lax.reduce_precision(second, 8, 7)
    second = jnp.stack([high, second - high], 1).astype(jnp.bfloat16)
    first_parts = second_parts = ()
    steps = len(second_masks)
    for step, (first_mask, second_mask) in enumerate(zip(zip(*first_masks), second_masks)):
        first_parts = [first, exchanged(first, first_mask)]
        first = jnp.concatenate(first_parts)
        if second_mask == tp_count:
            other_high = exchanged(second[:, 0], second_mask)[:, None]
            second = jnp.concatenate([second[:, :1], other_high, second[:, 1:]], 1)
        else:
            pieces = [second] if step + 1 < steps else [second[:, :2], second[:, 2:]]
            second_parts = [second, exchanged(pieces[0], second_mask)]
            if step + 1 == steps:
                second_parts.append(exchanged(pieces[1], second_mask))
            else:
                second = jnp.concatenate(second_parts)
    first_parts += [exchanged(first_parts[0], 1)]
    first_parts += [exchanged(first_parts[1], 1)]
    early_swapped = exchanged(second_parts[0], 1)
    late_swapped = [exchanged(part, 1) for part in second_parts[1:]]
    first_masks = [[mask] + each for each in first_masks]
    second_masks = [mask] + [later for later in second_masks if later != tp_count]
    sizes = (tp_count, stripe, block_rows, factor)
    *kept, weights, last, table = early_stage(first_masks, second_masks, *sizes)(
        *first_parts[::2], second_parts[0], early_swapped, hamiltonian, interaction
    )
    _, *known = first_stage(first_masks, *sizes)(*first_parts[1::2], weights, table, *kept[:3])
    result = second_stage(second_masks, *sizes)(
        *second_parts[1:], *late_swapped, weights, last, table, *known, *kept[3:]
    )
    return result[0][:, :, None]


def solution(mesh):
    in_specs = (P(None, None, "tp", None, "ta"), P(), P())
    out_specs = P(None, None, "tp", None, "ta")
    ta_count = mesh.shape["ta"]
    tp_count = mesh.shape["tp"]

    def shards(green, hamiltonian, interaction):
        whole_bytes = green.size * green.dtype.itemsize * ta_count * tp_count
        covered = ta_count == 2 and green.shape[1] == 2 and tp_count >= 16
        if covered and tp_count & (tp_count - 1) == 0 and whole_bytes <= 1 << 22:
            return replicated(green, hamiltonian, interaction)
        return windowed(green, hamiltonian, interaction)

    return jax.shard_map(shards, mesh=mesh, in_specs=in_specs, out_specs=out_specs, check_vma=False)
```

```python
import math

import jax
import jax.numpy as jnp
from jax import lax
from jax.experimental import pallas as pl
from jax.experimental.pallas import tpu as pltpu
from jax.sharding import PartitionSpec as P

NO = 32
ITERS = 2


highest = lax.Precision.HIGHEST


def shifted(block, axis, distance):
    devices = range(lax.axis_size(axis))
    route = [(i - distance, i) for i in devices if i - distance in devices]
    return lax.ppermute(block, axis, route)


def half_dot(left_side, right_side):
    return jnp.dot(left_side, right_side, preferred_element_type=jnp.float32)


def accumulate(left_side, right_side):
    product_real = half_dot(left_side[0], right_side[0]) - half_dot(left_side[1], right_side[1])
    product_imag = half_dot(left_side[0], right_side[1]) + half_dot(left_side[1], right_side[0])
    return (product_real, product_imag)


def self_energy(values, mirror_part, weights):
    real_square = values[0] * values[0] - values[1] * values[1]
    imag_square = 2.0 * values[0] * values[1]
    sigma_real = weights * (real_square * mirror_part[0] - imag_square * mirror_part[1])
    sigma_imag = weights * (real_square * mirror_part[1] + imag_square * mirror_part[0])
    return jnp.stack([sigma_real, sigma_imag])


def windowed(green, hamiltonian, interaction):
    tp_count = lax.axis_size("tp")
    ta_place = lax.axis_index("ta")
    tp_place = lax.axis_index("tp")
    groups = green.shape[1]
    stripe = green.shape[3]
    block_rows = green.shape[4]
    columns = groups * stripe
    factor = 1.0 / math.sqrt(2 * block_rows)
    current = green[:, :, 0].reshape(2, columns, block_rows)
    squared = interaction * interaction
    column_global = (
        jnp.arange(groups, dtype=jnp.int32)[:, None] * tp_count + tp_place
    ) * stripe + jnp.arange(stripe, dtype=jnp.int32)[None, :]
    column_orbital = (column_global % NO).reshape(columns)
    onehot = (column_orbital[:, None] == jnp.arange(NO, dtype=jnp.int32)[None, :]).astype(
        jnp.float32
    )
    lookup_table = jnp.dot(onehot, squared.T, precision=highest)
    coupling = jnp.tile(lookup_table, (1, block_rows // NO))
    row_time = jnp.arange(block_rows, dtype=jnp.int32) // NO
    column_time = (tp_place * stripe + jnp.arange(stripe, dtype=jnp.int32)) // NO
    is_later = column_time[:, None] > row_time[None, :]
    block_width = math.gcd(block_rows, 128)
    blocked = jnp.kron(jnp.eye(block_width // NO, dtype=jnp.float32), hamiltonian.T)
    zero_half = jnp.zeros((), jnp.bfloat16)
    for _ in range(ITERS):
        rounded = current.astype(jnp.bfloat16)
        outgoing = rounded.reshape(2, groups, stripe, tp_count, stripe)
        previous = shifted(rounded, "ta", 1)
        earliest = shifted(rounded, "ta", 2)
        hamilton_term = jnp.dot(
            current.reshape(-1, block_width), blocked, precision=highest
        ).reshape(2, columns, block_rows)
        selected = []
        nearby = jnp.stack(
            [
                lax.dynamic_index_in_dim(
                    outgoing, jnp.minimum(ta_place + step_ahead, groups - 1), 1, keepdims=False
                )
                for step_ahead in range(3)
            ],
            1,
        )
        spread = lax.all_to_all(nearby, "tp", split_axis=3, concat_axis=3, tiled=True)
        from_one = shifted(spread[:, 1], "ta", 1)
        from_two = shifted(spread[:, 2], "ta", 2)
        received = (from_two, from_one, spread[:, 0])
        by_current = current.reshape(2, groups, stripe, block_rows)
        for window_index in range(3):
            group_pick = jnp.maximum(ta_place - 2 + window_index, 0)
            own_part = lax.dynamic_index_in_dim(by_current, group_pick, 1, keepdims=False)
            flipped = (
                jnp.transpose(received[window_index], (0, 3, 2, 1))
                .reshape(2, stripe, block_rows)
                .astype(jnp.float32)
            )
            selected.append(self_energy(own_part, flipped, coupling[:stripe]))
        oldest = jnp.where(is_later[None], selected[0], 0.0)
        middle = selected[1]
        newest = jnp.where(is_later[None], 0.0, selected[2])
        sending = jnp.stack([oldest + newest, middle], 1).astype(jnp.bfloat16)[:, :, None]
        portion = lax.all_gather(sending, "tp", axis=2, tiled=True)
        row_count = portion.shape[2] * stripe
        arriving_time = jnp.arange(row_count, dtype=jnp.int32) // NO
        later_here = (arriving_time[:, None] > row_time[None, :])[None]
        merged = portion[:, 0].reshape(2, row_count, block_rows)
        recent = portion[:, 1].reshape(2, row_count, block_rows)
        right_side = jnp.concatenate(
            [
                jnp.where(later_here, merged, zero_half),
                recent,
                jnp.where(later_here, zero_half, merged),
            ],
            1,
        )
        memory = accumulate(
            jnp.concatenate([source for source in (earliest, previous, rounded)], 2), right_side
        )
        next_real = current[0] + 0.5 * (hamilton_term[1] + factor * memory[1])
        next_imag = current[1] - 0.5 * (hamilton_term[0] + factor * memory[0])
        current = jnp.stack([next_real, next_imag])
    return current.reshape(2, groups, 1, stripe, block_rows)


def exchange_masks(tp_count):
    bits = [1 << bit for bit in reversed(range(1, tp_count.bit_length() - 1))]
    middle, low, ta_bit = bits[1:-1], bits[-1:], [tp_count]
    even, odd = ta_bit + middle + low, low + middle + ta_bit
    return bits[0], (even, odd), ta_bit + low + middle


def offsets_of(masks):
    offsets = [0]
    for mask in masks:
        offsets = offsets + [known ^ mask for known in offsets]
    return offsets


def bf16_dot(left_side, right_side):
    return lax.dot_general(
        left_side, right_side, (((1,), (0,)), ((), ())), preferred_element_type=jnp.float32
    )


def halves(values):
    high = values.astype(jnp.bfloat16)
    return high, (values - high.astype(jnp.float32)).astype(jnp.bfloat16)


def squares_of(values, weights):
    real = values[0] * values[0] - values[1] * values[1]
    imag = 2.0 * values[0] * values[1]
    return real * weights, imag * weights


def window_of(squares, mirror):
    real = squares[0] * mirror[0] - squares[1] * mirror[1]
    imag = squares[0] * mirror[1] + squares[1] * mirror[0]
    real, imag = real.astype(jnp.bfloat16), imag.astype(jnp.bfloat16)
    return [jnp.concatenate([real, -imag]), jnp.concatenate([imag, real])]


def inside_only(weights, first_time):
    source_time = lax.broadcasted_iota(jnp.int32, weights.shape, 0) // NO
    target_time = lax.broadcasted_iota(jnp.int32, weights.shape, 1) // NO + first_time
    return jnp.where(source_time <= target_time, weights, 0.0)


def mirrored(rounded):
    return [jnp.transpose(part.astype(jnp.float32)) for part in rounded]


def products(left_side, right_side):
    left_side = jnp.concatenate(left_side, axis=1)
    return [bf16_dot(left_side, part) for part in right_side]


def tables_of(hamiltonian, interaction, block_rows):
    def repeated(tile):
        return jnp.concatenate([tile] * (block_rows // NO), axis=1)

    weights = repeated(jnp.transpose(interaction[...] * interaction[...]))
    table = jnp.concatenate([repeated(jnp.transpose(hamiltonian[...]))] * (block_rows // NO))
    same_time = (
        lax.broadcasted_iota(jnp.int32, table.shape, 0) // NO
        == lax.broadcasted_iota(jnp.int32, table.shape, 1) // NO
    )
    high, low = halves(jnp.where(same_time, table, 0.0))
    return weights, jnp.concatenate([high, high, low])


def turned_by(table, high, low=None):
    if low is None:
        return bf16_dot(jnp.concatenate([high, high], axis=1), table[high.shape[1] :])
    return bf16_dot(jnp.concatenate([low, high, high], axis=1), table)


def started(values, turned):
    return values[0] + 0.5 * turned[1], values[1] - 0.5 * turned[0]


def rows_of(pieces):
    return pieces.reshape(pieces.shape[0] * pieces.shape[1], pieces.shape[2])


def whole(source, block):
    tp_count, stripe, block_rows = source.shape[1] // 2, source.shape[2], source.shape[3]
    return [
        source[part, block * tp_count : (block + 1) * tp_count].reshape(
            tp_count * stripe, block_rows
        )
        for part in range(2)
    ]


def put(device, targets, results, index, stripe):
    for target, result in zip(targets, results):
        for part in range(2):
            target[part, device] = result[part][index * stripe : (index + 1) * stripe]


def take_first(sources, late, me, offsets, stripe, table, targets):
    count = len(offsets[0]) // 2
    for flip in range(2):
        values = [rows_of(sources[flip][:, part]) for part in range(2)]
        split = [halves(part) for part in values]
        base = started(values, [turned_by(table, high, low) for high, low in split])
        highs = [high for high, _ in split]
        for index in range(count):
            place = late * count + index
            mask = jnp.where(me % 2 == flip, offsets[0][place], offsets[1][place])
            put(me ^ (flip ^ mask), targets, (values, highs, base), index, stripe)


def take_second(sources, late, me, offsets, tp_count, stripe, table, targets):
    count = len(offsets) // 2
    for flip, source in sources:
        for plane in range(2):
            highs = [rows_of(source[:, plane, part]) for part in range(2)]
            values = [high.astype(jnp.float32) for high in highs]
            if plane == 0:
                lows = [rows_of(source[:, 2, part]) for part in range(2)]
                values = [values[part] + lows[part].astype(jnp.float32) for part in range(2)]
                turned = [turned_by(table, highs[part], lows[part]) for part in range(2)]
            else:
                turned = [turned_by(table, high) for high in highs]
            base = started(values, turned)
            for index in range(count):
                device = me ^ (flip ^ offsets[late * count + index] ^ (plane * tp_count))
                put(device, targets, (values, highs, base), index, stripe)


def own_place(tp_count):
    return lax.axis_index("ta") * tp_count + lax.axis_index("tp")


def kept_shapes(tp_count, stripe, block_rows):
    pieces = (2, 2 * tp_count, stripe, block_rows)
    return [jax.ShapeDtypeStruct(pieces, each) for each in (jnp.float32, jnp.bfloat16, jnp.float32)]


def in_vmem(count):
    return [pl.BlockSpec(memory_space=pltpu.VMEM)] * count


def early_stage(first_masks, second_masks, tp_count, stripe, block_rows, factor):
    offsets = [offsets_of(each) for each in first_masks]
    second_offsets = offsets_of(second_masks)

    def kernel(*refs):
        hamiltonian, interaction, diagonal, last, table_out = refs[4:6] + refs[12:]
        me = own_place(tp_count)
        weights, table = tables_of(hamiltonian, interaction, block_rows)
        weights = jnp.concatenate([weights] * (block_rows // NO))
        diagonal[0] = weights
        diagonal[1] = inside_only(weights, 0)
        last[...] = inside_only(
            jnp.concatenate([weights] * 2), lax.axis_index("ta") * (block_rows // NO)
        )
        table_out[...] = table
        take_first(refs[:2], 0, me, offsets, stripe, table, refs[6:9])
        take_second(enumerate(refs[2:4]), 0, me, second_offsets, tp_count, stripe, table, refs[9:12])

    shapes = kept_shapes(tp_count, stripe, block_rows)
    tables = [
        jax.ShapeDtypeStruct((2, block_rows, block_rows), jnp.float32),
        jax.ShapeDtypeStruct((2 * block_rows, block_rows), jnp.float32),
        jax.ShapeDtypeStruct((3 * block_rows, block_rows), jnp.bfloat16),
    ]
    return pl.pallas_call(
        kernel,
        out_shape=shapes + shapes + tables,
        in_specs=in_vmem(6),
        out_specs=in_vmem(9),
        compiler_params=pltpu.CompilerParams(vmem_limit_bytes=16 << 20),
        name="early_stage",
    )


def first_stage(masks, second_masks, tp_count, stripe, block_rows, factor):
    offsets = [offsets_of(each) for each in masks]
    second_offsets = offsets_of(second_masks)
    scale = 0.5 * factor

    def kernel(*refs):
        weights, table = refs[2], refs[3][...]
        me = own_place(tp_count)
        targets, window, squares = refs[11:14], refs[17], refs[18]
        take_second(
            [(0, refs[7])], 1, me, second_offsets, tp_count, stripe, table, refs[14:17]
        )
        take_first(refs[:2], 1, me, offsets, stripe, table, targets)
        values, highs, bases = targets
        high = whole(highs, 0)
        made = window_of(squares_of(whole(values, 0), weights[1]), mirrored(high))
        squares[0], squares[1] = squares_of(whole(values, 1), weights[0])
        memory = products(high, made)
        window[0] = made[0]
        window[1] = made[1]
        half = (tp_count, stripe, block_rows)
        bases[0, :tp_count] = bases[0, :tp_count] + scale * memory[1].reshape(half)
        bases[1, :tp_count] = bases[1, :tp_count] - scale * memory[0].reshape(half)

    square = jax.ShapeDtypeStruct((2, 2 * block_rows, block_rows), jnp.bfloat16)
    return pl.pallas_call(
        kernel,
        out_shape=kept_shapes(tp_count, stripe, block_rows) * 2
        + [square, jax.ShapeDtypeStruct((2, block_rows, block_rows), jnp.float32)],
        in_specs=in_vmem(11),
        out_specs=in_vmem(8),
        input_output_aliases={4: 0, 5: 1, 6: 2, 8: 3, 9: 4, 10: 5},
        compiler_params=pltpu.CompilerParams(vmem_limit_bytes=16 << 20),
        name="first_stage",
    )


def second_stage(masks, tp_count, stripe, block_rows, factor):
    offsets = offsets_of(masks)
    order_size = 2 * block_rows
    scale = 0.5 * factor

    def kernel(*refs):
        diagonal, last_weights, table = refs[1], refs[2], refs[3][...]
        lows, bases, window, squares = refs[4:8]
        out, targets, nexts, low_next = refs[11], refs[12:15], refs[15], refs[16]
        ta_place = lax.axis_index("ta")
        tp_place = lax.axis_index("tp")
        me = own_place(tp_count)
        take_second([(1, refs[0])], 1, me, offsets, tp_count, stripe, table, targets)
        second_values, second_highs, second_bases = targets
        high = [whole(second_highs, block) for block in range(2)]

        def stored(block, group, real, imag):
            for part, result in ((0, real), (1, imag)):
                nexts[part, block, group] = result
                low_next[part, group, :, block * block_rows : (block + 1) * block_rows] = (
                    result.astype(jnp.bfloat16)
                )

        stored(0, 0, *whole(bases, 0))
        memory = products(high[0], [window[0], window[1]])
        start = whole(second_bases, 0)
        stored(0, 1, start[0] + scale * memory[1], start[1] - scale * memory[0])
        later = [
            window_of([squares[0], squares[1]], mirrored(high[0])),
            window_of(squares_of(whole(second_values, 1), diagonal[1]), mirrored(high[1])),
        ]
        later = [jnp.concatenate([later[0][k], later[1][k]]) for k in range(2)]
        for group in range(2):
            start = whole(bases if group == 0 else second_bases, 1)
            rows = whole(lows, 0) + whole(lows, 1) if group == 0 else high[0] + high[1]
            memory = products(rows, later)
            stored(1, group, start[0] + scale * memory[1], start[1] - scale * memory[0])

        current = [nexts[part, ta_place].reshape(order_size, block_rows) for part in range(2)]
        mirror = mirrored([low_next[part, ta_place] for part in range(2)])
        last = window_of(squares_of(current, last_weights[...]), mirror)
        row = pl.multiple_of(tp_place * stripe, stripe)
        own = [
            nexts[part, ta_place, :, pl.ds(row, stripe), :].reshape(2 * stripe, block_rows)
            for part in range(2)
        ]
        own_rounded = [
            low_next[part, :, pl.ds(row, stripe), :].reshape(2 * stripe, order_size)
            for part in range(2)
        ]
        memory = products(own_rounded, last)
        real, imag = started(own, [turned_by(table, *halves(part)) for part in own])
        shape = (2, stripe, block_rows)
        out[0] = (real + scale * memory[1]).reshape(shape)
        out[1] = (imag - scale * memory[0]).reshape(shape)

    return pl.pallas_call(
        kernel,
        out_shape=[jax.ShapeDtypeStruct((2, 2, stripe, block_rows), jnp.float32)]
        + kept_shapes(tp_count, stripe, block_rows),
        in_specs=in_vmem(11),
        out_specs=in_vmem(4),
        input_output_aliases={8: 1, 9: 2, 10: 3},
        scratch_shapes=[
            pltpu.VMEM((2, 2, 2, block_rows, block_rows), jnp.float32),
            pltpu.VMEM((2, 2, block_rows, order_size), jnp.bfloat16),
        ],
        compiler_params=pltpu.CompilerParams(vmem_limit_bytes=24 << 20),
        name="second_stage",
    )


def replicated(green, hamiltonian, interaction):
    tp_count = lax.axis_size("tp")
    count = 2 * tp_count
    stripe = green.shape[3]
    block_rows = green.shape[4]
    factor = 1.0 / math.sqrt(2 * block_rows)
    mask, first_masks, second_masks = exchange_masks(tp_count)

    def exchanged(block, mask):
        masks = (mask, mask) if isinstance(mask, int) else mask
        return lax.ppermute(block, ("ta", "tp"), [(i, i ^ masks[i % 2]) for i in range(count)])

    arriving = exchanged(green.reshape(-1, block_rows), mask).reshape(green.shape)
    first = jnp.stack([green[:, 0, 0], arriving[:, 0, 0]])
    second = jnp.stack([green[:, 1, 0], arriving[:, 1, 0]])
    high = lax.reduce_precision(second, 8, 7)
    second = jnp.stack([high, second - high], 1).astype(jnp.bfloat16)
    first_parts = second_parts = ()
    for first_mask, second_mask in zip(zip(*first_masks), second_masks):
        first_parts = [first, exchanged(first, first_mask)]
        first = jnp.concatenate(first_parts)
        if second_mask == tp_count:
            other_high = exchanged(second[:, 0], second_mask)[:, None]
            second = jnp.concatenate([second[:, :1], other_high, second[:, 1:]], 1)
        else:
            second_parts = [second, exchanged(second, second_mask)]
            second = jnp.concatenate(second_parts)
    first_parts += [exchanged(first_parts[0], 1)]
    first_parts += [exchanged(first_parts[1], 1)]
    second_parts += [exchanged(second_parts[0], 1)]
    second_parts += [exchanged(second_parts[1], 1)]
    first_masks = [[mask] + each for each in first_masks]
    second_masks = [mask] + [later for later in second_masks if later != tp_count]
    sizes = (tp_count, stripe, block_rows, factor)
    *kept, weights, last, table = early_stage(first_masks, second_masks, *sizes)(
        *first_parts[::2], *second_parts[::2], hamiltonian, interaction
    )
    known = first_stage(first_masks, second_masks, *sizes)(
        *first_parts[1::2], weights, table, *kept[:3], second_parts[1], *kept[3:]
    )
    result = second_stage(second_masks, *sizes)(
        second_parts[3], weights, last, table, *known[1:3], *known[6:], *known[3:6]
    )
    return result[0][:, :, None]


def solution(mesh):
    in_specs = (P(None, None, "tp", None, "ta"), P(), P())
    out_specs = P(None, None, "tp", None, "ta")
    ta_count = mesh.shape["ta"]
    tp_count = mesh.shape["tp"]

    def shards(green, hamiltonian, interaction):
        whole_bytes = green.size * green.dtype.itemsize * ta_count * tp_count
        covered = ta_count == 2 and green.shape[1] == 2 and tp_count >= 16
        if covered and tp_count & (tp_count - 1) == 0 and whole_bytes <= 1 << 22:
            return replicated(green, hamiltonian, interaction)
        return windowed(green, hamiltonian, interaction)

    return jax.shard_map(shards, mesh=mesh, in_specs=in_specs, out_specs=out_specs, check_vma=False)
```

```python
import math

import jax
import jax.numpy as jnp
from jax import lax
from jax.experimental import pallas as pl
from jax.experimental.pallas import tpu as pltpu
from jax.sharding import PartitionSpec as P

NO = 32
ITERS = 2


highest = lax.Precision.HIGHEST


def shifted(block, axis, distance):
    devices = range(lax.axis_size(axis))
    route = [(i - distance, i) for i in devices if i - distance in devices]
    return lax.ppermute(block, axis, route)


def half_dot(left_side, right_side):
    return jnp.dot(left_side, right_side, preferred_element_type=jnp.float32)


def accumulate(left_side, right_side):
    product_real = half_dot(left_side[0], right_side[0]) - half_dot(left_side[1], right_side[1])
    product_imag = half_dot(left_side[0], right_side[1]) + half_dot(left_side[1], right_side[0])
    return (product_real, product_imag)


def self_energy(values, mirror_part, weights):
    real_square = values[0] * values[0] - values[1] * values[1]
    imag_square = 2.0 * values[0] * values[1]
    sigma_real = weights * (real_square * mirror_part[0] - imag_square * mirror_part[1])
    sigma_imag = weights * (real_square * mirror_part[1] + imag_square * mirror_part[0])
    return jnp.stack([sigma_real, sigma_imag])


def windowed(green, hamiltonian, interaction):
    tp_count = lax.axis_size("tp")
    ta_place = lax.axis_index("ta")
    tp_place = lax.axis_index("tp")
    groups = green.shape[1]
    stripe = green.shape[3]
    block_rows = green.shape[4]
    columns = groups * stripe
    factor = 1.0 / math.sqrt(2 * block_rows)
    current = green[:, :, 0].reshape(2, columns, block_rows)
    squared = interaction * interaction
    column_global = (
        jnp.arange(groups, dtype=jnp.int32)[:, None] * tp_count + tp_place
    ) * stripe + jnp.arange(stripe, dtype=jnp.int32)[None, :]
    column_orbital = (column_global % NO).reshape(columns)
    onehot = (column_orbital[:, None] == jnp.arange(NO, dtype=jnp.int32)[None, :]).astype(
        jnp.float32
    )
    lookup_table = jnp.dot(onehot, squared.T, precision=highest)
    coupling = jnp.tile(lookup_table, (1, block_rows // NO))
    row_time = jnp.arange(block_rows, dtype=jnp.int32) // NO
    column_time = (tp_place * stripe + jnp.arange(stripe, dtype=jnp.int32)) // NO
    is_later = column_time[:, None] > row_time[None, :]
    block_width = math.gcd(block_rows, 128)
    blocked = jnp.kron(jnp.eye(block_width // NO, dtype=jnp.float32), hamiltonian.T)
    zero_half = jnp.zeros((), jnp.bfloat16)
    for _ in range(ITERS):
        rounded = current.astype(jnp.bfloat16)
        outgoing = rounded.reshape(2, groups, stripe, tp_count, stripe)
        previous = shifted(rounded, "ta", 1)
        earliest = shifted(rounded, "ta", 2)
        hamilton_term = jnp.dot(
            current.reshape(-1, block_width), blocked, precision=highest
        ).reshape(2, columns, block_rows)
        selected = []
        nearby = jnp.stack(
            [
                lax.dynamic_index_in_dim(
                    outgoing, jnp.minimum(ta_place + step_ahead, groups - 1), 1, keepdims=False
                )
                for step_ahead in range(3)
            ],
            1,
        )
        spread = lax.all_to_all(nearby, "tp", split_axis=3, concat_axis=3, tiled=True)
        from_one = shifted(spread[:, 1], "ta", 1)
        from_two = shifted(spread[:, 2], "ta", 2)
        received = (from_two, from_one, spread[:, 0])
        by_current = current.reshape(2, groups, stripe, block_rows)
        for window_index in range(3):
            group_pick = jnp.maximum(ta_place - 2 + window_index, 0)
            own_part = lax.dynamic_index_in_dim(by_current, group_pick, 1, keepdims=False)
            flipped = (
                jnp.transpose(received[window_index], (0, 3, 2, 1))
                .reshape(2, stripe, block_rows)
                .astype(jnp.float32)
            )
            selected.append(self_energy(own_part, flipped, coupling[:stripe]))
        oldest = jnp.where(is_later[None], selected[0], 0.0)
        middle = selected[1]
        newest = jnp.where(is_later[None], 0.0, selected[2])
        sending = jnp.stack([oldest + newest, middle], 1).astype(jnp.bfloat16)[:, :, None]
        portion = lax.all_gather(sending, "tp", axis=2, tiled=True)
        row_count = portion.shape[2] * stripe
        arriving_time = jnp.arange(row_count, dtype=jnp.int32) // NO
        later_here = (arriving_time[:, None] > row_time[None, :])[None]
        merged = portion[:, 0].reshape(2, row_count, block_rows)
        recent = portion[:, 1].reshape(2, row_count, block_rows)
        right_side = jnp.concatenate(
            [
                jnp.where(later_here, merged, zero_half),
                recent,
                jnp.where(later_here, zero_half, merged),
            ],
            1,
        )
        memory = accumulate(
            jnp.concatenate([source for source in (earliest, previous, rounded)], 2), right_side
        )
        next_real = current[0] + 0.5 * (hamilton_term[1] + factor * memory[1])
        next_imag = current[1] - 0.5 * (hamilton_term[0] + factor * memory[0])
        current = jnp.stack([next_real, next_imag])
    return current.reshape(2, groups, 1, stripe, block_rows)


def exchange_masks(tp_count):
    bits = [1 << bit for bit in reversed(range(1, tp_count.bit_length() - 1))]
    middle, low, ta_bit = bits[1:-1], bits[-1:], [tp_count]
    even, odd = ta_bit + middle + low, low + middle + ta_bit
    return bits[0], (even, odd), ta_bit + low + middle


def offsets_of(masks):
    offsets = [0]
    for mask in masks:
        offsets = offsets + [known ^ mask for known in offsets]
    return offsets


def bf16_dot(left_side, right_side):
    return lax.dot_general(
        left_side, right_side, (((1,), (0,)), ((), ())), preferred_element_type=jnp.float32
    )


def halves(values):
    high = values.astype(jnp.bfloat16)
    return high, (values - high.astype(jnp.float32)).astype(jnp.bfloat16)


def squares_of(values, weights):
    real = values[0] * values[0] - values[1] * values[1]
    imag = 2.0 * values[0] * values[1]
    return real * weights, imag * weights


def window_of(squares, mirror):
    real = squares[0] * mirror[0] - squares[1] * mirror[1]
    imag = squares[0] * mirror[1] + squares[1] * mirror[0]
    real, imag = real.astype(jnp.bfloat16), imag.astype(jnp.bfloat16)
    return [jnp.concatenate([real, -imag]), jnp.concatenate([imag, real])]


def inside_only(weights, first_time):
    source_time = lax.broadcasted_iota(jnp.int32, weights.shape, 0) // NO
    target_time = lax.broadcasted_iota(jnp.int32, weights.shape, 1) // NO + first_time
    return jnp.where(source_time <= target_time, weights, 0.0)


def mirrored(rounded):
    return [jnp.transpose(part.astype(jnp.float32)) for part in rounded]


def products(left_side, right_side):
    left_side = jnp.concatenate(left_side, axis=1)
    return [bf16_dot(left_side, part) for part in right_side]


def tables_of(hamiltonian, interaction, block_rows):
    def repeated(tile):
        return jnp.concatenate([tile] * (block_rows // NO), axis=1)

    weights = repeated(jnp.transpose(interaction[...] * interaction[...]))
    table = jnp.concatenate([repeated(jnp.transpose(hamiltonian[...]))] * (block_rows // NO))
    same_time = (
        lax.broadcasted_iota(jnp.int32, table.shape, 0) // NO
        == lax.broadcasted_iota(jnp.int32, table.shape, 1) // NO
    )
    high, low = halves(jnp.where(same_time, table, 0.0))
    return weights, jnp.concatenate([high, high, low])


def turned_by(table, high, low=None):
    if low is None:
        return bf16_dot(jnp.concatenate([high, high], axis=1), table[high.shape[1] :])
    return bf16_dot(jnp.concatenate([low, high, high], axis=1), table)


def started(values, turned):
    return values[0] + 0.5 * turned[1], values[1] - 0.5 * turned[0]


def rows_of(pieces):
    return pieces.reshape(pieces.shape[0] * pieces.shape[1], pieces.shape[2])


def whole(source, block):
    tp_count, stripe, block_rows = source.shape[1] // 2, source.shape[2], source.shape[3]
    return [
        source[part, block * tp_count : (block + 1) * tp_count].reshape(
            tp_count * stripe, block_rows
        )
        for part in range(2)
    ]


def put(device, targets, results, index, stripe):
    for target, result in zip(targets, results):
        for part in range(2):
            target[part, device] = result[part][index * stripe : (index + 1) * stripe]


def take_first(sources, late, me, offsets, stripe, table, targets):
    count = len(offsets[0]) // 2
    for flip, source in sources:
        values = [rows_of(source[:, part]) for part in range(2)]
        split = [halves(part) for part in values]
        base = started(values, [turned_by(table, high, low) for high, low in split])
        highs = [high for high, _ in split]
        for index in range(count):
            place = late * count + index
            mask = jnp.where(me % 2 == flip, offsets[0][place], offsets[1][place])
            put(me ^ (flip ^ mask), targets, (values, highs, base), index, stripe)


def take_second(sources, late, me, offsets, tp_count, stripe, table, targets):
    count = len(offsets) // 2
    for flip, source in sources:
        for plane in range(2):
            highs = [rows_of(source[:, plane, part]) for part in range(2)]
            values = [high.astype(jnp.float32) for high in highs]
            if plane == 0:
                lows = [rows_of(source[:, 2, part]) for part in range(2)]
                values = [values[part] + lows[part].astype(jnp.float32) for part in range(2)]
                turned = [turned_by(table, highs[part], lows[part]) for part in range(2)]
            else:
                turned = [turned_by(table, high) for high in highs]
            base = started(values, turned)
            for index in range(count):
                device = me ^ (flip ^ offsets[late * count + index] ^ (plane * tp_count))
                put(device, targets, (values, highs, base), index, stripe)


def own_place(tp_count):
    return lax.axis_index("ta") * tp_count + lax.axis_index("tp")


def kept_shapes(tp_count, stripe, block_rows):
    pieces = (2, 2 * tp_count, stripe, block_rows)
    return [jax.ShapeDtypeStruct(pieces, each) for each in (jnp.float32, jnp.bfloat16, jnp.float32)]


def in_vmem(count):
    return [pl.BlockSpec(memory_space=pltpu.VMEM)] * count


def early_stage(first_masks, second_masks, tp_count, stripe, block_rows, factor):
    offsets = [offsets_of(each) for each in first_masks]
    second_offsets = offsets_of(second_masks)

    def kernel(*refs):
        hamiltonian, interaction, diagonal, last, table_out = refs[4:6] + refs[12:]
        me = own_place(tp_count)
        weights, table = tables_of(hamiltonian, interaction, block_rows)
        weights = jnp.concatenate([weights] * (block_rows // NO))
        diagonal[0] = weights
        diagonal[1] = inside_only(weights, 0)
        last[...] = inside_only(
            jnp.concatenate([weights] * 2), lax.axis_index("ta") * (block_rows // NO)
        )
        table_out[...] = table
        take_first(enumerate(refs[:2]), 0, me, offsets, stripe, table, refs[6:9])
        take_second(enumerate(refs[2:4]), 0, me, second_offsets, tp_count, stripe, table, refs[9:12])

    shapes = kept_shapes(tp_count, stripe, block_rows)
    tables = [
        jax.ShapeDtypeStruct((2, block_rows, block_rows), jnp.float32),
        jax.ShapeDtypeStruct((2 * block_rows, block_rows), jnp.float32),
        jax.ShapeDtypeStruct((3 * block_rows, block_rows), jnp.bfloat16),
    ]
    return pl.pallas_call(
        kernel,
        out_shape=shapes + shapes + tables,
        in_specs=in_vmem(6),
        out_specs=in_vmem(9),
        compiler_params=pltpu.CompilerParams(vmem_limit_bytes=16 << 20),
        name="early_stage",
    )


def near_stage(masks, tp_count, stripe, block_rows, factor):
    offsets = [offsets_of(each) for each in masks]

    def kernel(*refs):
        table = refs[1][...]
        take_first([(0, refs[0])], 1, own_place(tp_count), offsets, stripe, table, refs[5:])

    return pl.pallas_call(
        kernel,
        out_shape=kept_shapes(tp_count, stripe, block_rows),
        in_specs=in_vmem(5),
        out_specs=in_vmem(3),
        input_output_aliases={2: 0, 3: 1, 4: 2},
        compiler_params=pltpu.CompilerParams(vmem_limit_bytes=16 << 20),
        name="near_stage",
    )


def first_stage(masks, second_masks, tp_count, stripe, block_rows, factor):
    offsets = [offsets_of(each) for each in masks]
    second_offsets = offsets_of(second_masks)
    scale = 0.5 * factor

    def kernel(*refs):
        weights, table = refs[1], refs[2][...]
        me = own_place(tp_count)
        targets, window, squares = refs[10:13], refs[16], refs[17]
        take_second(
            [(0, refs[6])], 1, me, second_offsets, tp_count, stripe, table, refs[13:16]
        )
        take_first([(1, refs[0])], 1, me, offsets, stripe, table, targets)
        values, highs, bases = targets
        high = whole(highs, 0)
        made = window_of(squares_of(whole(values, 0), weights[1]), mirrored(high))
        squares[0], squares[1] = squares_of(whole(values, 1), weights[0])
        memory = products(high, made)
        window[0] = made[0]
        window[1] = made[1]
        half = (tp_count, stripe, block_rows)
        bases[0, :tp_count] = bases[0, :tp_count] + scale * memory[1].reshape(half)
        bases[1, :tp_count] = bases[1, :tp_count] - scale * memory[0].reshape(half)

    square = jax.ShapeDtypeStruct((2, 2 * block_rows, block_rows), jnp.bfloat16)
    return pl.pallas_call(
        kernel,
        out_shape=kept_shapes(tp_count, stripe, block_rows) * 2
        + [square, jax.ShapeDtypeStruct((2, block_rows, block_rows), jnp.float32)],
        in_specs=in_vmem(10),
        out_specs=in_vmem(8),
        input_output_aliases={3: 0, 4: 1, 5: 2, 7: 3, 8: 4, 9: 5},
        compiler_params=pltpu.CompilerParams(vmem_limit_bytes=16 << 20),
        name="first_stage",
    )


def second_stage(masks, tp_count, stripe, block_rows, factor):
    offsets = offsets_of(masks)
    order_size = 2 * block_rows
    scale = 0.5 * factor

    def kernel(*refs):
        diagonal, last_weights, table = refs[1], refs[2], refs[3][...]
        lows, bases, window, squares = refs[4:8]
        out, targets, nexts, low_next = refs[11], refs[12:15], refs[15], refs[16]
        ta_place = lax.axis_index("ta")
        tp_place = lax.axis_index("tp")
        me = own_place(tp_count)
        take_second([(1, refs[0])], 1, me, offsets, tp_count, stripe, table, targets)
        second_values, second_highs, second_bases = targets
        high = [whole(second_highs, block) for block in range(2)]

        def stored(block, group, real, imag):
            for part, result in ((0, real), (1, imag)):
                nexts[part, block, group] = result
                low_next[part, group, :, block * block_rows : (block + 1) * block_rows] = (
                    result.astype(jnp.bfloat16)
                )

        stored(0, 0, *whole(bases, 0))
        memory = products(high[0], [window[0], window[1]])
        start = whole(second_bases, 0)
        stored(0, 1, start[0] + scale * memory[1], start[1] - scale * memory[0])
        later = [
            window_of([squares[0], squares[1]], mirrored(high[0])),
            window_of(squares_of(whole(second_values, 1), diagonal[1]), mirrored(high[1])),
        ]
        later = [jnp.concatenate([later[0][k], later[1][k]]) for k in range(2)]
        for group in range(2):
            start = whole(bases if group == 0 else second_bases, 1)
            rows = whole(lows, 0) + whole(lows, 1) if group == 0 else high[0] + high[1]
            memory = products(rows, later)
            stored(1, group, start[0] + scale * memory[1], start[1] - scale * memory[0])

        current = [nexts[part, ta_place].reshape(order_size, block_rows) for part in range(2)]
        mirror = mirrored([low_next[part, ta_place] for part in range(2)])
        last = window_of(squares_of(current, last_weights[...]), mirror)
        row = pl.multiple_of(tp_place * stripe, stripe)
        own = [
            nexts[part, ta_place, :, pl.ds(row, stripe), :].reshape(2 * stripe, block_rows)
            for part in range(2)
        ]
        own_rounded = [
            low_next[part, :, pl.ds(row, stripe), :].reshape(2 * stripe, order_size)
            for part in range(2)
        ]
        memory = products(own_rounded, last)
        real, imag = started(own, [turned_by(table, *halves(part)) for part in own])
        shape = (2, stripe, block_rows)
        out[0] = (real + scale * memory[1]).reshape(shape)
        out[1] = (imag - scale * memory[0]).reshape(shape)

    return pl.pallas_call(
        kernel,
        out_shape=[jax.ShapeDtypeStruct((2, 2, stripe, block_rows), jnp.float32)]
        + kept_shapes(tp_count, stripe, block_rows),
        in_specs=in_vmem(11),
        out_specs=in_vmem(4),
        input_output_aliases={8: 1, 9: 2, 10: 3},
        scratch_shapes=[
            pltpu.VMEM((2, 2, 2, block_rows, block_rows), jnp.float32),
            pltpu.VMEM((2, 2, block_rows, order_size), jnp.bfloat16),
        ],
        compiler_params=pltpu.CompilerParams(vmem_limit_bytes=24 << 20),
        name="second_stage",
    )


def replicated(green, hamiltonian, interaction):
    tp_count = lax.axis_size("tp")
    count = 2 * tp_count
    stripe = green.shape[3]
    block_rows = green.shape[4]
    factor = 1.0 / math.sqrt(2 * block_rows)
    mask, first_masks, second_masks = exchange_masks(tp_count)

    def exchanged(block, mask):
        masks = (mask, mask) if isinstance(mask, int) else mask
        return lax.ppermute(block, ("ta", "tp"), [(i, i ^ masks[i % 2]) for i in range(count)])

    arriving = exchanged(green.reshape(-1, block_rows), mask).reshape(green.shape)
    first = jnp.stack([green[:, 0, 0], arriving[:, 0, 0]])
    second = jnp.stack([green[:, 1, 0], arriving[:, 1, 0]])
    high = lax.reduce_precision(second, 8, 7)
    second = jnp.stack([high, second - high], 1).astype(jnp.bfloat16)
    first_parts = second_parts = ()
    for first_mask, second_mask in zip(zip(*first_masks), second_masks):
        first_parts = [first, exchanged(first, first_mask)]
        first = jnp.concatenate(first_parts)
        if second_mask == tp_count:
            other_high = exchanged(second[:, 0], second_mask)[:, None]
            second = jnp.concatenate([second[:, :1], other_high, second[:, 1:]], 1)
        else:
            second_parts = [second, exchanged(second, second_mask)]
            second = jnp.concatenate(second_parts)
    first_parts += [exchanged(first_parts[0], 1)]
    first_parts += [exchanged(first_parts[1], 1)]
    second_parts += [exchanged(second_parts[0], 1)]
    second_parts += [exchanged(second_parts[1], 1)]
    first_masks = [[mask] + each for each in first_masks]
    second_masks = [mask] + [later for later in second_masks if later != tp_count]
    sizes = (tp_count, stripe, block_rows, factor)
    *kept, weights, last, table = early_stage(first_masks, second_masks, *sizes)(
        *first_parts[::2], *second_parts[::2], hamiltonian, interaction
    )
    placed = near_stage(first_masks, *sizes)(first_parts[1], table, *kept[:3])
    known = first_stage(first_masks, second_masks, *sizes)(
        first_parts[3], weights, table, *placed, second_parts[1], *kept[3:]
    )
    result = second_stage(second_masks, *sizes)(
        second_parts[3], weights, last, table, *known[1:3], *known[6:], *known[3:6]
    )
    return result[0][:, :, None]


def solution(mesh):
    in_specs = (P(None, None, "tp", None, "ta"), P(), P())
    out_specs = P(None, None, "tp", None, "ta")
    ta_count = mesh.shape["ta"]
    tp_count = mesh.shape["tp"]

    def shards(green, hamiltonian, interaction):
        whole_bytes = green.size * green.dtype.itemsize * ta_count * tp_count
        covered = ta_count == 2 and green.shape[1] == 2 and tp_count >= 16
        if covered and tp_count & (tp_count - 1) == 0 and whole_bytes <= 1 << 22:
            return replicated(green, hamiltonian, interaction)
        return windowed(green, hamiltonian, interaction)

    return jax.shard_map(shards, mesh=mesh, in_specs=in_specs, out_specs=out_specs, check_vma=False)
```
